32 devices in a mesh: dp: 16 (over z, x, core), tensor: 2 (over y).
Axes of the slice: x: 2, y: 2, z: 4, core: 2. Of those that a mesh axis runs over, the one named last changes fastest.
Arguments:
- short_images: bfloat16 [64, 197, 768], P('dp'), may hold values from -6 to 6
- short_texts: bfloat16 [64, 58, 768], P('dp'), may hold values from -6 to 6
- short_lengths: int32 [64], P('dp'), may hold values from 8 to 58, as said below
- short_cotangent: bfloat16 [64, 256, 768], P('dp'), may hold values from -6 to 6
- long_images: bfloat16 [16, 197, 768], P('dp'), may hold values from -6 to 6
- long_texts: bfloat16 [16, 512, 768], P('dp'), may hold values from -6 to 6
- long_lengths: int32 [16], P('dp'), may hold values from 59 to 512, as said below
- long_cotangent: bfloat16 [16, 710, 768], P('dp'), may hold values from -6 to 6
- img_weight: bfloat16 [768, 768], P(('dp', 'tensor')), may hold values from -0.21875 to 0.21875
- img_bias: bfloat16 [768], P(('dp', 'tensor')), may hold values from -2 to 2
- text_weight: bfloat16 [768, 768], P(('dp', 'tensor')), may hold values from -0.21875 to 0.21875
- text_bias: bfloat16 [768], P(('dp', 'tensor')), may hold values from -2 to 2
- cls_token: bfloat16 [768], P(('dp', 'tensor')), may hold values from -5 to 5
- attn_gain: bfloat16 [768], P(('dp', 'tensor')), may hold values from 0.5 to 1.5
- attn_shift: bfloat16 [768], P(('dp', 'tensor')), may hold values from -2 to 2
- query_weight: bfloat16 [768, 768], P('dp', 'tensor'), may hold values from -0.21875 to 0.21875
- query_bias: bfloat16 [768], P(('dp', 'tensor')), may hold values from -2 to 2
- key_weight: bfloat16 [768, 768], P('dp', 'tensor'), may hold values from -0.21875 to 0.21875
- value_weight: bfloat16 [768, 768], P('dp', 'tensor'), may hold values from -0.21875 to 0.21875
- value_bias: bfloat16 [768], P(('dp', 'tensor')), may hold values from -2 to 2
- out_weight: bfloat16 [768, 768], P('tensor', 'dp'), may hold values from -2 to 2
- out_bias: bfloat16 [768], P(('dp', 'tensor')), may hold values from -2 to 2
- mlp_gain: bfloat16 [768], P(('dp', 'tensor')), may hold values from 0.5 to 1.5
- mlp_shift: bfloat16 [768], P(('dp', 'tensor')), may hold values from -2 to 2
- up_weight: bfloat16 [768, 3072], P('dp', 'tensor'), may hold values from -0.21875 to 0.21875
- up_bias: bfloat16 [3072], P(('dp', 'tensor')), may hold values from -2 to 2
- down_weight: bfloat16 [3072, 768], P('tensor', 'dp'), may hold values from -0.109375 to 0.109375
- down_bias: bfloat16 [768], P(('dp', 'tensor')), may hold values from -2 to 2
Outputs:
- short_output: bfloat16 [64, 256, 768], P('dp')
- long_output: bfloat16 [16, 710, 768], P('dp')
- short_image_grad: float32 [64, 197, 768], P('dp')
- short_text_grad: float32 [64, 58, 768], P('dp')
- long_image_grad: float32 [16, 197, 768], P('dp')
- long_text_grad: float32 [16, 512, 768], P('dp')
- img_weight_grad: float32 [768, 768], P(('dp', 'tensor'))
- img_bias_grad: float32 [768], P(('dp', 'tensor'))
- text_weight_grad: float32 [768, 768], P(('dp', 'tensor'))
- text_bias_grad: float32 [768], P(('dp', 'tensor'))
- cls_grad: float32 [768], P(('dp', 'tensor'))
- attn_gain_grad: float32 [768], P(('dp', 'tensor'))
- attn_shift_grad: float32 [768], P(('dp', 'tensor'))
- query_weight_grad: float32 [768, 768], P('dp', 'tensor')
- query_bias_grad: float32 [768], P(('dp', 'tensor'))
- key_weight_grad: float32 [768, 768], P('dp', 'tensor')
- value_weight_grad: float32 [768, 768], P('dp', 'tensor')
- value_bias_grad: float32 [768], P(('dp', 'tensor'))
- out_weight_grad: float32 [768, 768], P('tensor', 'dp')
- out_bias_grad: float32 [768], P(('dp', 'tensor'))
- mlp_gain_grad: float32 [768], P(('dp', 'tensor'))
- mlp_shift_grad: float32 [768], P(('dp', 'tensor'))
- up_weight_grad: float32 [768, 3072], P('dp', 'tensor')
- up_bias_grad: float32 [3072], P(('dp', 'tensor'))
- down_weight_grad: float32 [3072, 768], P('tensor', 'dp')
- down_bias_grad: float32 [768], P(('dp', 'tensor'))
The draws below stay inside these ranges and needn't reach their ends.
Inputs may be any that keep to these rules, and one draw needn't show every extreme that they name: `short_lengths`: caption tokens of each pair of the short micro-batch; some pair has exactly 58. `long_lengths`: caption tokens of each pair of the long micro-batch; some pair has exactly 512.
All inputs are finite; a program needn't handle non-finite values.
Results may differ from the reference program's by a relative error of at most 0.017.
Values may be sent and summed in bfloat16 or wider, within the bound.
No kernel may reach another device: no remote copies, remote signals or barrier semaphores. Data moves between devices by JAX's collectives and lax.ppermute only.
A program may use at most 192 MiB of HBM per device.

```python
import jax
import jax.numpy as jnp
from jax import lax

D = 768
HEADS = 12
HEAD = 64
FF = 3072
IMG = 197
MIN_CAP = 8
CAP_SHORT = 58
CAP_LONG = 512
SHORT_PAIRS = 64
LONG_PAIRS = 16
S_SHORT = 256
S_LONG = 710
N_TENSOR = 2


def draw_short_lengths(key, part):
    first_key, second_key = jax.random.split(jax.random.fold_in(key, 11))
    values = jax.random.randint(first_key, (SHORT_PAIRS,), MIN_CAP, CAP_SHORT + 1)
    place = jax.random.randint(second_key, (), 0, SHORT_PAIRS)
    return values.at[place].set(CAP_SHORT).astype(jnp.int32)


def draw_long_lengths(key, part):
    keys = jax.random.split(jax.random.fold_in(key, 23), 3)
    span_len = CAP_LONG - CAP_SHORT
    first_draw = jax.random.randint(keys[0], (LONG_PAIRS,), 0, span_len)
    second_draw = jax.random.randint(keys[1], (LONG_PAIRS,), 0, span_len)
    values = CAP_SHORT + 1 + first_draw * second_draw // span_len
    place = jax.random.randint(keys[2], (), 0, LONG_PAIRS)
    return values.at[place].set(CAP_LONG).astype(jnp.int32)


def raised(values, own_key, source, target, blocks, factor):
    def block_of(axis_at):
        return (jnp.arange(values.shape[axis_at]) // (values.shape[axis_at] // blocks)).reshape((-1,) + (1,) * (values.ndim - 1 - axis_at))

    near = jax.random.permutation(own_key, blocks)[block_of(target)]
    second = (block_of(target) + blocks // 2) % blocks
    return jnp.where((block_of(source) == near) | (block_of(source) == second), factor * values, values)


def block_levels(rng, shape, cuts, low, high):
    factor_of, own = 1.0, jax.random.fold_in(rng, 6)
    for axis_at, parts in cuts:
        heights = jnp.exp(jax.random.uniform(jax.random.fold_in(own, axis_at), (parts,), jnp.float32, low / len(cuts), high / len(cuts)))
        factor_of = factor_of * jnp.repeat(heights, shape[axis_at] // parts).reshape([-1 if axis == axis_at else 1 for axis in range(len(shape))])
    return factor_of


def gaussian(own_key, dims, deviation, bound, cuts=(), held_as=jnp.bfloat16):
    drawn = jax.random.normal(own_key, dims, jnp.float32) * deviation
    if len(cuts) > 0:
        drawn = block_levels(own_key, dims, cuts, -0.22, 0.18) * drawn
    return jnp.clip(drawn, min=-bound, max=bound).astype(held_as)


def heavy_noise(own_key, shape, spread, most, cuts, heavy, dtype=jnp.bfloat16):
    drawn = spread * jax.random.normal(own_key, shape, jnp.float32)
    if cuts:
        drawn = drawn * block_levels(own_key, shape, cuts, -0.22, 0.18)
    return jnp.clip(raised(drawn, jax.random.fold_in(own_key, 3), *heavy), -most, most).astype(dtype)


def setup_inputs(seed: int = 0) -> dict:
    splits = jax.random.split(jax.random.key(seed), 29)
    short_images = gaussian(splits[0], (SHORT_PAIRS, IMG, D), 1.0, 6.0, ((0, 16),))
    short_texts = gaussian(splits[1], (SHORT_PAIRS, CAP_SHORT, D), 1.0, 6.0, ((0, 16),))
    short_lengths = draw_short_lengths(jax.random.fold_in(splits[28], 71), 0)
    short_cotangent = heavy_noise(splits[3], (SHORT_PAIRS, S_SHORT, D), 1.0, 6.0, ((0, 16),), (0, 2, 16, 2.0))
    long_images = gaussian(splits[4], (LONG_PAIRS, IMG, D), 1.0, 6.0, ((0, 16),))
    long_texts = gaussian(splits[5], (LONG_PAIRS, CAP_LONG, D), 1.0, 6.0, ((0, 16),))
    long_lengths = draw_long_lengths(jax.random.fold_in(splits[28], 71), 0)
    long_cotangent = heavy_noise(splits[7], (LONG_PAIRS, S_LONG, D), 1.0, 6.0, ((0, 16),), (0, 2, 16, 2.0))
    img_weight = gaussian(splits[8], (D, D), D ** -0.5, 0.21875, ((0, 32),))
    img_bias = gaussian(splits[9], (D,), 0.3, 2.0, ((0, 32),))
    text_weight = gaussian(splits[10], (D, D), D ** -0.5, 0.21875, ((0, 32),))
    text_bias = gaussian(splits[11], (D,), 0.3, 2.0, ((0, 32),))
    cls_token = gaussian(splits[12], (D,), 1.0, 5.0, ((0, 32),))
    attn_gain = jnp.clip(1.0 + 0.1 * jax.random.normal(splits[13], (D,), jnp.float32), 0.5, 1.5).astype(jnp.bfloat16)
    attn_shift = gaussian(splits[14], (D,), 0.3, 2.0, ((0, 32),))
    query_weight = gaussian(splits[15], (D, D), D ** -0.5, 0.21875, ((0, 16), (1, 2)))
    query_bias = gaussian(splits[16], (D,), 0.3, 2.0, ((0, 32),))
    key_weight = gaussian(splits[17], (D, D), D ** -0.5, 0.21875, ((0, 16), (1, 2)))
    value_weight = gaussian(splits[18], (D, D), D ** -0.5, 0.21875, ((0, 16), (1, 2)))
    value_bias = gaussian(splits[19], (D,), 0.3, 2.0, ((0, 32),))
    out_weight = gaussian(splits[20], (D, D), 8 ** -0.5, 2.0, ((0, 2), (1, 16)))
    out_bias = gaussian(splits[21], (D,), 0.3, 2.0, ((0, 32),))
    mlp_gain = jnp.clip(1.0 + 0.1 * jax.random.normal(splits[22], (D,), jnp.float32), 0.5, 1.5).astype(jnp.bfloat16)
    mlp_shift = gaussian(splits[23], (D,), 0.3, 2.0, ((0, 32),))
    up_weight = gaussian(splits[24], (D, FF), D ** -0.5, 0.21875, ((0, 16), (1, 2)))
    up_bias = gaussian(splits[25], (FF,), 0.3, 2.0, ((0, 32),))
    down_weight = gaussian(splits[26], (FF, D), FF ** -0.5, 0.109375, ((0, 2), (1, 16)))
    down_bias = gaussian(splits[27], (D,), 0.3, 2.0, ((0, 32),))
    return dict(short_images=short_images, short_texts=short_texts, short_lengths=short_lengths, short_cotangent=short_cotangent, long_images=long_images, long_texts=long_texts, long_lengths=long_lengths, long_cotangent=long_cotangent, img_weight=img_weight, img_bias=img_bias, text_weight=text_weight, text_bias=text_bias, cls_token=cls_token, attn_gain=attn_gain, attn_shift=attn_shift, query_weight=query_weight, query_bias=query_bias, key_weight=key_weight, value_weight=value_weight, value_bias=value_bias, out_weight=out_weight, out_bias=out_bias, mlp_gain=mlp_gain, mlp_shift=mlp_shift, up_weight=up_weight, up_bias=up_bias, down_weight=down_weight, down_bias=down_bias)


EPS = 1e-06
NEG = -1e+30

@jax.custom_vjp
def low(v):
    return lax.optimization_barrier(v.astype(jnp.bfloat16)).astype(jnp.float32)

@jax.custom_vjp
def low_back(v):
    return v

def low_keep(v):
    return (low(v), None)

def low_pass(kept, grad):
    return (grad,)

def back_keep(v):
    return (v, None)

def back_low(kept, grad):
    return (low(grad),)
low.defvjp(low_keep, low_pass)
low_back.defvjp(back_keep, back_low)

def normalize(values, norm_gain, norm_shift):
    row_mean = lax.optimization_barrier(jnp.mean(values, axis=-1, keepdims=True))
    centred = values - row_mean
    row_var = lax.optimization_barrier(jnp.mean(centred * centred, axis=-1, keepdims=True))
    return centred * lax.rsqrt(row_var + EPS) * norm_gain + norm_shift

def product(left, right):
    return jnp.einsum('...d,de->...e', left, right, precision=lax.Precision.HIGHEST)

def attend(member):
    query_rows, key_rows, value_rows, limit = member
    seq_len = query_rows.shape[0]
    heads_query = query_rows.reshape(seq_len, HEADS, HEAD)
    heads_key = key_rows.reshape(seq_len, HEADS, HEAD)
    heads_value = value_rows.reshape(seq_len, HEADS, HEAD)
    scores = jnp.einsum('qhd,khd->hqk', heads_query, heads_key, precision=lax.Precision.HIGHEST) * HEAD ** (-0.5)
    scores = low_back(scores)
    key_valid = jnp.arange(seq_len) < limit
    scores = jnp.where(key_valid[None, None, :], scores, NEG)
    attn_probs = jax.nn.softmax(scores, axis=-1)
    mixed = jnp.einsum('hqk,khd->qhd', low(attn_probs), heads_value, precision=lax.Precision.HIGHEST)
    return mixed.reshape(seq_len, HEADS * HEAD)

def block(params, images, texts, lengths):
    img_weight, img_bias, text_weight, text_bias, cls_token, attn_gain, attn_shift, query_weight, query_bias, key_weight, value_weight, value_bias, out_weight, out_bias, mlp_gain, mlp_shift, up_weight, up_bias, down_weight, down_bias = params
    pair_count, image_len, model_width = images.shape
    image_rows = low_back(product(images, img_weight)) + img_bias
    text_rows = low_back(product(texts, text_weight)) + text_bias
    cls_rows = jnp.broadcast_to(cls_token, (pair_count, 1, model_width))
    stream_in = jnp.concatenate([cls_rows, image_rows, text_rows], axis=1)
    normed_one = low(normalize(stream_in, attn_gain, attn_shift))
    query_rows = low(low_back(product(normed_one, query_weight) + query_bias))
    key_rows = low(low_back(product(normed_one, key_weight)))
    value_rows = low(low_back(product(normed_one, value_weight) + value_bias))
    limits = 1 + image_len + lengths
    attended = lax.map(jax.checkpoint(attend), (query_rows, key_rows, value_rows, limits))
    attended = low(low_back(attended))
    head_width = model_width // N_TENSOR
    attn_total = jnp.zeros_like(stream_in)
    for member in range(N_TENSOR):
        lower_edge = member * head_width
        attn_total = attn_total + low(product(attended[..., lower_edge:lower_edge + head_width], out_weight[lower_edge:lower_edge + head_width]))
    stream_mid = stream_in + low_back(attn_total) + out_bias
    normed_two = low(normalize(stream_mid, mlp_gain, mlp_shift))
    pre_act = low_back(product(normed_two, up_weight) + up_bias)
    hidden = low(jax.nn.gelu(pre_act, approximate=False))
    unit_width = up_weight.shape[1] // N_TENSOR
    mlp_total = jnp.zeros_like(stream_in)
    for member in range(N_TENSOR):
        lower_edge = member * unit_width
        mlp_total = mlp_total + low(product(hidden[..., lower_edge:lower_edge + unit_width], down_weight[lower_edge:lower_edge + unit_width]))
    return stream_mid + low_back(mlp_total) + down_bias

def bucket_size(count, seq_len):
    size_best = 1
    for candidate in range(1, count + 1):
        if count % candidate == 0 and candidate * seq_len <= 4096:
            size_best = candidate
    return size_best

def run_bucket(params, images, texts, lengths, cotangent):
    count = images.shape[0]
    seq_len = 1 + images.shape[1] + texts.shape[1]
    batch_size = bucket_size(count, seq_len)
    steps_total = count // batch_size

    def split_rows(values):
        return values.reshape((steps_total, batch_size) + values.shape[1:])

    def join_rows(values):
        return values.reshape((count,) + values.shape[2:])

    def advance(carry, member):
        image_block, text_block, length_block, cot_block = member

        def forward(weights, image_vals, text_vals):
            return block(weights, image_vals, text_vals, length_block)
        result, pullback = jax.vjp(forward, params, image_block.astype(jnp.float32), text_block.astype(jnp.float32))
        weight_grads, image_grad, text_grad = pullback(cot_block.astype(jnp.float32))
        carry = jax.tree.map(lambda summed, addend: summed + addend, carry, weight_grads)
        return (carry, (result.astype(jnp.bfloat16), image_grad, text_grad))
    initial = jax.tree.map(jnp.zeros_like, params)
    totals, (outputs, image_grads, text_grads) = lax.scan(advance, initial, (split_rows(images), split_rows(texts), split_rows(lengths), split_rows(cotangent)))
    return (totals, join_rows(outputs), join_rows(image_grads), join_rows(text_grads))

def reference(short_images, short_texts, short_lengths, short_cotangent, long_images, long_texts, long_lengths, long_cotangent, img_weight, img_bias, text_weight, text_bias, cls_token, attn_gain, attn_shift, query_weight, query_bias, key_weight, value_weight, value_bias, out_weight, out_bias, mlp_gain, mlp_shift, up_weight, up_bias, down_weight, down_bias):
    params = tuple((weight.astype(jnp.float32) for weight in (img_weight, img_bias, text_weight, text_bias, cls_token, attn_gain, attn_shift, query_weight, query_bias, key_weight, value_weight, value_bias, out_weight, out_bias, mlp_gain, mlp_shift, up_weight, up_bias, down_weight, down_bias)))
    short_totals, short_output, short_image_grad, short_text_grad = run_bucket(params, short_images, short_texts, short_lengths, short_cotangent)
    long_totals, long_output, long_image_grad, long_text_grad = run_bucket(params, long_images, long_texts, long_lengths, long_cotangent)
    grads = jax.tree.map(lambda first, second: first + second, short_totals, long_totals)
    return (short_output, long_output, short_image_grad, short_text_grad, long_image_grad, long_text_grad, grads[0], grads[1], grads[2], grads[3], grads[4], grads[5], grads[6], grads[7], grads[8], grads[9], grads[10], grads[11], grads[12], grads[13], grads[14], grads[15], grads[16], grads[17], grads[18], grads[19])
```

```python
from functools import partial

import jax
import jax.numpy as jnp
from jax import lax
from jax.experimental import pallas as pl
from jax.experimental.pallas import tpu as pltpu
from jax.sharding import PartitionSpec as P

DP = "dp"
TP = "tensor"
BOTH = (TP, DP)
EPS = 1e-06
NEG = -1e30
BF = jnp.bfloat16
F32 = jnp.float32
ROWS = 1024
BLK = 256
MIB = 1 << 20


def dot_nn(left, right):
    return lax.dot_general(left, right, (((1,), (0,)), ((), ())), preferred_element_type=F32)


def dot_nt(left, right):
    return lax.dot_general(left, right, (((1,), (1,)), ((), ())), preferred_element_type=F32)


def flip(values):
    return values.astype(F32).T.astype(BF)


def params(limit=56):
    return pltpu.CompilerParams(dimension_semantics=("arbitrary",), vmem_limit_bytes=limit * MIB)


def norm_parts(values):
    row_mean = jnp.mean(values, axis=-1, keepdims=True)
    centred = values - row_mean
    row_var = jnp.mean(centred * centred, axis=-1, keepdims=True)
    inverse = lax.rsqrt(row_var + EPS)
    return centred * inverse, inverse


def norm_back(xhat, inverse, scaled):
    first = jnp.mean(scaled, axis=-1, keepdims=True)
    second = jnp.mean(scaled * xhat, axis=-1, keepdims=True)
    return (scaled - first - xhat * second) * inverse


def is_short(meta):
    return meta[0] == 1


def half_slot(meta, half):
    return meta[5 + half]


def group_slot(meta, group):
    return meta[7 + group]


def active(meta, step):
    return jnp.logical_or(is_short(meta), step < 3)


def put_pieces(meta, out_ref, result):
    groups, height = out_ref.shape[-3], out_ref.shape[-2]
    for group in range(groups):
        out_ref[0, group_slot(meta, group)] = result[group * height : (group + 1) * height].astype(BF)


def embed_kernel(meta, x_ref, gat_ref, sm_ref, stream_ref, n1_ref, qkv_ref, wimg_ref, wtext_ref, wf, wqkv):
    step = pl.program_id(0)

    @pl.when(step == 0)
    def _():
        for part, dst in ((0, wimg_ref), (1, wtext_ref)):
            for half in range(2):
                for group in range(16):
                    piece = gat_ref[half_slot(meta, half), group_slot(meta, group), :, 1152:1920]
                    start = 24 * (2 * group + half)
                    wf[start : start + 24, :] = piece.astype(F32)[24 * part : 24 * part + 24]
            dst[...] = wf[...].astype(BF)
        for half in range(2):
            for group in range(16):
                wqkv[half, 48 * group : 48 * group + 48, :] = gat_ref[
                    half_slot(meta, half), group_slot(meta, group), :, 0:1152
                ]

    @pl.when(active(meta, step))
    def _():
        with_image = jnp.logical_or(is_short(meta), step == 0)

        @pl.when(with_image)
        def _():
            first = dot_nn(x_ref[0:208, :], wimg_ref[...]) + sm_ref[0:1, :]
            second = dot_nn(x_ref[192:256, :], wtext_ref[...]) + sm_ref[1:2, :]
            index = lax.broadcasted_iota(jnp.int32, (16, 768), 0)
            stream_ref[0:192, :] = first[0:192]
            stream_ref[192:208, :] = jnp.where(index < 6, first[192:208], second[0:16])
            stream_ref[208:256, :] = second[16:64]
            stream_ref[0:1, :] = sm_ref[2:3, :]

        @pl.when(jnp.logical_not(with_image))
        def _():
            stream_ref[...] = dot_nn(x_ref[...], wtext_ref[...]) + sm_ref[1:2, :]

        xhat, _ = norm_parts(stream_ref[...])
        normed = (xhat * sm_ref[3:4, :] + sm_ref[4:5, :]).astype(BF)
        n1_ref[...] = normed
        for half in range(2):
            out = dot_nn(normed, wqkv[half])
            lanes = slice(384 * half, 384 * half + 384)
            base = 1152 * half
            qkv_ref[:, base : base + 384] = (out[:, 0:384] + sm_ref[5:6, lanes]).astype(BF)
            qkv_ref[:, base + 384 : base + 768] = out[:, 384:768].astype(BF)
            qkv_ref[:, base + 768 : base + 1152] = (out[:, 768:1152] + sm_ref[6:7, lanes]).astype(BF)


def embed(meta, x, gathered, smalls):
    row = lambda width: pl.BlockSpec((BLK, width), lambda i, m: (i, 0))
    whole = lambda *shape: pl.BlockSpec(shape, lambda i, m: (0,) * len(shape))
    return pl.pallas_call(
        embed_kernel,
        grid_spec=pltpu.PrefetchScalarGridSpec(
            num_scalar_prefetch=1,
            grid=(4,),
            in_specs=[row(768), whole(*gathered.shape), whole(16, 768)],
            out_specs=[row(768), row(768), row(2304), whole(768, 768), whole(768, 768)],
            scratch_shapes=[pltpu.VMEM((768, 768), F32), pltpu.VMEM((2, 768, 1152), BF)],
        ),
        out_shape=[
            jax.ShapeDtypeStruct((ROWS, 768), F32),
            jax.ShapeDtypeStruct((ROWS, 768), BF),
            jax.ShapeDtypeStruct((ROWS, 2304), BF),
            jax.ShapeDtypeStruct((768, 768), BF),
            jax.ShapeDtypeStruct((768, 768), BF),
        ],
        compiler_params=params(),
        name="embed",
    )(meta, x, gathered, smalls)


def head_lanes(values, head):
    lane = lax.broadcasted_iota(jnp.int32, values.shape, 1)
    keep = lane < 64 if head == 0 else lane >= 64
    return jnp.where(keep, values, jnp.zeros_like(values))


def attn_forward_part(q, k, value_t, limit):
    out_t, lse = [], []
    for head in range(2):
        scores = dot_nt(k, head_lanes(q, head))
        index = lax.broadcasted_iota(jnp.int32, scores.shape, 0)
        scores = jnp.where(index < limit, scores, NEG)
        top = jnp.max(scores, axis=0, keepdims=True)
        weight = jnp.exp(scores - top)
        total = jnp.sum(weight, axis=0, keepdims=True)
        probs = (weight * (1.0 / total)).astype(BF)
        out_t.append(dot_nn(value_t[64 * head : 64 * head + 64], probs))
        lse.append(top + jnp.log(total))
    return jnp.concatenate(out_t, axis=0).T.astype(BF), jnp.concatenate(lse, axis=0)


def attn_forward_kernel(meta, qkv_ref, out_ref, lse_ref):
    pair = lax.rem(pl.program_id(0), 3)

    def part(kind, start, size):
        lanes = pl.ds(pl.multiple_of(384 * kind + 128 * pair, 128), 128)
        return qkv_ref[start : start + size, lanes]

    @pl.when(is_short(meta))
    def _():
        for member in range(4):
            start = 256 * member
            q = part(0, start, 256) * BF(0.125)
            out, lse = attn_forward_part(
                q, part(1, start, 256), flip(part(2, start, 256)), meta[1 + member]
            )
            out_ref[start : start + 256, :] = out
            lse_ref[0, :, start : start + 256] = lse

    @pl.when(jnp.logical_not(is_short(meta)))
    def _():
        k = part(1, 0, 768)
        value_t = flip(part(2, 0, 768))
        for member in range(3):
            start = 256 * member
            q = part(0, start, 256) * BF(0.125)
            out, lse = attn_forward_part(q, k, value_t, meta[1])
            out_ref[start : start + 256, :] = out
            lse_ref[0, :, start : start + 256] = lse


def attn_forward(meta, qkv):
    return pl.pallas_call(
        attn_forward_kernel,
        grid_spec=pltpu.PrefetchScalarGridSpec(
            num_scalar_prefetch=1,
            grid=(6,),
            in_specs=[pl.BlockSpec((ROWS, 1152), lambda j, m: (0, j // 3))],
            out_specs=[
                pl.BlockSpec((ROWS, 128), lambda j, m: (0, j)),
                pl.BlockSpec((1, 2, ROWS), lambda j, m: (j, 0, 0)),
            ],
        ),
        out_shape=[
            jax.ShapeDtypeStruct((ROWS, 768), BF),
            jax.ShapeDtypeStruct((6, 2, ROWS), F32),
        ],
        compiler_params=params(),
        name="attn_forward",
    )(meta, qkv)


def attn_back_part(q, k, v, key_t, grad, lse, limit):
    grad_k, grad_v, grad_q = None, None, []
    for head in range(2):
        q_head = head_lanes(q, head)
        g_head = head_lanes(grad, head)
        scores = dot_nt(k, q_head)
        index = lax.broadcasted_iota(jnp.int32, scores.shape, 0)
        probs = jnp.exp(scores - lse[head : head + 1])
        probs = jnp.where(index < limit, probs, 0.0)
        grad_probs = dot_nt(v, g_head)
        row_dot = jnp.sum(probs * grad_probs, axis=0, keepdims=True)
        grad_scores = (probs * (grad_probs - row_dot)).astype(BF)
        add_v = dot_nn(probs.astype(BF), g_head)
        add_k = dot_nn(grad_scores, q_head)
        grad_v = add_v if grad_v is None else grad_v + add_v
        grad_k = add_k if grad_k is None else grad_k + add_k
        grad_q.append(dot_nn(key_t[64 * head : 64 * head + 64], grad_scores))
    return (jnp.concatenate(grad_q, axis=0).T * 0.125).astype(BF), grad_k, grad_v


def attn_back_kernel(meta, qkv_ref, grad_ref, lse_ref, out_ref, acc_k, acc_v):
    pair = lax.rem(pl.program_id(0), 3)

    def lanes(kind):
        return pl.ds(pl.multiple_of(384 * kind + 128 * pair, 128), 128)

    def part(kind, start, size):
        return qkv_ref[start : start + size, lanes(kind)]

    @pl.when(is_short(meta))
    def _():
        for member in range(4):
            rows = slice(256 * member, 256 * member + 256)
            start = 256 * member
            q = part(0, start, 256) * BF(0.125)
            k = part(1, start, 256)
            grad_q, grad_k, grad_v = attn_back_part(
                q, k, part(2, start, 256), flip(k), grad_ref[rows, :], lse_ref[0, :, rows], meta[1 + member]
            )
            out_ref[rows, lanes(0)] = grad_q
            out_ref[rows, lanes(1)] = grad_k.astype(BF)
            out_ref[rows, lanes(2)] = grad_v.astype(BF)

    @pl.when(jnp.logical_not(is_short(meta)))
    def _():
        k = part(1, 0, 768)
        v = part(2, 0, 768)
        key_t = flip(k)
        for member in range(3):
            rows = slice(256 * member, 256 * member + 256)
            start = 256 * member
            q = part(0, start, 256) * BF(0.125)
            grad_q, grad_k, grad_v = attn_back_part(
                q, k, v, key_t, grad_ref[rows, :], lse_ref[0, :, rows], meta[1]
            )
            out_ref[rows, lanes(0)] = grad_q
            if member == 0:
                acc_k[...] = grad_k
                acc_v[...] = grad_v
            else:
                acc_k[...] += grad_k
                acc_v[...] += grad_v
        out_ref[0:768, lanes(1)] = acc_k[...].astype(BF)
        out_ref[0:768, lanes(2)] = acc_v[...].astype(BF)


def attn_back(meta, qkv, grad, lse):
    return pl.pallas_call(
        attn_back_kernel,
        grid_spec=pltpu.PrefetchScalarGridSpec(
            num_scalar_prefetch=1,
            grid=(6,),
            in_specs=[
                pl.BlockSpec((ROWS, 1152), lambda j, m: (0, j // 3)),
                pl.BlockSpec((ROWS, 128), lambda j, m: (0, j)),
                pl.BlockSpec((1, 2, ROWS), lambda j, m: (j, 0, 0)),
            ],
            out_specs=pl.BlockSpec((ROWS, 1152), lambda j, m: (0, j // 3)),
            scratch_shapes=[pltpu.VMEM((768, 128), F32), pltpu.VMEM((768, 128), F32)],
        ),
        out_shape=jax.ShapeDtypeStruct((ROWS, 2304), BF),
        compiler_params=params(),
        name="attn_back",
    )(meta, qkv, grad, lse)


def mid_kernel(meta, att_ref, stream_ref, gat_ref, sm_ref, mid_ref, n2_ref, wout):
    step = pl.program_id(0)

    @pl.when(step == 0)
    def _():
        for half in range(2):
            for group in range(16):
                wout[48 * group : 48 * group + 48, 384 * half : 384 * half + 384] = gat_ref[
                    half_slot(meta, half), group_slot(meta, group)
                ]

    @pl.when(active(meta, step))
    def _():
        mid = stream_ref[...] + dot_nt(att_ref[...], wout[...]) + sm_ref[7:8, :]
        mid_ref[...] = mid
        xhat, _ = norm_parts(mid)
        n2_ref[...] = (xhat * sm_ref[8:9, :] + sm_ref[9:10, :]).astype(BF)


def mid_stage(meta, attended, stream, gathered, smalls):
    row = pl.BlockSpec((BLK, 768), lambda i, m: (i, 0))
    return pl.pallas_call(
        mid_kernel,
        grid_spec=pltpu.PrefetchScalarGridSpec(
            num_scalar_prefetch=1,
            grid=(4,),
            in_specs=[
                row,
                row,
                pl.BlockSpec((2, 16, 48, 384), lambda i, m: (0, 0, 0, 8)),
                pl.BlockSpec((16, 768), lambda i, m: (0, 0)),
            ],
            out_specs=[row, row],
            scratch_shapes=[pltpu.VMEM((768, 768), BF)],
        ),
        out_shape=[jax.ShapeDtypeStruct((ROWS, 768), F32), jax.ShapeDtypeStruct((ROWS, 768), BF)],
        compiler_params=params(),
        name="mid_stage",
    )(meta, attended, stream, gathered, smalls)


INV_ROOT2 = 0.7071067811865476
INV_ROOT2PI = 0.3989422804014327


def mlp_kernel(
    meta, n2_ref, cot_ref, up_ref, down_ref, bias_ref,
    out_ref, gn_ref, gup_ref, gdown_ref, gbias_ref,
    wup, wdown, n2_t, cot_t, hid, gpre,
):
    step = pl.program_id(0)
    rows_blocks = jnp.where(is_short(meta), 4, 3)

    for group in range(16):
        wup[48 * group : 48 * group + 48, :] = up_ref[0, group_slot(meta, group)]
        wdown[48 * group : 48 * group + 48, :] = down_ref[0, group_slot(meta, group)]

    @pl.when(step == 0)
    def _():
        for block in range(4):
            rows = slice(256 * block, 256 * block + 256)
            n2_t[:, rows] = flip(n2_ref[rows, :])
            cot_t[:, rows] = flip(cot_ref[rows, :])

    bias = bias_ref[0]

    def block_body(block, bias_sum):
        rows = pl.ds(pl.multiple_of(256 * block, 256), 256)
        pre = dot_nn(n2_ref[rows, :], wup[...]) + bias
        cdf = 0.5 + 0.5 * lax.erf(pre * INV_ROOT2)
        hidden = (pre * cdf).astype(BF)
        hid[rows, :] = hidden
        slope = cdf + pre * (jnp.exp(pre * pre * -0.5) * INV_ROOT2PI)
        grad_pre = (dot_nn(cot_ref[rows, :], wdown[...]) * slope).astype(BF)
        gpre[rows, :] = grad_pre
        out_add = dot_nt(hidden, wdown[...])
        gn_add = dot_nt(grad_pre, wup[...])

        @pl.when(step == 0)
        def _():
            out_ref[rows, :] = out_add
            gn_ref[rows, :] = gn_add

        @pl.when(step > 0)
        def _():
            out_ref[rows, :] += out_add
            gn_ref[rows, :] += gn_add

        return bias_sum + jnp.sum(grad_pre.astype(F32), axis=0, keepdims=True)

    gbias_ref[0] = lax.fori_loop(0, rows_blocks, block_body, jnp.zeros((1, 768), F32))

    for size, chosen in ((1024, is_short(meta)), (768, jnp.logical_not(is_short(meta)))):

        @pl.when(chosen)
        def _(size=size):
            put_pieces(meta, gup_ref, dot_nn(n2_t[:, 0:size], gpre[0:size, :]))
            put_pieces(meta, gdown_ref, dot_nn(cot_t[:, 0:size], hid[0:size, :]))


def mlp_stage(meta, n2, cot, gathered, up_bias):
    whole = pl.BlockSpec((ROWS, 768), lambda c, m: (0, 0))
    piece = (1, 16, 48, 768)
    half = lambda c, m: m[5 + c // 2]
    return pl.pallas_call(
        mlp_kernel,
        grid_spec=pltpu.PrefetchScalarGridSpec(
            num_scalar_prefetch=1,
            grid=(4,),
            in_specs=[
                whole,
                whole,
                pl.BlockSpec(piece, lambda c, m: (half(c, m), 0, 0, c % 2)),
                pl.BlockSpec(piece, lambda c, m: (half(c, m), 0, 0, 2 + c % 2)),
                pl.BlockSpec((1, 1, 768), lambda c, m: (c, 0, 0)),
            ],
            out_specs=[
                whole,
                whole,
                pl.BlockSpec(piece, lambda c, m: (half(c, m), 0, 0, c % 2)),
                pl.BlockSpec(piece, lambda c, m: (half(c, m), 0, 0, c % 2)),
                pl.BlockSpec((1, 1, 768), lambda c, m: (c, 0, 0)),
            ],
            scratch_shapes=[
                pltpu.VMEM((768, 768), BF),
                pltpu.VMEM((768, 768), BF),
                pltpu.VMEM((768, ROWS), BF),
                pltpu.VMEM((768, ROWS), BF),
                pltpu.VMEM((ROWS, 768), BF),
                pltpu.VMEM((ROWS, 768), BF),
            ],
        ),
        out_shape=[
            jax.ShapeDtypeStruct((ROWS, 768), F32),
            jax.ShapeDtypeStruct((ROWS, 768), F32),
            jax.ShapeDtypeStruct((2, 16, 48, 1536), BF),
            jax.ShapeDtypeStruct((2, 16, 48, 1536), BF),
            jax.ShapeDtypeStruct((4, 1, 768), F32),
        ],
        compiler_params=params(),
        name="mlp_stage",
    )(meta, n2, cot, gathered, gathered, up_bias)


def back_mid_kernel(
    meta, mlp_ref, gn_ref, mid_ref, cot_ref, att_ref, gat_ref, sm_ref,
    out_ref, gmid_ref, gatt_ref, gout_ref, sums_ref,
    wout, low_t,
):
    step = pl.program_id(0)

    @pl.when(step == 0)
    def _():
        sums_ref[...] = jnp.zeros_like(sums_ref)
        for half in range(2):
            for group in range(16):
                wout[48 * group : 48 * group + 48, 384 * half : 384 * half + 384] = gat_ref[
                    half_slot(meta, half), group_slot(meta, group)
                ]

    @pl.when(jnp.logical_and(active(meta, step), step < 4))
    def _():
        mid = mid_ref[...]
        out_ref[...] = (mid + mlp_ref[...] + sm_ref[10:11, :]).astype(BF)
        xhat, inverse = norm_parts(mid)
        grad = gn_ref[...]
        cot = cot_ref[...].astype(F32)
        grad_mid = cot + norm_back(xhat, inverse, grad * sm_ref[8:9, :])
        gmid_ref[...] = grad_mid
        low = grad_mid.astype(BF)
        gatt_ref[...] = dot_nn(low, wout[...]).astype(BF)
        low_t[step] = flip(low)
        sums_ref[0:1, :] += jnp.sum(grad_mid, axis=0, keepdims=True)
        sums_ref[1:2, :] += jnp.sum(grad * xhat, axis=0, keepdims=True)
        sums_ref[2:3, :] += jnp.sum(grad, axis=0, keepdims=True)
        sums_ref[3:4, :] += jnp.sum(cot, axis=0, keepdims=True)

    @pl.when(step >= 4)
    def _():
        half = step - 4
        for count, chosen in ((4, is_short(meta)), (3, jnp.logical_not(is_short(meta)))):

            @pl.when(chosen)
            def _(count=count):
                total = None
                for block in range(count):
                    add = dot_nn(
                        low_t[block],
                        att_ref[256 * block : 256 * block + 256, pl.ds(pl.multiple_of(384 * half, 128), 384)],
                    )
                    total = add if total is None else total + add
                put_pieces(meta, gout_ref, total)


def back_mid(meta, mlp_sum, grad_norm, mid, cot, attended, gathered, smalls):
    row = pl.BlockSpec((BLK, 768), lambda i, m: (jnp.minimum(i, 3), 0))
    return pl.pallas_call(
        back_mid_kernel,
        grid_spec=pltpu.PrefetchScalarGridSpec(
            num_scalar_prefetch=1,
            grid=(6,),
            in_specs=[
                row,
                row,
                row,
                row,
                pl.BlockSpec((ROWS, 768), lambda i, m: (0, 0)),
                pl.BlockSpec((2, 16, 48, 384), lambda i, m: (0, 0, 0, 8)),
                pl.BlockSpec((16, 768), lambda i, m: (0, 0)),
            ],
            out_specs=[
                row,
                row,
                row,
                pl.BlockSpec((1, 16, 48, 384), lambda i, m: (m[5 + jnp.maximum(i - 4, 0)], 0, 0, 0)),
                pl.BlockSpec((8, 768), lambda i, m: (0, 0)),
            ],
            scratch_shapes=[pltpu.VMEM((768, 768), BF), pltpu.VMEM((4, 768, 256), BF)],
        ),
        out_shape=[
            jax.ShapeDtypeStruct((ROWS, 768), BF),
            jax.ShapeDtypeStruct((ROWS, 768), F32),
            jax.ShapeDtypeStruct((ROWS, 768), BF),
            jax.ShapeDtypeStruct((2, 16, 48, 384), BF),
            jax.ShapeDtypeStruct((8, 768), F32),
        ],
        compiler_params=params(),
        name="back_mid",
    )(meta, mlp_sum, grad_norm, mid, cot, attended, gathered, smalls)


def back_in_kernel(
    meta, dqkv_ref, stream_ref, gmid_ref, gat_ref, sm_ref, low_ref, sums_ref, qsum_ref, wqkv
):
    step = pl.program_id(0)

    @pl.when(step == 0)
    def _():
        sums_ref[...] = jnp.zeros_like(sums_ref)
        qsum_ref[...] = jnp.zeros_like(qsum_ref)
        for half in range(2):
            for group in range(16):
                wqkv[half, 48 * group : 48 * group + 48, :] = gat_ref[
                    half_slot(meta, half), group_slot(meta, group), :, 0:1152
                ]

    @pl.when(active(meta, step))
    def _():
        dqkv = dqkv_ref[...]
        grad = dot_nt(dqkv[:, 0:1152], wqkv[0]) + dot_nt(dqkv[:, 1152:2304], wqkv[1])
        xhat, inverse = norm_parts(stream_ref[...])
        grad_in = gmid_ref[...] + norm_back(xhat, inverse, grad * sm_ref[3:4, :])
        low_ref[...] = grad_in.astype(BF)
        with_image = jnp.logical_or(is_short(meta), step == 0)
        limit = jnp.where(with_image, 198, 0)
        index = lax.broadcasted_iota(jnp.int32, (BLK, 768), 0)
        before = jnp.sum(jnp.where(index < limit, grad_in, 0.0), axis=0, keepdims=True)
        cls = jnp.where(with_image, grad_in[0:1], 0.0)
        everything = jnp.sum(grad_in, axis=0, keepdims=True)
        sums_ref[0:1, :] += before - cls
        sums_ref[1:2, :] += everything - before
        sums_ref[2:3, :] += cls
        sums_ref[3:4, :] += jnp.sum(grad * xhat, axis=0, keepdims=True)
        sums_ref[4:5, :] += jnp.sum(grad, axis=0, keepdims=True)
        qsum_ref[...] += jnp.sum(dqkv.astype(F32), axis=0, keepdims=True)


def back_in(meta, dqkv, stream, grad_mid, gathered, smalls):
    row = lambda width: pl.BlockSpec((BLK, width), lambda i, m: (i, 0))
    whole = lambda *shape: pl.BlockSpec(shape, lambda i, m: (0,) * len(shape))
    return pl.pallas_call(
        back_in_kernel,
        grid_spec=pltpu.PrefetchScalarGridSpec(
            num_scalar_prefetch=1,
            grid=(4,),
            in_specs=[row(2304), row(768), row(768), whole(*gathered.shape), whole(16, 768)],
            out_specs=[row(768), whole(8, 768), whole(1, 2304)],
            scratch_shapes=[pltpu.VMEM((2, 768, 1152), BF)],
        ),
        out_shape=[
            jax.ShapeDtypeStruct((ROWS, 768), BF),
            jax.ShapeDtypeStruct((8, 768), F32),
            jax.ShapeDtypeStruct((1, 2304), F32),
        ],
        compiler_params=params(),
        name="back_in",
    )(meta, dqkv, stream, grad_mid, gathered, smalls)


def proj_grad_kernel(meta, n1_ref, dqkv_ref, out_ref, n1_t):
    @pl.when(pl.program_id(0) == 0)
    def _():
        for block in range(4):
            rows = slice(256 * block, 256 * block + 256)
            n1_t[:, rows] = flip(n1_ref[rows, :])

    for size, chosen in ((1024, is_short(meta)), (768, jnp.logical_not(is_short(meta)))):

        @pl.when(chosen)
        def _(size=size):
            put_pieces(meta, out_ref, dot_nn(n1_t[:, 0:size], dqkv_ref[0:size, :]))


def proj_grad(meta, n1, dqkv):
    return pl.pallas_call(
        proj_grad_kernel,
        grid_spec=pltpu.PrefetchScalarGridSpec(
            num_scalar_prefetch=1,
            grid=(2,),
            in_specs=[
                pl.BlockSpec((ROWS, 768), lambda h, m: (0, 0)),
                pl.BlockSpec((ROWS, 1152), lambda h, m: (0, h)),
            ],
            out_specs=pl.BlockSpec((1, 16, 48, 1152), lambda h, m: (m[5 + h], 0, 0, 0)),
            scratch_shapes=[pltpu.VMEM((768, ROWS), BF)],
        ),
        out_shape=jax.ShapeDtypeStruct((2, 16, 48, 1152), BF),
        compiler_params=params(),
        name="proj_grad",
    )(meta, n1, dqkv)


def tower_grad_kernel(meta, x_ref, low_ref, small_ref, out_ref, x_t, gimg, gtext, wimg, wtext):
    for block in range(4):
        rows = slice(256 * block, 256 * block + 256)
        x_t[:, rows] = flip(x_ref[rows, :])
        with_image = jnp.logical_or(is_short(meta), block == 0)
        limit = jnp.where(with_image, 198, 0)
        index = lax.broadcasted_iota(jnp.int32, (BLK, 768), 0)
        low = low_ref[rows, :].astype(F32)
        gimg[rows, :] = jnp.where(index < limit, low, 0.0).astype(BF)
        gtext[rows, :] = jnp.where(index < limit, 0.0, low).astype(BF)

    for size, chosen in ((1024, is_short(meta)), (768, jnp.logical_not(is_short(meta)))):

        @pl.when(chosen)
        def _(size=size):
            wtext[...] = dot_nn(x_t[:, 0:size], gtext[0:size, :])
            image_size = size if size == 1024 else 256
            wimg[...] = dot_nn(x_t[:, 0:image_size], gimg[0:image_size, :])

    for half in range(2):
        for group in range(16):
            rows = slice(24 * (2 * group + half), 24 * (2 * group + half) + 24)
            piece = jnp.concatenate([wimg[rows, :], wtext[rows, :]], axis=0).astype(BF)
            hs, gs = half_slot(meta, half), group_slot(meta, group)
            out_ref[hs, gs, :, 0:768] = piece
            small = jnp.concatenate([small_ref[2 * group + half], jnp.zeros((40, 128), F32)], axis=0)
            out_ref[hs, gs, :, 768:896] = small.astype(BF)


def tower_grad(meta, x, low, small_pieces):
    whole = lambda *shape: pl.BlockSpec(shape, lambda i, m: (0,) * len(shape))
    return pl.pallas_call(
        tower_grad_kernel,
        grid_spec=pltpu.PrefetchScalarGridSpec(
            num_scalar_prefetch=1,
            grid=(1,),
            in_specs=[whole(ROWS, 768), whole(ROWS, 768), whole(32, 8, 128)],
            out_specs=whole(2, 16, 48, 896),
            scratch_shapes=[
                pltpu.VMEM((768, ROWS), BF),
                pltpu.VMEM((ROWS, 768), BF),
                pltpu.VMEM((ROWS, 768), BF),
                pltpu.VMEM((768, 768), F32),
                pltpu.VMEM((768, 768), F32),
            ],
        ),
        out_shape=jax.ShapeDtypeStruct((2, 16, 48, 896), BF),
        compiler_params=params(),
        name="tower_grad",
    )(meta, x, low, small_pieces)


def input_grad_kernel(gs_ref, gl_ref, wimg_ref, wtext_ref, si_ref, st_ref, li_ref, lt_ref, held):
    step = pl.program_id(0)

    @pl.when(step < 4)
    def _():
        held[0:208, :] = dot_nt(gs_ref[0:208, :], wimg_ref[...])
        si_ref[0] = held[1:198, :]
        held[0:64, :] = dot_nt(gs_ref[192:256, :], wtext_ref[...])
        st_ref[0] = held[6:64, :]

    @pl.when(step == 4)
    def _():
        held[0:208, :] = dot_nt(gl_ref[0:208, :], wimg_ref[...])
        li_ref[0] = held[1:198, :]
        held[0:576, :] = dot_nt(gl_ref[192:768, :], wtext_ref[...])
        lt_ref[0] = held[6:518, :]


def input_grad(grad_short, grad_long, wimg, wtext):
    pair = lambda i: (jnp.minimum(i, 3), 0, 0)
    return pl.pallas_call(
        input_grad_kernel,
        grid=(5,),
        in_specs=[
            pl.BlockSpec((BLK, 768), lambda i: (jnp.minimum(i, 3), 0)),
            pl.BlockSpec((768, 768), lambda i: (0, 0)),
            pl.BlockSpec((768, 768), lambda i: (0, 0)),
            pl.BlockSpec((768, 768), lambda i: (0, 0)),
        ],
        out_specs=[
            pl.BlockSpec((1, 197, 768), pair),
            pl.BlockSpec((1, 58, 768), pair),
            pl.BlockSpec((1, 197, 768), lambda i: (0, 0, 0)),
            pl.BlockSpec((1, 512, 768), lambda i: (0, 0, 0)),
        ],
        out_shape=[
            jax.ShapeDtypeStruct((4, 197, 768), F32),
            jax.ShapeDtypeStruct((4, 58, 768), F32),
            jax.ShapeDtypeStruct((1, 197, 768), F32),
            jax.ShapeDtypeStruct((1, 512, 768), F32),
        ],
        scratch_shapes=[pltpu.VMEM((576, 768), F32)],
        compiler_params=params(),
        name="input_grad",
    )(grad_short, grad_long, wimg, wtext)


def gather_pieces(shard):
    cols = shard.shape[1]
    if shard.shape[0] == 48:
        return lax.all_gather(shard, BOTH, axis=0, tiled=False).reshape(2, 16, 48, cols)
    return lax.all_gather(shard, BOTH, axis=0, tiled=True).reshape(2, 16, 48, cols)


def scatter_pieces(pieces):
    return lax.psum_scatter(pieces.reshape(2 * 768, pieces.shape[-1]), BOTH, scatter_dimension=0, tiled=True)


def small_shard(vectors, up_bias):
    flat = jnp.concatenate(list(vectors) + [up_bias])
    return flat


def on_device(
    short_images, short_texts, short_lengths, short_cotangent,
    long_images, long_texts, long_lengths, long_cotangent,
    img_weight, img_bias, text_weight, text_bias, cls_token, attn_gain, attn_shift,
    query_weight, query_bias, key_weight, value_weight, value_bias, out_weight, out_bias,
    mlp_gain, mlp_shift, up_weight, up_bias, down_weight, down_bias,
):
    half = lax.axis_index(TP)
    short = half == 1
    part = img_weight.shape[0]
    devices = 768 // part

    flat = jnp.concatenate(
        [img_bias, text_bias, cls_token, attn_gain, attn_shift, query_bias, value_bias, out_bias,
         mlp_gain, mlp_shift, down_bias, up_bias]
    )
    flat_all = lax.all_gather(flat, (DP, TP), axis=0, tiled=False)
    vectors = flat_all[:, : 11 * part].reshape(devices, 11, part).transpose(1, 0, 2).reshape(11, 768)
    up_bias_all = flat_all[:, 11 * part :].reshape(4, 1, 768).astype(F32)
    smalls = jnp.concatenate([vectors.astype(F32), jnp.zeros((5, 768), F32)])

    tower_shard = jnp.concatenate([img_weight, text_weight], axis=0)
    if part == 24:
        first_shard = jnp.concatenate([query_weight, key_weight, value_weight, tower_shard], axis=1)
        first = gather_pieces(first_shard)
    else:
        first_shard = jnp.concatenate([query_weight, key_weight, value_weight], axis=1)
        towers = lax.all_gather(jnp.concatenate([img_weight, text_weight], axis=1), (DP, TP), axis=0, tiled=True)
        towers = towers.reshape(16, 2, 24, 2, 768).transpose(1, 0, 3, 2, 4).reshape(2, 16, 48, 768)
        first = jnp.concatenate([gather_pieces(first_shard), towers], axis=-1)
    second = gather_pieces(jnp.concatenate([up_weight, down_weight.T, out_weight.T], axis=1))

    zero = jnp.zeros((4, 1, 768), BF)
    short_rows = jnp.concatenate([zero, short_images, short_texts], axis=1).reshape(ROWS, 768)
    long_rows = jnp.concatenate([zero[0, 0:1], long_images[0], long_texts[0], jnp.zeros((ROWS - 710, 768), BF)], axis=0)
    x = jnp.where(short, short_rows, long_rows)
    cot = jnp.where(
        short,
        short_cotangent.reshape(ROWS, 768),
        jnp.concatenate([long_cotangent[0], jnp.zeros((ROWS - 710, 768), BF)], axis=0),
    )
    limits = 198 + jnp.where(short, short_lengths, jnp.broadcast_to(long_lengths, (4,)))
    meta = jnp.concatenate(
        [
            half.astype(jnp.int32)[None],
            limits.astype(jnp.int32),
            jnp.arange(2, dtype=jnp.int32),
            jnp.arange(16, dtype=jnp.int32),
            jnp.zeros((1,), jnp.int32),
        ]
    )

    stream, n1, qkv, wimg, wtext = embed(meta, x, first, smalls)
    attended, lse = attn_forward(meta, qkv)
    mid, n2 = mid_stage(meta, attended, stream, second, smalls)
    mlp_sum, grad_norm, grad_up, grad_down, grad_up_bias = mlp_stage(meta, n2, cot, second, up_bias_all)
    red_up = scatter_pieces(grad_up)
    red_down = scatter_pieces(grad_down)
    out, grad_mid, grad_att, grad_out, sums_two = back_mid(
        meta, mlp_sum, grad_norm, mid, cot, attended, second, smalls
    )
    out_other = lax.ppermute(out, TP, [(0, 1), (1, 0)])
    red_out = scatter_pieces(grad_out)
    dqkv = attn_back(meta, qkv, grad_att, lse)
    low, sums_one, qkv_sums = back_in(meta, dqkv, stream, grad_mid, first, smalls)
    low_other = lax.ppermute(low, TP, [(0, 1), (1, 0)])
    red_qkv = scatter_pieces(proj_grad(meta, n1, dqkv))

    qkv_sums = qkv_sums.reshape(2, 3, 384)
    sums = jnp.concatenate(
        [sums_one[0:5], qkv_sums[:, 0].reshape(1, 768), qkv_sums[:, 2].reshape(1, 768),
         sums_two[0:3], sums_two[3:4]], axis=0
    )
    small_pieces = jnp.concatenate(
        [sums.reshape(11, 32, 24).transpose(1, 0, 2).reshape(32, 264), grad_up_bias.reshape(32, 96),
         jnp.zeros((32, 1024 - 360), F32)], axis=1
    ).reshape(32, 8, 128)
    towers = tower_grad(meta, x, low, small_pieces)
    if part == 24:
        red_tower = scatter_pieces(towers)
        red_img, red_text = red_tower[0:24, 0:768], red_tower[24:48, 0:768]
        red_small = red_tower[0:8, 768:896].reshape(-1)
        red_vectors = [red_small[24 * k : 24 * k + 24] for k in range(11)] + [red_small[264:360]]
    else:
        mats = towers[..., 0:768].reshape(2, 16, 2, 24, 768).transpose(2, 1, 0, 3, 4).reshape(2, 768, 768)
        red_img = lax.psum_scatter(mats[0], (DP, TP), scatter_dimension=0, tiled=True)
        red_text = lax.psum_scatter(mats[1], (DP, TP), scatter_dimension=0, tiled=True)
        red_vectors = [lax.psum_scatter(v, (DP, TP), scatter_dimension=0, tiled=True) for v in sums]
        red_vectors.append(lax.psum_scatter(grad_up_bias.reshape(3072), (DP, TP), scatter_dimension=0, tiled=True))

    short_output = jnp.where(short, out, out_other).reshape(4, 256, 768)
    long_output = jnp.where(short, out_other, out)[None, 0:710]
    grad_short = jnp.where(short, low, low_other)
    grad_long = jnp.where(short, low_other, low)[0:768]
    si, st, li, lt = input_grad(grad_short, grad_long, wimg, wtext)

    f = lambda v: v.astype(F32)
    vec = [f(v) for v in red_vectors]
    red_qkv = f(red_qkv)
    return (
        short_output, long_output, si, st, li, lt,
        f(red_img), vec[0], f(red_text), vec[1], vec[2], vec[3], vec[4],
        red_qkv[:, 0:384], vec[5], red_qkv[:, 384:768], red_qkv[:, 768:1152], vec[6],
        f(red_out).T, vec[7], vec[8], vec[9],
        f(red_up), vec[11], f(red_down).T, vec[10],
    )


def solution(mesh):
    rows = P(DP, None, None)
    vec = P((DP, TP))
    tower = P((DP, TP), None)
    col = P(DP, TP)
    back = P(TP, DP)
    return jax.shard_map(
        on_device,
        mesh=mesh,
        in_specs=(
            rows, rows, P(DP), rows, rows, rows, P(DP), rows,
            tower, vec, tower, vec, vec, vec, vec,
            col, vec, col, col, vec, back, vec, vec, vec, col, vec, back, vec,
        ),
        out_specs=(
            rows, rows, rows, rows, rows, rows,
            tower, vec, tower, vec, vec, vec, vec,
            col, vec, col, col, vec, back, vec, vec, vec, col, vec, back, vec,
        ),
        check_vma=False,
    )
```

```python
from functools import partial

import jax
import jax.numpy as jnp
from jax import lax
from jax.experimental import pallas as pl
from jax.experimental.pallas import tpu as pltpu
from jax.sharding import PartitionSpec as P

DP = "dp"
TP = "tensor"
BOTH = (TP, DP)
EPS = 1e-06
NEG = -1e30
BF = jnp.bfloat16
F32 = jnp.float32
ROWS = 1024
BLK = 256
MIB = 1 << 20


def dot_nn(left, right):
    return lax.dot_general(left, right, (((1,), (0,)), ((), ())), preferred_element_type=F32)


def dot_nt(left, right):
    return lax.dot_general(left, right, (((1,), (1,)), ((), ())), preferred_element_type=F32)


def flip(values):
    return values.astype(F32).T.astype(BF)


def cost(micros):
    return pl.CostEstimate(flops=int(micros * 2e8), bytes_accessed=int(micros * 1e5), transcendentals=0)


def params(limit=56):
    return pltpu.CompilerParams(dimension_semantics=("arbitrary",), vmem_limit_bytes=limit * MIB)


def whole(*shape):
    return pl.BlockSpec(shape, lambda *_: (0,) * len(shape), pipeline_mode=pl.Buffered(1))


def norm_parts(values):
    row_mean = jnp.mean(values, axis=-1, keepdims=True)
    centred = values - row_mean
    row_var = jnp.mean(centred * centred, axis=-1, keepdims=True)
    inverse = lax.rsqrt(row_var + EPS)
    return centred * inverse, inverse


def norm_back(xhat, inverse, scaled):
    first = jnp.mean(scaled, axis=-1, keepdims=True)
    second = jnp.mean(scaled * xhat, axis=-1, keepdims=True)
    return (scaled - first - xhat * second) * inverse


def is_short(meta):
    return meta[0] == 1


def active(meta, step):
    return jnp.logical_or(is_short(meta), step < 3)


CORE, X, LOW, HIGH, Y = 1, 2, 4, 8, 16
HALVES = ((LOW, X, HIGH), (X, LOW, HIGH))
TOWERS = (X, LOW, HIGH, Y)
GATHER_QKV = (Y, X, LOW, HIGH)
GATHER_TOWER = (X, Y, LOW, HIGH)
GATHER_UP = (Y, LOW, HIGH, X)
GATHER_DOWN = (X, LOW, HIGH, Y)


def relatives(meta, order):
    rest = [bit for bit in order if bit != Y]
    for core in range(2):
        for place in range(8):
            offset = core * CORE + sum(bit * (place >> (2 - k) & 1) for k, bit in enumerate(rest))
            yield core, place, jnp.bitwise_xor(meta[6], offset)


def places(meta, order):
    for core in range(2):
        for place in range(16):
            offset = core * CORE + sum(bit * (place >> (3 - k) & 1) for k, bit in enumerate(order))
            other = offset // 16
            yield core, place, jnp.bitwise_xor(meta[6], offset % 16), other, jnp.bitwise_xor(meta[5], other)


def hold_pieces(held, result):
    for group in range(16):
        held[group] = result[group * 48 : (group + 1) * 48].astype(BF)


def halves_shapes(width):
    return [jax.ShapeDtypeStruct((8, 48, width), BF)] * 2


def pack_kernel(q_ref, k_ref, v_ref, img_ref, text_ref, out_ref, small_ref, packed_ref):
    packed_ref[0, :, 0:384] = q_ref[...]
    packed_ref[0, :, 384:768] = k_ref[...]
    packed_ref[0, :, 768:1152] = v_ref[...]
    tower = jnp.concatenate([img_ref[...].astype(F32), text_ref[...].astype(F32)], axis=0)
    packed_ref[0, :, 1152:1920] = tower.astype(BF)
    packed_ref[0, :, 1920:2304] = out_ref[...]
    small = jnp.concatenate([small_ref[...].astype(F32), jnp.zeros((112, 24), F32)], axis=0).T
    packed_ref[0, :, 2304:2432] = jnp.concatenate([small, jnp.zeros((24, 128), F32)], axis=0).astype(BF)


def pack(*args):
    return pl.pallas_call(
        pack_kernel,
        grid=(1,),
        in_specs=[whole(*arg.shape) for arg in args],
        out_specs=whole(1, 48, 2432),
        out_shape=jax.ShapeDtypeStruct((1, 48, 2432), BF),
        compiler_params=params(8),
        name="pack",
        cost_estimate=cost(2),
    )(*args)


def prepare_kernel(x_ref, cot_ref, xt_ref, cott_ref, sum_ref):
    xt_ref[...] = flip(x_ref[...])
    cott_ref[...] = flip(cot_ref[...])

    @pl.when(pl.program_id(0) == 0)
    def _():
        sum_ref[...] = jnp.zeros_like(sum_ref)

    sum_ref[...] += jnp.sum(cot_ref[...].astype(F32), axis=0, keepdims=True)


def prepare(x, cot):
    row = pl.BlockSpec((BLK, 768), lambda i: (i, 0))
    column = pl.BlockSpec((768, BLK), lambda i: (0, i))
    return pl.pallas_call(
        prepare_kernel,
        grid=(4,),
        in_specs=[row, row],
        out_specs=[column, column, whole(1, 768)],
        out_shape=[
            jax.ShapeDtypeStruct((768, ROWS), BF),
            jax.ShapeDtypeStruct((768, ROWS), BF),
            jax.ShapeDtypeStruct((1, 768), F32),
        ],
        compiler_params=params(16),
        name="prepare",
        cost_estimate=cost(4),
    )(x, cot)


def embed_kernel(
    meta, x_ref, qkv_00, qkv_01, qkv_10, qkv_11, tower_00, tower_01, tower_10, tower_11,
    stream_ref, n1t_ref, qkv0_ref, qkv1_ref, wimg_ref, wtext_ref, wqkv_ref, wout_ref, sm_ref, bias_ref,
    wimg_f, wtext_f, wout_pieces, columns, up_columns,
):
    step = pl.program_id(0)
    qkv = (qkv_00, qkv_01), (qkv_10, qkv_11)
    towers = (tower_00, tower_01), (tower_10, tower_11)

    @pl.when(step == 0)
    def _():
        for core, place, group, other, _ in places(meta, GATHER_QKV):
            wqkv_ref[other, group] = qkv[core][place // 8][place % 8]
        for core, place, group, other, half in places(meta, GATHER_TOWER):
            tower = towers[core][place // 8].at[place % 8]
            piece = tower[:, 0:768].astype(F32)
            rows = pl.ds(pl.multiple_of(24 * (2 * group + half), 8), 24)
            wimg_f[rows, :] = piece[0:24]
            wtext_f[rows, :] = piece[24:48]
            wout_pieces[other, group] = tower[:, 768:1152]
            device = 2 * group + half
            small = tower[0:32, 1152:1280].astype(F32)[0:24]
            columns[rows, :] = small
            for part in range(4):
                start = pl.multiple_of(96 * device + 24 * part, 8)
                up_columns[pl.ds(start, 24), :] = pltpu.roll(small, 128 - 11 - part, 1)
        wimg_ref[...] = wimg_f[...].astype(BF)
        wtext_ref[...] = wtext_f[...].astype(BF)
        for half in range(2):
            wout_ref[:, 384 * half : 384 * half + 384] = wout_pieces[half].reshape(768, 384)
        sm_ref[...] = columns[...].T[0:16]
        for chunk in range(4):
            bias_ref[chunk] = up_columns[768 * chunk : 768 * chunk + 768, :].T[0:1]

    @pl.when(active(meta, step))
    def _():
        with_image = jnp.logical_or(is_short(meta), step == 0)

        @pl.when(with_image)
        def _():
            first = dot_nn(x_ref[0:208, :], wimg_ref[...]) + sm_ref[0:1, :]
            second = dot_nn(x_ref[192:256, :], wtext_ref[...]) + sm_ref[1:2, :]
            index = lax.broadcasted_iota(jnp.int32, (16, 768), 0)
            stream_ref[0:192, :] = first[0:192]
            stream_ref[192:208, :] = jnp.where(index < 6, first[192:208], second[0:16])
            stream_ref[208:256, :] = second[16:64]
            stream_ref[0:1, :] = sm_ref[2:3, :]

        @pl.when(jnp.logical_not(with_image))
        def _():
            stream_ref[...] = dot_nn(x_ref[...], wtext_ref[...]) + sm_ref[1:2, :]

        xhat, _ = norm_parts(stream_ref[...])
        scaled = xhat * sm_ref[3:4, :] + sm_ref[4:5, :]
        normed = scaled.astype(BF)
        n1t_ref[...] = flip(normed)
        for half, qkv_ref in enumerate((qkv0_ref, qkv1_ref)):
            out = dot_nn(normed, wqkv_ref[half].reshape(768, 1152))
            lanes = pl.ds(pl.multiple_of(384 * jnp.bitwise_xor(meta[5], half), 128), 384)
            qkv_ref[:, 0:384] = (out[:, 0:384] + sm_ref[5:6, lanes]).astype(BF)
            qkv_ref[:, 384:768] = out[:, 384:768].astype(BF)
            qkv_ref[:, 768:1152] = (out[:, 768:1152] + sm_ref[6:7, lanes]).astype(BF)


def embed(meta, x, qkv_all, tower_all):
    row = lambda width: pl.BlockSpec((BLK, width), lambda i, m: (i, 0))
    return pl.pallas_call(
        embed_kernel,
        grid_spec=pltpu.PrefetchScalarGridSpec(
            num_scalar_prefetch=1,
            grid=(4,),
            in_specs=[row(768)] + [whole(8, 48, 1152)] * 4 + [whole(8, 48, 1280)] * 4,
            out_specs=[
                row(768),
                pl.BlockSpec((768, BLK), lambda i, m: (0, i)),
                row(1152),
                row(1152),
                whole(768, 768),
                whole(768, 768),
                whole(2, 16, 48, 1152),
                whole(768, 768),
                whole(16, 768),
                whole(4, 1, 768),
            ],
            scratch_shapes=[
                pltpu.VMEM((768, 768), F32),
                pltpu.VMEM((768, 768), F32),
                pltpu.VMEM((2, 16, 48, 384), BF),
                pltpu.VMEM((768, 128), F32),
                pltpu.VMEM((3072, 128), F32),
            ],
        ),
        out_shape=[
            jax.ShapeDtypeStruct((ROWS, 768), F32),
            jax.ShapeDtypeStruct((768, ROWS), BF),
            jax.ShapeDtypeStruct((ROWS, 1152), BF),
            jax.ShapeDtypeStruct((ROWS, 1152), BF),
            jax.ShapeDtypeStruct((768, 768), BF),
            jax.ShapeDtypeStruct((768, 768), BF),
            jax.ShapeDtypeStruct((2, 16, 48, 1152), BF),
            jax.ShapeDtypeStruct((768, 768), BF),
            jax.ShapeDtypeStruct((16, 768), F32),
            jax.ShapeDtypeStruct((4, 1, 768), F32),
        ],
        compiler_params=params(44),
        name="embed",
        cost_estimate=cost(12),
    )(meta, x, *qkv_all, *tower_all)


def head_lanes(values, head):
    lane = lax.broadcasted_iota(jnp.int32, values.shape, 1)
    keep = lane < 64 if head == 0 else lane >= 64
    return jnp.where(keep, values, jnp.zeros_like(values))


def attn_forward_part(q, k, v, limit):
    out, lse = None, []
    for head in range(2):
        scores = dot_nt(head_lanes(q, head), k)
        index = lax.broadcasted_iota(jnp.int32, scores.shape, 1)
        scores = jnp.where(index < limit, scores, NEG)
        top = jnp.max(scores, axis=1, keepdims=True)
        weight = jnp.exp(scores - top)
        total = jnp.sum(weight, axis=1, keepdims=True)
        add = dot_nn(weight.astype(BF), head_lanes(v, head)) * (1.0 / total)
        out = add if out is None else out + add
        lse.append(jnp.broadcast_to(top + jnp.log(total), (256, 128)).T[0:1])
    return out.astype(BF), jnp.concatenate(lse, axis=0)


def attn_forward_kernel(meta, qkv_ref, out_ref, lse_ref):
    pair = pl.program_id(0)

    def part(kind, start, size):
        lanes = pl.ds(pl.multiple_of(384 * kind + 128 * pair, 128), 128)
        return qkv_ref[start : start + size, lanes]

    @pl.when(is_short(meta))
    def _():
        for member in range(4):
            start = 256 * member
            q = part(0, start, 256) * BF(0.125)
            out, lse = attn_forward_part(
                q, part(1, start, 256), part(2, start, 256), meta[1 + member]
            )
            out_ref[start : start + 256, :] = out
            lse_ref[0, :, start : start + 256] = lse

    @pl.when(jnp.logical_not(is_short(meta)))
    def _():
        k = part(1, 0, 768)
        v = part(2, 0, 768)
        for member in range(3):
            start = 256 * member
            q = part(0, start, 256) * BF(0.125)
            out, lse = attn_forward_part(q, k, v, meta[1])
            out_ref[start : start + 256, :] = out
            lse_ref[0, :, start : start + 256] = lse


def attn_forward(meta, qkv):
    return pl.pallas_call(
        attn_forward_kernel,
        grid_spec=pltpu.PrefetchScalarGridSpec(
            num_scalar_prefetch=1,
            grid=(3,),
            in_specs=[whole(ROWS, 1152)],
            out_specs=[
                pl.BlockSpec((ROWS, 128), lambda j, m: (0, j)),
                pl.BlockSpec((1, 2, ROWS), lambda j, m: (j, 0, 0)),
            ],
        ),
        out_shape=[
            jax.ShapeDtypeStruct((ROWS, 384), BF),
            jax.ShapeDtypeStruct((3, 2, ROWS), F32),
        ],
        compiler_params=params(20),
        name="attn_forward",
        cost_estimate=cost(14),
    )(meta, qkv)


def attn_back_part(q, k, v, grad, lse, limit):
    grad_k, grad_v, grad_q = None, None, None
    for head in range(2):
        q_head = head_lanes(q, head)
        g_head = head_lanes(grad, head)
        scores = dot_nt(k, q_head)
        index = lax.broadcasted_iota(jnp.int32, scores.shape, 0)
        probs = jnp.exp(scores - lse[head : head + 1])
        probs = jnp.where(index < limit, probs, 0.0)
        grad_probs = dot_nt(v, g_head)
        row_dot = jnp.sum(probs * grad_probs, axis=0, keepdims=True)
        grad_scores = (probs * (grad_probs - row_dot)).astype(BF)
        add_v = dot_nn(probs.astype(BF), g_head)
        add_k = dot_nn(grad_scores, q_head)
        grad_v = add_v if grad_v is None else grad_v + add_v
        grad_k = add_k if grad_k is None else grad_k + add_k
        add_q = lax.dot_general(
            grad_scores, head_lanes(k, head), (((0,), (0,)), ((), ())), preferred_element_type=F32
        )
        grad_q = add_q if grad_q is None else grad_q + add_q
    return (grad_q * 0.125).astype(BF), grad_k, grad_v


def attn_back_kernel(meta, qkv_ref, grad_ref, lse_ref, out_ref, acc_k, acc_v):
    pair = pl.program_id(0)

    def lanes(kind):
        return pl.ds(pl.multiple_of(384 * kind + 128 * pair, 128), 128)

    def part(kind, start, size):
        return qkv_ref[start : start + size, lanes(kind)]

    @pl.when(is_short(meta))
    def _():
        for member in range(4):
            rows = slice(256 * member, 256 * member + 256)
            start = 256 * member
            q = part(0, start, 256) * BF(0.125)
            k = part(1, start, 256)
            grad_q, grad_k, grad_v = attn_back_part(
                q, k, part(2, start, 256), grad_ref[rows, :], lse_ref[0, :, rows], meta[1 + member]
            )
            out_ref[rows, lanes(0)] = grad_q
            out_ref[rows, lanes(1)] = grad_k.astype(BF)
            out_ref[rows, lanes(2)] = grad_v.astype(BF)

    @pl.when(jnp.logical_not(is_short(meta)))
    def _():
        k = part(1, 0, 768)
        v = part(2, 0, 768)
        for member in range(3):
            rows = slice(256 * member, 256 * member + 256)
            start = 256 * member
            q = part(0, start, 256) * BF(0.125)
            grad_q, grad_k, grad_v = attn_back_part(
                q, k, v, grad_ref[rows, :], lse_ref[0, :, rows], meta[1]
            )
            out_ref[rows, lanes(0)] = grad_q
            if member == 0:
                acc_k[...] = grad_k
                acc_v[...] = grad_v
            else:
                acc_k[...] += grad_k
                acc_v[...] += grad_v
        out_ref[0:768, lanes(1)] = acc_k[...].astype(BF)
        out_ref[0:768, lanes(2)] = acc_v[...].astype(BF)


def attn_back(meta, qkv, grad, lse):
    return pl.pallas_call(
        attn_back_kernel,
        grid_spec=pltpu.PrefetchScalarGridSpec(
            num_scalar_prefetch=1,
            grid=(3,),
            in_specs=[
                whole(ROWS, 1152),
                pl.BlockSpec((ROWS, 128), lambda j, m: (0, j)),
                pl.BlockSpec((1, 2, ROWS), lambda j, m: (j, 0, 0)),
            ],
            out_specs=whole(ROWS, 1152),
            scratch_shapes=[pltpu.VMEM((768, 128), F32), pltpu.VMEM((768, 128), F32)],
        ),
        out_shape=jax.ShapeDtypeStruct((ROWS, 1152), BF),
        compiler_params=params(24),
        name="attn_back",
        cost_estimate=cost(15),
    )(meta, qkv, grad, lse)


def mid_kernel(meta, att0_ref, att1_ref, stream_ref, wout_ref, sm_ref, mid_ref, n2_ref, n2t_ref):
    @pl.when(active(meta, pl.program_id(0)))
    def _():
        attended = jnp.concatenate([att0_ref[...], att1_ref[...]], axis=1)
        mid = stream_ref[...] + dot_nt(attended, wout_ref[...]) + sm_ref[7:8, :]
        mid_ref[...] = mid
        xhat, _ = norm_parts(mid)
        normed = (xhat * sm_ref[8:9, :] + sm_ref[9:10, :]).astype(BF)
        n2_ref[...] = normed
        n2t_ref[...] = flip(normed)


def mid_stage(meta, attended, stream, wout, smalls):
    row = lambda width: pl.BlockSpec((BLK, width), lambda i, m: (i, 0))
    return pl.pallas_call(
        mid_kernel,
        grid_spec=pltpu.PrefetchScalarGridSpec(
            num_scalar_prefetch=1,
            grid=(4,),
            in_specs=[
                row(384),
                row(384),
                row(768),
                whole(768, 768),
                whole(16, 768),
            ],
            out_specs=[row(768), row(768), pl.BlockSpec((768, BLK), lambda i, m: (0, i))],
        ),
        out_shape=[
            jax.ShapeDtypeStruct((ROWS, 768), F32),
            jax.ShapeDtypeStruct((ROWS, 768), BF),
            jax.ShapeDtypeStruct((768, ROWS), BF),
        ],
        compiler_params=params(20),
        name="mid_stage",
        cost_estimate=cost(7),
    )(meta, *attended, stream, wout, smalls)


INV_ROOT2 = 0.7071067811865476
INV_ROOT2PI = 0.3989422804014327


def mlp_kernel(
    other,
    meta, n2_ref, n2_t, cot_ref, cot_t, up_near, up_far, down_00, down_01, down_10, down_11, bias_ref,
    out_ref, gn_ref, keep_ref, send_ref, gbias_ref,
    wup_pieces, wdown_pieces, hid, gpre, held, out_sum, gn_sum,
):
    step = pl.program_id(0)
    down = (down_00, down_01), (down_10, down_11)
    for core, place, group, half, _ in places(meta, GATHER_UP):
        if half == other:
            wup_pieces[group] = (up_near, up_far)[core][place % 8]
    for core, place, group, half, _ in places(meta, GATHER_DOWN):
        if half == other:
            wdown_pieces[group] = down[core][place // 8][place % 8 // 2, 0]
    bias = bias_ref[0]

    for size, chosen in ((1024, is_short(meta)), (768, jnp.logical_not(is_short(meta)))):

        @pl.when(chosen)
        def _(size=size):
            wup = wup_pieces[...].reshape(768, 768)
            wdown = wdown_pieces[...].reshape(768, 768)
            rows = slice(0, size)
            pre = dot_nn(n2_ref[rows, :], wup) + bias
            cdf = 0.5 + 0.5 * lax.erf(pre * INV_ROOT2)
            hid[rows, :] = (pre * cdf).astype(BF)
            slope = cdf + pre * (jnp.exp(pre * pre * -0.5) * INV_ROOT2PI)
            grad_pre = (dot_nn(cot_ref[rows, :], wdown) * slope).astype(BF)
            gpre[rows, :] = grad_pre
            gbias_ref[0] = jnp.sum(grad_pre.astype(F32), axis=0, keepdims=True)
            out_add = dot_nt(hid[rows, :], wdown)
            gn_add = dot_nt(gpre[rows, :], wup)

            @pl.when(step == 0)
            def _():
                out_sum[rows, :] = out_add
                gn_sum[rows, :] = gn_add

            @pl.when(step > 0)
            def _():
                out_ref[rows, :] = (out_sum[rows, :] + out_add).astype(BF)
                gn_ref[rows, :] = (gn_sum[rows, :] + gn_add).astype(BF)

            for kind, left, right in ((0, n2_t, gpre), (1, cot_t, hid)):
                hold_pieces(held, dot_nn(left[:, rows], right[rows, :]))
                lanes = slice(768 * kind, 768 * kind + 768)
                for core, place, group in relatives(meta, HALVES[other]):
                    (keep_ref, send_ref)[core][place, :, lanes] = held[group]


def mlp_half(meta, other, n2, n2_t, cot, cot_t, up_all, down_all, up_bias):
    rows, turned = whole(ROWS, 768), whole(768, ROWS)
    bias = pl.BlockSpec((1, 1, 768), lambda c, m: (2 * jnp.bitwise_xor(other, m[5]) + c, 0, 0))
    return pl.pallas_call(
        partial(mlp_kernel, other),
        grid_spec=pltpu.PrefetchScalarGridSpec(
            num_scalar_prefetch=1,
            grid=(2,),
            in_specs=[
                rows,
                turned,
                rows,
                turned,
                *[pl.BlockSpec((8, 48, 768), lambda c, m: (0, 0, c))] * 2,
                *[pl.BlockSpec((4, 1, 48, 768), lambda c, m: (0, other, 0, c))] * 4,
                bias,
            ],
            out_specs=[
                rows,
                rows,
                pl.BlockSpec((8, 48, 1536), lambda c, m: (0, 0, c)),
                pl.BlockSpec((8, 48, 1536), lambda c, m: (0, 0, c)),
                pl.BlockSpec((1, 1, 768), lambda c, m: (c, 0, 0)),
            ],
            scratch_shapes=[
                pltpu.VMEM((16, 48, 768), BF),
                pltpu.VMEM((16, 48, 768), BF),
                pltpu.VMEM((ROWS, 768), BF),
                pltpu.VMEM((ROWS, 768), BF),
                pltpu.VMEM((16, 48, 768), BF),
                pltpu.VMEM((ROWS, 768), F32),
                pltpu.VMEM((ROWS, 768), F32),
            ],
        ),
        out_shape=[
            jax.ShapeDtypeStruct((ROWS, 768), BF),
            jax.ShapeDtypeStruct((ROWS, 768), BF),
            *halves_shapes(3072),
            jax.ShapeDtypeStruct((2, 1, 768), F32),
        ],
        compiler_params=params(48),
        name="mlp_half",
        cost_estimate=cost(22),
    )(
        meta, n2, n2_t, cot, cot_t,
        up_all[other], up_all[2 + other],
        *(part.reshape(4, 2, 48, 1536) for part in down_all),
        up_bias,
    )


def back_mid_kernel(
    meta, mlp0_ref, gn0_ref, mlp1_ref, gn1_ref, mid_ref, cot_ref, att0_ref, att1_ref, wout_ref, sm_ref,
    out_ref, gmid_ref, gatt0_ref, gatt1_ref, gout0_keep, gout0_send, gout1_keep, gout1_send, sums_ref,
    low_t, held,
):
    step = pl.program_id(0)

    @pl.when(step == 0)
    def _():
        sums_ref[...] = jnp.zeros_like(sums_ref)

    @pl.when(jnp.logical_and(active(meta, step), step < 4))
    def _():
        mid = mid_ref[...]
        out_ref[...] = (mid + (mlp0_ref[...].astype(F32) + mlp1_ref[...].astype(F32)) + sm_ref[10:11, :]).astype(BF)
        xhat, inverse = norm_parts(mid)
        grad = gn0_ref[...].astype(F32) + gn1_ref[...].astype(F32)
        cot = cot_ref[...].astype(F32)
        grad_mid = cot + norm_back(xhat, inverse, grad * sm_ref[8:9, :])
        gmid_ref[...] = grad_mid
        low = grad_mid.astype(BF)
        grad_att = dot_nn(low, wout_ref[...]).astype(BF)
        gatt0_ref[...] = grad_att[:, 0:384]
        gatt1_ref[...] = grad_att[:, 384:768]
        low_t[step] = flip(low)
        sums_ref[0:1, :] += jnp.sum(grad_mid, axis=0, keepdims=True)
        sums_ref[1:2, :] += jnp.sum(grad * xhat, axis=0, keepdims=True)
        sums_ref[2:3, :] += jnp.sum(grad, axis=0, keepdims=True)

    for half, att_ref in enumerate((att0_ref, att1_ref)):
        for count, chosen in ((4, is_short(meta)), (3, jnp.logical_not(is_short(meta)))):

            @pl.when(jnp.logical_and(chosen, step == 4 + half))
            def _(count=count, att_ref=att_ref, half=half):
                total = None
                for block in range(count):
                    add = dot_nn(low_t[block], att_ref[256 * block : 256 * block + 256, :])
                    total = add if total is None else total + add
                hold_pieces(held, total)
                gouts = ((gout0_keep, gout0_send), (gout1_keep, gout1_send))[half]
                for core, place, group in relatives(meta, HALVES[half]):
                    gouts[core][place] = held[group]


def back_mid(meta, mlp_sums, mid, cot, attended, wout, smalls):
    row = pl.BlockSpec((BLK, 768), lambda i, m: (jnp.minimum(i, 3), 0))
    thin = pl.BlockSpec((BLK, 384), lambda i, m: (jnp.minimum(i, 3), 0))
    return pl.pallas_call(
        back_mid_kernel,
        grid_spec=pltpu.PrefetchScalarGridSpec(
            num_scalar_prefetch=1,
            grid=(6,),
            in_specs=[
                row,
                row,
                row,
                row,
                row,
                row,
                whole(ROWS, 384),
                whole(ROWS, 384),
                whole(768, 768),
                whole(16, 768),
            ],
            out_specs=[
                row,
                row,
                thin,
                thin,
                *[whole(8, 48, 384)] * 4,
                whole(8, 768),
            ],
            scratch_shapes=[
                pltpu.VMEM((4, 768, 256), BF),
                pltpu.VMEM((16, 48, 384), BF),
            ],
        ),
        out_shape=[
            jax.ShapeDtypeStruct((ROWS, 768), BF),
            jax.ShapeDtypeStruct((ROWS, 768), F32),
            jax.ShapeDtypeStruct((ROWS, 384), BF),
            jax.ShapeDtypeStruct((ROWS, 384), BF),
            *halves_shapes(384),
            *halves_shapes(384),
            jax.ShapeDtypeStruct((8, 768), F32),
        ],
        compiler_params=params(28),
        name="back_mid",
        cost_estimate=cost(13),
    )(meta, *mlp_sums, mid, cot, *attended, wout, smalls)


def back_in_kernel(
    meta, dqkv0_ref, dqkv1_ref, stream_ref, gmid_ref, wqkv_ref, sm_ref, low_ref, sums_ref, qsum_ref
):
    step = pl.program_id(0)

    @pl.when(step == 0)
    def _():
        sums_ref[...] = jnp.zeros_like(sums_ref)
        qsum_ref[...] = jnp.zeros_like(qsum_ref)

    @pl.when(active(meta, step))
    def _():
        grad = None
        for half, dqkv_ref in enumerate((dqkv0_ref, dqkv1_ref)):
            dqkv = dqkv_ref[...]
            add = dot_nt(dqkv, wqkv_ref[half].reshape(768, 1152))
            grad = add if grad is None else grad + add
            qsum_ref[half : half + 1, :] += jnp.sum(dqkv.astype(F32), axis=0, keepdims=True)
        xhat, inverse = norm_parts(stream_ref[...])
        grad_in = gmid_ref[...] + norm_back(xhat, inverse, grad * sm_ref[3:4, :])
        low_ref[...] = grad_in.astype(BF)
        with_image = jnp.logical_or(is_short(meta), step == 0)
        limit = jnp.where(with_image, 198, 0)
        index = lax.broadcasted_iota(jnp.int32, (BLK, 768), 0)
        before = jnp.sum(jnp.where(index < limit, grad_in, 0.0), axis=0, keepdims=True)
        cls = jnp.where(with_image, grad_in[0:1], 0.0)
        everything = jnp.sum(grad_in, axis=0, keepdims=True)
        sums_ref[0:1, :] += before - cls
        sums_ref[1:2, :] += everything - before
        sums_ref[2:3, :] += cls
        sums_ref[3:4, :] += jnp.sum(grad * xhat, axis=0, keepdims=True)
        sums_ref[4:5, :] += jnp.sum(grad, axis=0, keepdims=True)


def back_in(meta, dqkv, stream, grad_mid, wqkv, smalls):
    row = lambda width: pl.BlockSpec((BLK, width), lambda i, m: (i, 0))
    return pl.pallas_call(
        back_in_kernel,
        grid_spec=pltpu.PrefetchScalarGridSpec(
            num_scalar_prefetch=1,
            grid=(4,),
            in_specs=[row(1152), row(1152), row(768), row(768), whole(2, 16, 48, 1152), whole(16, 768)],
            out_specs=[row(768), whole(8, 768), whole(2, 1152)],
        ),
        out_shape=[
            jax.ShapeDtypeStruct((ROWS, 768), BF),
            jax.ShapeDtypeStruct((8, 768), F32),
            jax.ShapeDtypeStruct((2, 1152), F32),
        ],
        compiler_params=params(24),
        name="back_in",
        cost_estimate=cost(11),
    )(meta, *dqkv, stream, grad_mid, wqkv, smalls)


def proj_grad_kernel(other, meta, n1t_ref, dqkv_ref, gout_keep, gout_send, keep_ref, send_ref, held):
    step = pl.program_id(0)
    for size, chosen in ((1024, is_short(meta)), (768, jnp.logical_not(is_short(meta)))):

        @pl.when(jnp.logical_and(chosen, step < 3))
        def _(size=size):
            hold_pieces(held, dot_nn(n1t_ref[:, 0:size], dqkv_ref[0:size, :]))
            for core, place, group in relatives(meta, HALVES[other]):
                (keep_ref, send_ref)[core][place] = held[group]

    @pl.when(step == 3)
    def _():
        keep_ref[...] = gout_keep[...]
        send_ref[...] = gout_send[...]


def proj_grad(meta, other, n1_t, dqkv, grad_out):
    columns = pl.BlockSpec((8, 48, 384), lambda c, m: (0, 0, c))
    return pl.pallas_call(
        partial(proj_grad_kernel, other),
        grid_spec=pltpu.PrefetchScalarGridSpec(
            num_scalar_prefetch=1,
            grid=(4,),
            in_specs=[
                whole(768, ROWS),
                pl.BlockSpec((ROWS, 384), lambda c, m: (0, jnp.minimum(c, 2))),
                whole(8, 48, 384),
                whole(8, 48, 384),
            ],
            out_specs=[columns, columns],
            scratch_shapes=[pltpu.VMEM((16, 48, 384), BF)],
        ),
        out_shape=halves_shapes(1536),
        compiler_params=params(20),
        name="proj_grad",
        cost_estimate=cost(5),
    )(meta, n1_t, dqkv, *grad_out)


def tower_grad_kernel(
    meta, x_t, low_ref, one_ref, two_ref, qkv_ref, down_ref, up0_ref, up1_ref,
    keep_ref, send_ref, gimg, gtext, wimg, wtext, vectors, columns,
):
    vectors[...] = jnp.zeros_like(vectors)
    vectors[0:5, :] = one_ref[0:5, :]
    for half in range(2):
        lanes = pl.ds(pl.multiple_of(384 * jnp.bitwise_xor(meta[5], half), 128), 384)
        vectors[5:6, lanes] = qkv_ref[half : half + 1, 0:384]
        vectors[6:7, lanes] = qkv_ref[half : half + 1, 768:1152]
    vectors[7:10, :] = two_ref[0:3, :]
    vectors[10:11, :] = down_ref[...]
    for half, up_ref in enumerate((up0_ref, up1_ref)):
        for chunk in range(2):
            vectors[pl.ds(11 + 2 * jnp.bitwise_xor(meta[5], half) + chunk, 1), :] = up_ref[chunk]
    columns[...] = vectors[...].T
    for block in range(4):
        rows = slice(256 * block, 256 * block + 256)
        with_image = jnp.logical_or(is_short(meta), block == 0)
        limit = jnp.where(with_image, 198, 0)
        index = lax.broadcasted_iota(jnp.int32, (BLK, 768), 0)
        low = low_ref[rows, :].astype(F32)
        gimg[rows, :] = jnp.where(index < limit, low, 0.0).astype(BF)
        gtext[rows, :] = jnp.where(index < limit, 0.0, low).astype(BF)

    for size, chosen in ((1024, is_short(meta)), (768, jnp.logical_not(is_short(meta)))):

        @pl.when(chosen)
        def _(size=size):
            wtext[...] = dot_nn(x_t[:, 0:size], gtext[0:size, :])
            image_size = size if size == 1024 else 256
            wimg[...] = dot_nn(x_t[:, 0:image_size], gimg[0:image_size, :])

    lane = lax.broadcasted_iota(jnp.int32, (24, 128), 1)
    for core, place, group in relatives(meta, TOWERS):
        ref = (keep_ref, send_ref)[core]
        for half in range(2):
            device = 2 * group + jnp.bitwise_xor(meta[5], half)
            rows = pl.ds(pl.multiple_of(24 * device, 8), 24)
            piece = jnp.concatenate([wimg[rows, :], wtext[rows, :]], axis=0).astype(BF)
            ref[place, half, :, 0:768] = piece
            small = jnp.where(lane < 11, columns[rows, :], 0.0)
            for part in range(4):
                start = 96 * jnp.bitwise_and(device, 7) + 24 * part
                some = columns[pl.ds(pl.multiple_of(start, 8), 24), :]
                some = jnp.where(lane == 11 + lax.shift_right_logical(device, 3), some, 0.0)
                small += some if part == 0 else pltpu.roll(some, part, 1)
            ref[place, half, :, 768:896] = jnp.concatenate([small, jnp.zeros_like(small)], axis=0).astype(BF)


def tower_grad(meta, x_t, low, *sums):
    return pl.pallas_call(
        tower_grad_kernel,
        grid_spec=pltpu.PrefetchScalarGridSpec(
            num_scalar_prefetch=1,
            grid=(1,),
            in_specs=[
                whole(768, ROWS),
                whole(ROWS, 768),
                whole(8, 768),
                whole(8, 768),
                whole(2, 1152),
                whole(1, 768),
                whole(2, 1, 768),
                whole(2, 1, 768),
            ],
            out_specs=[whole(8, 2, 48, 896)] * 2,
            scratch_shapes=[
                pltpu.VMEM((ROWS, 768), BF),
                pltpu.VMEM((ROWS, 768), BF),
                pltpu.VMEM((768, 768), F32),
                pltpu.VMEM((768, 768), F32),
                pltpu.VMEM((128, 768), F32),
                pltpu.VMEM((768, 128), F32),
            ],
        ),
        out_shape=[jax.ShapeDtypeStruct((8, 2, 48, 896), BF)] * 2,
        compiler_params=params(24),
        name="tower_grad",
        cost_estimate=cost(7),
    )(meta, x_t, low, *sums)


def input_grad_kernel(own, meta, rows_ref, wimg_ref, wtext_ref, si_ref, st_ref, li_ref, lt_ref, held):
    step = pl.program_id(0)
    short = is_short(meta) if own else jnp.logical_not(is_short(meta))

    @pl.when(short)
    def _():
        start = pl.multiple_of(256 * step, 256)
        held[0:208, :] = dot_nt(rows_ref[pl.ds(start, 208), :], wimg_ref[...])
        si_ref[0] = held[1:198, :]
        held[0:64, :] = dot_nt(rows_ref[pl.ds(start + 192, 64), :], wtext_ref[...])
        st_ref[0] = held[6:64, :]

    @pl.when(jnp.logical_and(jnp.logical_not(short), step == 0))
    def _():
        held[0:208, :] = dot_nt(rows_ref[0:208, :], wimg_ref[...])
        li_ref[0] = held[1:198, :]

    @pl.when(jnp.logical_and(jnp.logical_not(short), step == 1))
    def _():
        held[0:576, :] = dot_nt(rows_ref[192:768, :], wtext_ref[...])
        lt_ref[0] = held[6:518, :]


def input_grad(meta, own, rows, wimg, wtext):
    pair = lambda i, m: (i * (m[0] if own else 1 - m[0]), 0, 0)
    return pl.pallas_call(
        partial(input_grad_kernel, own),
        grid_spec=pltpu.PrefetchScalarGridSpec(
            num_scalar_prefetch=1,
            grid=(4,),
            in_specs=[whole(ROWS, 768), whole(768, 768), whole(768, 768)],
            out_specs=[
                pl.BlockSpec((1, 197, 768), pair),
                pl.BlockSpec((1, 58, 768), pair),
                whole(1, 197, 768),
                whole(1, 512, 768),
            ],
            scratch_shapes=[pltpu.VMEM((576, 768), F32)],
        ),
        out_shape=[
            jax.ShapeDtypeStruct((4, 197, 768), F32),
            jax.ShapeDtypeStruct((4, 58, 768), F32),
            jax.ShapeDtypeStruct((1, 197, 768), F32),
            jax.ShapeDtypeStruct((1, 512, 768), F32),
        ],
        compiler_params=params(16),
        name="input_grad",
        cost_estimate=cost(5),
    )(meta, rows, wimg, wtext)


def swap(values, bits):
    if bits == Y:
        return lax.ppermute(values, TP, [(0, 1), (1, 0)])
    if bits < Y:
        return lax.ppermute(values, DP, [(i, i ^ bits) for i in range(16)])
    step = 2 * (bits - Y) + 1
    return lax.ppermute(values, (DP, TP), [(i, i ^ step) for i in range(32)])


def after(values, *others):
    return lax.optimization_barrier((values, *others))[0]


def plus(left, right):
    return (left.astype(F32) + right.astype(F32)).astype(BF)


def absolute(arrays, order):
    width = arrays[0].shape[-1]
    both = jnp.stack(arrays).reshape(2, *(2 for _ in order), 48, width)
    at = {bit: 1 + k for k, bit in enumerate(order)}
    first = [at[Y]] if Y in at else []
    both = both.transpose(*first, at[HIGH], at[LOW], at[X], 0, len(order) + 1, len(order) + 2)
    return both.reshape(-1, width)


class Scatter:
    def __init__(self, pieces, order):
        self.order = (CORE, *order)
        self.arrived = None
        if lax.axis_size(DP) != 16:
            rows = absolute(pieces, order)
            self.total = lax.psum_scatter(rows, BOTH, scatter_dimension=0, tiled=True).astype(F32)
            self.order = ()
            return
        shape = (2, 2, 2, 2, 48, pieces[0].shape[-1])
        self.keep, self.sent = pieces[0].reshape(shape), pieces[1].reshape(shape)

    def send(self):
        if self.order:
            self.arrived = swap(self.sent, self.order[0])

    def add(self):
        if self.order:
            if len(self.order) == 1:
                self.total = self.keep.astype(F32) + self.arrived.astype(F32)
            else:
                self.keep, self.sent = plus(self.keep[0], self.arrived[0]), plus(self.keep[1], self.arrived[1])
            self.arrived = None
            self.order = self.order[1:]


class Half:
    def __init__(self, pieces, other):
        self.other = other
        self.order = (CORE, *HALVES[other][0:2])
        self.arrived = None
        self.pieces = pieces
        if lax.axis_size(DP) != 16:
            self.order = ()
            return
        shape = (2, 2, 2, 48, pieces[0].shape[-1])
        self.keep, self.sent = pieces[0].reshape(shape), pieces[1].reshape(shape)

    def send(self):
        if self.order:
            self.arrived = swap(self.sent, self.order[0])

    def add(self):
        if self.order:
            self.order = self.order[1:]
            if self.order:
                self.keep, self.sent = plus(self.keep[0], self.arrived[0]), plus(self.keep[1], self.arrived[1])
            else:
                self.keep = plus(self.keep, self.arrived)
            self.arrived = None


class Cross:
    def __init__(self, own, other):
        self.own, self.other = own, other
        self.arrived = None
        self.order = (Y, HIGH)
        if lax.axis_size(DP) != 16:
            rows = jnp.concatenate([absolute(half.pieces, HALVES[half.other]) for half in (own, other)])
            self.total = lax.psum_scatter(rows, BOTH, scatter_dimension=0, tiled=True).astype(F32)
            self.order = ()

    def send(self):
        if self.order and self.order[0] == Y and not self.other.order:
            self.arrived = swap(self.other.keep, Y)
        elif self.order and self.order[0] == HIGH and not self.own.order:
            self.sent = plus(self.own.keep[1], self.crossed[1])
            self.arrived = swap(self.sent, HIGH)

    def add(self):
        if self.order and self.order[0] == Y:
            self.crossed = self.arrived
        elif self.order:
            keep = self.own.keep[0].astype(F32) + self.crossed[0].astype(F32)
            self.total = keep + self.arrived.astype(F32)
        self.arrived = None
        self.order = self.order[1:]


class Gather:
    def __init__(self, joined, widths, phases, orders, whole=None):
        self.joined, self.widths, self.phases = joined, widths, phases
        self.parts = None if joined is None else self.split(joined)
        self.arrived = None
        if lax.axis_size(DP) != 16:
            if whole is None:
                whole = lax.all_gather(joined[0], BOTH, axis=0, tiled=True)
            rows = whole.reshape(2, 2, 2, 2, 2, 48, sum(widths))
            at = {Y: 0, HIGH: 1, LOW: 2, X: 3}
            self.rows = tuple(
                tuple(self.split(rows.transpose(4, *(at[bit] for bit in order), 5, 6).reshape(4, 8, 48, -1))[kind])
                for kind, order in enumerate(orders)
            )
            self.phases = ()

    def split(self, values):
        return values[..., : self.widths[0]], values[..., self.widths[0] :]

    def send(self):
        if not self.phases:
            return
        if self.phases[0] in (HIGH, LOW):
            if self.joined is None:
                self.joined = jnp.concatenate(self.parts, axis=-1)
            self.arrived = swap(self.joined, self.phases[0])
            return
        first, second = self.parts
        if self.phases[0] == X:
            self.arrived = swap(first, X), swap(second, Y)
        elif self.phases[0] == Y:
            self.arrived = swap(first, Y), swap(second, X)
        else:
            self.arrived = tuple(tuple(swap(part, CORE) for part in rows) for rows in self.rows)

    def add(self):
        joined = None
        if self.phases[0] == HIGH:
            joined = jnp.concatenate([self.joined, self.arrived], axis=0)
        elif self.phases[0] == LOW:
            pieces = self.split(self.joined), self.split(self.arrived)
            self.parts = tuple(jnp.concatenate([piece[kind] for piece in pieces], axis=0) for kind in range(2))
        elif self.phases[0] == X:
            self.parts = tuple(jnp.concatenate(pair, axis=0) for pair in zip(self.parts, self.arrived))
        elif self.phases[0] == Y:
            self.rows = tuple(zip(self.parts, self.arrived))
        else:
            self.rows = tuple(near + far for near, far in zip(self.rows, self.arrived))
        self.joined, self.arrived = joined, None
        self.phases = self.phases[1:]


def seal(values, movers, swaps=()):
    flying = [mover for mover in movers if mover.arrived is not None]
    values, arrived, swaps = lax.optimization_barrier(
        (tuple(values), tuple(mover.arrived for mover in flying), tuple(swaps))
    )
    for mover, data in zip(flying, arrived):
        mover.arrived = data
        mover.add()
    for mover in movers:
        mover.send()
    return values, swaps


def on_device(
    short_images, short_texts, short_lengths, short_cotangent,
    long_images, long_texts, long_lengths, long_cotangent,
    img_weight, img_bias, text_weight, text_bias, cls_token, attn_gain, attn_shift,
    query_weight, query_bias, key_weight, value_weight, value_bias, out_weight, out_bias,
    mlp_gain, mlp_shift, up_weight, up_bias, down_weight, down_bias,
):
    half = lax.axis_index(TP)
    short = half == 1
    part = img_weight.shape[0]
    devices = 768 // part
    grouped = lax.axis_size(DP) == 16

    vectors = [img_bias, text_bias, cls_token, attn_gain, attn_shift, query_bias, value_bias, out_bias,
               mlp_gain, mlp_shift, down_bias]
    if grouped:
        small = jnp.concatenate([jnp.stack(vectors), up_bias.reshape(4, 24), jnp.zeros((1, 24), BF)])
        shard = pack(query_weight, key_weight, value_weight, img_weight, text_weight, out_weight.T, small)
        towers = None
    else:
        every = lambda v: lax.all_gather(v, (DP, TP), axis=0, tiled=True)
        towers = every(jnp.concatenate([img_weight, text_weight], axis=1))
        towers = towers.reshape(16, 2, 24, 2, 768).transpose(1, 0, 3, 2, 4).reshape(2, 768, 768)
        columns = jnp.stack([every(v) for v in vectors]).reshape(11, 32, 24).transpose(1, 2, 0)
        columns = jnp.concatenate([columns, every(up_bias).reshape(32, 4, 24).transpose(0, 2, 1)], axis=2)
        columns = jnp.pad(columns, ((0, 0), (0, 24), (0, 113)))
        columns = columns.reshape(16, 2, 48, 128).transpose(1, 0, 2, 3).reshape(2, 768, 128)
        outs = lax.all_gather(out_weight.T, BOTH, axis=0, tiled=True).reshape(2, 768, 384)
        towers = jnp.concatenate([towers, outs, columns], axis=2)
        qkv = jnp.concatenate([query_weight, key_weight, value_weight], axis=1)
        towers = jnp.concatenate([lax.all_gather(qkv, BOTH, axis=0, tiled=True).reshape(2, 768, 1152), towers], axis=2)
        shard = None
    joined = None if grouped else jnp.concatenate([up_weight, down_weight.T], axis=1)[None]
    first_gather = Gather(shard, (1152, 1280), (HIGH, LOW, X, Y, CORE), (GATHER_QKV, GATHER_TOWER), towers)
    wide_gather = Gather(joined, (1536, 1536), (X, HIGH, LOW, Y, CORE), (GATHER_UP, GATHER_DOWN))
    wide_gather.parts = up_weight[None], down_weight.T[None]
    near, wide = [first_gather], [wide_gather]
    first_gather.send()
    wide_gather.send()
    seal((), near + wide)
    seal((), near)
    seal((), near + wide)

    zero = jnp.zeros((4, 1, 768), BF)
    short_rows = jnp.concatenate([zero, short_images, short_texts], axis=1).reshape(ROWS, 768)
    long_rows = jnp.concatenate([zero[0, 0:1], long_images[0], long_texts[0], jnp.zeros((ROWS - 710, 768), BF)], axis=0)
    x = jnp.where(short, short_rows, long_rows)
    cot = jnp.where(
        short,
        short_cotangent.reshape(ROWS, 768),
        jnp.concatenate([long_cotangent[0], jnp.zeros((ROWS - 710, 768), BF)], axis=0),
    )
    place = lax.axis_index(DP) if grouped else jnp.int32(0)
    half_place = half.astype(jnp.int32) if grouped else jnp.int32(0)
    limits = 198 + jnp.where(short, short_lengths, jnp.broadcast_to(long_lengths, (4,)))
    meta = jnp.concatenate(
        [
            half.astype(jnp.int32)[None],
            limits.astype(jnp.int32),
            half_place[None],
            place.astype(jnp.int32)[None],
            jnp.zeros((1,), jnp.int32),
        ]
    )

    x_t, cot_t, cot_sum = prepare(x, cot)
    (x, cot, x_t, cot_t, meta), _ = seal((x, cot, x_t, cot_t, meta), near)
    seal((), near)
    (x,), _ = seal((x,), near + wide)
    stream, n1_t, qkv0, qkv1, wimg, wtext, wqkv, wout, smalls, up_bias_all = embed(
        meta, x, *first_gather.rows
    )
    att1, lse1 = attn_forward(meta, qkv1)
    (att1, qkv0), _ = seal((att1, qkv0), wide)
    att0, lse0 = attn_forward(meta, qkv0)
    mid, n2, n2_t = mid_stage(meta, (att0, att1), stream, wout, smalls)
    (n2,), _ = seal((n2,), wide)
    weights = (*wide_gather.rows, up_bias_all)
    mlp1, gn1, *rest = mlp_half(meta, 1, n2, n2_t, cot, cot_t, *weights)
    ff_other, grad_up_bias1 = Half(rest[0:2], 1), rest[2]
    ff_other.send()
    mlp0, gn0, *rest = mlp_half(meta, 0, after(n2, mlp1), n2_t, cot, cot_t, *weights)
    (mlp0, *rest), _ = seal((mlp0, *rest), [ff_other])
    ff_own, grad_up_bias0 = Half(rest[0:2], 0), rest[2]
    ff_own.send()
    ff = Cross(ff_own, ff_other)
    out, grad_mid, gatt0, gatt1, *rest = back_mid(
        meta, (mlp0, gn0, mlp1, gn1), mid, cot, (att0, att1), wout, smalls
    )
    gout0, gout1, sums_two = rest[0:2], rest[2:4], rest[4]
    (out, gatt0, gatt1), _ = seal((out, gatt0, gatt1), [ff_own])
    out_other = swap(out, Y)
    dqkv1 = attn_back(meta, qkv1, gatt1, lse1)
    (dqkv1,), _ = seal((dqkv1,), [ff_other])
    proj_other = Half(proj_grad(meta, 1, n1_t, dqkv1, gout1), 1)
    proj_other.send()
    dqkv0 = attn_back(meta, qkv0, after(gatt0, *proj_other.pieces), lse0)
    (dqkv0,), (out_other,) = seal((dqkv0,), [ff_own, ff_other, proj_other], (out_other,))
    ff.send()
    rest = proj_grad(meta, 0, n1_t, dqkv0, gout0)
    (dqkv0, *rest), _ = seal((dqkv0, *rest), [])
    proj_own = Half(rest, 0)
    proj_own.send()
    proj = Cross(proj_own, proj_other)
    low, sums_one, qkv_sums = back_in(meta, (dqkv0, dqkv1), stream, grad_mid, wqkv, smalls)
    (low,), _ = seal((low,), [proj_own])
    low_other = swap(low, Y)
    towers = tower_grad(meta, x_t, low, sums_one, sums_two, qkv_sums, cot_sum, grad_up_bias0, grad_up_bias1)
    tower = Scatter(towers, TOWERS)
    tower.send()
    (out, out_other, low), _ = lax.optimization_barrier(((out, out_other, low), towers))
    mine = input_grad(meta, True, low, wimg, wtext)
    short_output = jnp.where(short, out, out_other).reshape(4, 256, 768)
    long_output = jnp.where(short, out_other, out)[None, 0:710]
    (short_output, long_output, *mine), _ = seal(
        (short_output, long_output, *mine), [ff_own, ff, proj_other, tower]
    )
    seal((), [proj_own, proj_other])
    proj.send()
    (low_other,), _ = seal((low_other,), [tower])
    theirs = input_grad(meta, False, low_other, wimg, wtext)
    theirs, _ = seal(theirs, [proj_own, ff, proj, tower])
    si, st = (jnp.where(short, mine[k], theirs[k]) for k in (0, 1))
    li, lt = (jnp.where(short, theirs[k], mine[k]) for k in (2, 3))
    (si, st, li, lt), _ = seal((si, st, li, lt), [proj, tower])
    seal((), [tower])
    red_ff, red_proj = ff.total, proj.total
    if grouped:
        red_tower = tower.total
        red_img, red_text = red_tower[0:24, 0:768], red_tower[24:48, 0:768]
        red_vectors = [red_tower[0:24, 768 + k] for k in range(11)]
        device = 2 * lax.axis_index(DP) + lax.axis_index(TP)
        red_up_bias = lax.dynamic_slice(red_tower, (0, 779 + device // 8), (24, 4))
        red_vectors.append(red_up_bias.T.reshape(96))
    else:
        mats = jnp.stack([absolute([part_[:, half_, :, 0:768] for part_ in towers], TOWERS[0:3]) for half_ in range(2)])
        mats = mats.reshape(2, 16, 2, 24, 768).transpose(2, 1, 0, 3, 4).reshape(2, 768, 768)
        red_img = lax.psum_scatter(mats[0], (DP, TP), scatter_dimension=0, tiled=True)
        red_text = lax.psum_scatter(mats[1], (DP, TP), scatter_dimension=0, tiled=True)
        sums = [*sums_one[0:5], qkv_sums[:, 0:384].reshape(768), qkv_sums[:, 768:1152].reshape(768),
                *sums_two[0:3], cot_sum[0], jnp.concatenate([grad_up_bias0, grad_up_bias1]).reshape(3072)]
        red_vectors = [lax.psum_scatter(v, (DP, TP), scatter_dimension=0, tiled=True) for v in sums]

    f = lambda v: v.astype(F32)
    vec = [f(v) for v in red_vectors]
    return (
        short_output, long_output, si, st, li, lt,
        f(red_img), vec[0], f(red_text), vec[1], vec[2], vec[3], vec[4],
        red_proj[:, 0:384], vec[5], red_proj[:, 384:768], red_proj[:, 768:1152], vec[6],
        red_proj[:, 1152:1536].T, vec[7], vec[8], vec[9],
        jnp.concatenate([red_ff[:, 0:768], red_ff[:, 1536:2304]], axis=1), vec[11],
        jnp.concatenate([red_ff[:, 768:1536], red_ff[:, 2304:3072]], axis=1).T, vec[10],
    )


def solution(mesh):
    rows = P(DP, None, None)
    vec = P((DP, TP))
    tower = P((DP, TP), None)
    col = P(DP, TP)
    back = P(TP, DP)
    return jax.shard_map(
        on_device,
        mesh=mesh,
        in_specs=(
            rows, rows, P(DP), rows, rows, rows, P(DP), rows,
            tower, vec, tower, vec, vec, vec, vec,
            col, vec, col, col, vec, back, vec, vec, vec, col, vec, back, vec,
        ),
        out_specs=(
            rows, rows, rows, rows, rows, rows,
            tower, vec, tower, vec, vec, vec, vec,
            col, vec, col, col, vec, back, vec, vec, vec, col, vec, back, vec,
        ),
        check_vma=False,
    )
```

```python
from functools import partial

import jax
import jax.numpy as jnp
from jax import lax
from jax.experimental import pallas as pl
from jax.experimental.pallas import tpu as pltpu
from jax.sharding import PartitionSpec as P

DP = "dp"
TP = "tensor"
BOTH = (TP, DP)
EPS = 1e-06
NEG = -1e30
BF = jnp.bfloat16
F32 = jnp.float32
ROWS = 1024
BLK = 256
MIB = 1 << 20


def dot_nn(left, right):
    return lax.dot_general(left, right, (((1,), (0,)), ((), ())), preferred_element_type=F32)


def dot_nt(left, right):
    return lax.dot_general(left, right, (((1,), (1,)), ((), ())), preferred_element_type=F32)


def flip(values):
    return values.astype(F32).T.astype(BF)


def cost(micros):
    return pl.CostEstimate(flops=int(micros * 2e8), bytes_accessed=int(micros * 1e5), transcendentals=0)


def params(limit=56):
    return pltpu.CompilerParams(dimension_semantics=("arbitrary",), vmem_limit_bytes=limit * MIB)


def whole(*shape):
    return pl.BlockSpec(shape, lambda *_: (0,) * len(shape), pipeline_mode=pl.Buffered(1))


def norm_parts(values):
    row_mean = jnp.mean(values, axis=-1, keepdims=True)
    centred = values - row_mean
    row_var = jnp.mean(centred * centred, axis=-1, keepdims=True)
    inverse = lax.rsqrt(row_var + EPS)
    return centred * inverse, inverse


def norm_back(xhat, inverse, scaled):
    first = jnp.mean(scaled, axis=-1, keepdims=True)
    second = jnp.mean(scaled * xhat, axis=-1, keepdims=True)
    return (scaled - first - xhat * second) * inverse


def is_short(meta):
    return meta[0] == 1


def active(meta, step):
    return jnp.logical_or(is_short(meta), step < 3)


CORE, X, LOW, HIGH, Y = 1, 2, 4, 8, 16
HALVES = ((LOW, X, HIGH), (X, LOW, HIGH))
TOWERS = (X, LOW, HIGH, Y)
GATHER_QKV = (Y, X, LOW, HIGH)
GATHER_TOWER = (X, Y, LOW, HIGH)
GATHER_UP = (Y, LOW, HIGH, X)
GATHER_DOWN = (X, LOW, HIGH, Y)


def relatives(meta, order):
    rest = [bit for bit in order if bit != Y]
    for core in range(2):
        for place in range(8):
            offset = core * CORE + sum(bit * (place >> (2 - k) & 1) for k, bit in enumerate(rest))
            yield core, place, jnp.bitwise_xor(meta[6], offset)


def places(meta, order):
    for core in range(2):
        for place in range(16):
            offset = core * CORE + sum(bit * (place >> (3 - k) & 1) for k, bit in enumerate(order))
            other = offset // 16
            yield core, place, jnp.bitwise_xor(meta[6], offset % 16), other, jnp.bitwise_xor(meta[5], other)


def hold_pieces(held, result):
    for group in range(16):
        held[group] = result[group * 48 : (group + 1) * 48].astype(BF)


def halves_shapes(width):
    return [jax.ShapeDtypeStruct((8, 48, width), BF)] * 2


def pack_kernel(q_ref, k_ref, v_ref, img_ref, text_ref, out_ref, small_ref, packed_ref):
    packed_ref[0, :, 0:384] = q_ref[...]
    packed_ref[0, :, 384:768] = k_ref[...]
    packed_ref[0, :, 768:1152] = v_ref[...]
    tower = jnp.concatenate([img_ref[...].astype(F32), text_ref[...].astype(F32)], axis=0)
    packed_ref[0, :, 1152:1920] = tower.astype(BF)
    packed_ref[0, :, 1920:2304] = out_ref[...]
    small = jnp.concatenate([small_ref[...].astype(F32), jnp.zeros((112, 24), F32)], axis=0).T
    packed_ref[0, :, 2304:2432] = jnp.concatenate([small, jnp.zeros((24, 128), F32)], axis=0).astype(BF)


def pack(*args):
    return pl.pallas_call(
        pack_kernel,
        grid=(1,),
        in_specs=[whole(*arg.shape) for arg in args],
        out_specs=whole(1, 48, 2432),
        out_shape=jax.ShapeDtypeStruct((1, 48, 2432), BF),
        compiler_params=params(40),
        name="pack",
        cost_estimate=cost(2),
    )(*args)


def prepare_kernel(x_ref, cot_ref, xt_ref, cott_ref, sum_ref):
    xt_ref[...] = flip(x_ref[...])
    cott_ref[...] = flip(cot_ref[...])

    @pl.when(pl.program_id(0) == 0)
    def _():
        sum_ref[...] = jnp.zeros_like(sum_ref)

    sum_ref[...] += jnp.sum(cot_ref[...].astype(F32), axis=0, keepdims=True)


def prepare(x, cot):
    row = pl.BlockSpec((BLK, 768), lambda i: (i, 0))
    column = pl.BlockSpec((768, BLK), lambda i: (0, i))
    return pl.pallas_call(
        prepare_kernel,
        grid=(4,),
        in_specs=[row, row],
        out_specs=[column, column, whole(1, 768)],
        out_shape=[
            jax.ShapeDtypeStruct((768, ROWS), BF),
            jax.ShapeDtypeStruct((768, ROWS), BF),
            jax.ShapeDtypeStruct((1, 768), F32),
        ],
        compiler_params=params(8),
        name="prepare",
        cost_estimate=cost(0.1),
    )(x, cot)


def embed_kernel(
    meta, x_ref, qkv_00, qkv_01, qkv_10, qkv_11, tower_00, tower_01, tower_10, tower_11,
    stream_ref, n1t_ref, qkv0_ref, qkv1_ref, wimg_ref, wtext_ref, wqkv_ref, wout_ref, sm_ref, bias_ref,
    wimg_f, wtext_f, wout_pieces, columns, up_columns,
):
    step = pl.program_id(0)
    qkv = (qkv_00, qkv_01), (qkv_10, qkv_11)
    towers = (tower_00, tower_01), (tower_10, tower_11)

    @pl.when(step == 0)
    def _():
        for core, place, group, other, _ in places(meta, GATHER_QKV):
            wqkv_ref[other, group] = qkv[core][place // 8][place % 8]
        for core, place, group, other, half in places(meta, GATHER_TOWER):
            tower = towers[core][place // 8].at[place % 8]
            piece = tower[:, 0:768].astype(F32)
            rows = pl.ds(pl.multiple_of(24 * (2 * group + half), 8), 24)
            wimg_f[rows, :] = piece[0:24]
            wtext_f[rows, :] = piece[24:48]
            wout_pieces[other, group] = tower[:, 768:1152]
            device = 2 * group + half
            small = tower[0:32, 1152:1280].astype(F32)[0:24]
            columns[rows, :] = small
            for part in range(4):
                start = pl.multiple_of(96 * device + 24 * part, 8)
                up_columns[pl.ds(start, 24), :] = pltpu.roll(small, 128 - 11 - part, 1)
        wimg_ref[...] = wimg_f[...].astype(BF)
        wtext_ref[...] = wtext_f[...].astype(BF)
        for half in range(2):
            wout_ref[:, 384 * half : 384 * half + 384] = wout_pieces[half].reshape(768, 384)
        sm_ref[...] = columns[...].T[0:16]
        for chunk in range(4):
            bias_ref[chunk] = up_columns[768 * chunk : 768 * chunk + 768, :].T[0:1]

    @pl.when(active(meta, step))
    def _():
        with_image = jnp.logical_or(is_short(meta), step == 0)

        @pl.when(with_image)
        def _():
            first = dot_nn(x_ref[0:208, :], wimg_ref[...]) + sm_ref[0:1, :]
            second = dot_nn(x_ref[192:256, :], wtext_ref[...]) + sm_ref[1:2, :]
            index = lax.broadcasted_iota(jnp.int32, (16, 768), 0)
            stream_ref[0:192, :] = first[0:192]
            stream_ref[192:208, :] = jnp.where(index < 6, first[192:208], second[0:16])
            stream_ref[208:256, :] = second[16:64]
            stream_ref[0:1, :] = sm_ref[2:3, :]

        @pl.when(jnp.logical_not(with_image))
        def _():
            stream_ref[...] = dot_nn(x_ref[...], wtext_ref[...]) + sm_ref[1:2, :]

        xhat, _ = norm_parts(stream_ref[...])
        scaled = xhat * sm_ref[3:4, :] + sm_ref[4:5, :]
        normed = scaled.astype(BF)
        n1t_ref[...] = flip(normed)
        for half, qkv_ref in enumerate((qkv0_ref, qkv1_ref)):
            out = dot_nn(normed, wqkv_ref[half].reshape(768, 1152))
            lanes = pl.ds(pl.multiple_of(384 * jnp.bitwise_xor(meta[5], half), 128), 384)
            qkv_ref[:, 0:384] = (out[:, 0:384] + sm_ref[5:6, lanes]).astype(BF)
            qkv_ref[:, 384:768] = out[:, 384:768].astype(BF)
            qkv_ref[:, 768:1152] = (out[:, 768:1152] + sm_ref[6:7, lanes]).astype(BF)


def embed(meta, x, qkv_all, tower_all):
    row = lambda width: pl.BlockSpec((BLK, width), lambda i, m: (i, 0))
    return pl.pallas_call(
        embed_kernel,
        grid_spec=pltpu.PrefetchScalarGridSpec(
            num_scalar_prefetch=1,
            grid=(4,),
            in_specs=[row(768)] + [whole(8, 48, 1152)] * 4 + [whole(8, 48, 1280)] * 4,
            out_specs=[
                row(768),
                pl.BlockSpec((768, BLK), lambda i, m: (0, i)),
                row(1152),
                row(1152),
                whole(768, 768),
                whole(768, 768),
                whole(2, 16, 48, 1152),
                whole(768, 768),
                whole(16, 768),
                whole(4, 1, 768),
            ],
            scratch_shapes=[
                pltpu.VMEM((768, 768), F32),
                pltpu.VMEM((768, 768), F32),
                pltpu.VMEM((2, 16, 48, 384), BF),
                pltpu.VMEM((768, 128), F32),
                pltpu.VMEM((3072, 128), F32),
            ],
        ),
        out_shape=[
            jax.ShapeDtypeStruct((ROWS, 768), F32),
            jax.ShapeDtypeStruct((768, ROWS), BF),
            jax.ShapeDtypeStruct((ROWS, 1152), BF),
            jax.ShapeDtypeStruct((ROWS, 1152), BF),
            jax.ShapeDtypeStruct((768, 768), BF),
            jax.ShapeDtypeStruct((768, 768), BF),
            jax.ShapeDtypeStruct((2, 16, 48, 1152), BF),
            jax.ShapeDtypeStruct((768, 768), BF),
            jax.ShapeDtypeStruct((16, 768), F32),
            jax.ShapeDtypeStruct((4, 1, 768), F32),
        ],
        compiler_params=params(28),
        name="embed",
        cost_estimate=cost(12),
    )(meta, x, *qkv_all, *tower_all)


def head_lanes(values, head):
    lane = lax.broadcasted_iota(jnp.int32, values.shape, 1)
    keep = lane < 64 if head == 0 else lane >= 64
    return jnp.where(keep, values, jnp.zeros_like(values))


def attn_forward_part(q, k, v, limit):
    out, lse = None, []
    for head in range(2):
        scores = dot_nt(head_lanes(q, head), k)
        index = lax.broadcasted_iota(jnp.int32, scores.shape, 1)
        scores = jnp.where(index < limit, scores, NEG)
        top = jnp.max(scores, axis=1, keepdims=True)
        weight = jnp.exp(scores - top)
        total = jnp.sum(weight, axis=1, keepdims=True)
        add = dot_nn(weight.astype(BF), head_lanes(v, head)) * (1.0 / total)
        out = add if out is None else out + add
        lse.append(jnp.broadcast_to(top + jnp.log(total), (256, 128)).T[0:1])
    return out.astype(BF), jnp.concatenate(lse, axis=0)


def attn_forward_kernel(meta, qkv_ref, out_ref, lse_ref):
    pair = pl.program_id(0)

    def part(kind, start, size):
        lanes = pl.ds(pl.multiple_of(384 * kind + 128 * pair, 128), 128)
        return qkv_ref[start : start + size, lanes]

    @pl.when(is_short(meta))
    def _():
        for member in range(4):
            start = 256 * member
            q = part(0, start, 256) * BF(0.125)
            out, lse = attn_forward_part(
                q, part(1, start, 256), part(2, start, 256), meta[1 + member]
            )
            out_ref[start : start + 256, :] = out
            lse_ref[0, :, start : start + 256] = lse

    @pl.when(jnp.logical_not(is_short(meta)))
    def _():
        k = part(1, 0, 768)
        v = part(2, 0, 768)
        for member in range(3):
            start = 256 * member
            q = part(0, start, 256) * BF(0.125)
            out, lse = attn_forward_part(q, k, v, meta[1])
            out_ref[start : start + 256, :] = out
            lse_ref[0, :, start : start + 256] = lse


def attn_forward(meta, qkv):
    return pl.pallas_call(
        attn_forward_kernel,
        grid_spec=pltpu.PrefetchScalarGridSpec(
            num_scalar_prefetch=1,
            grid=(3,),
            in_specs=[whole(ROWS, 1152)],
            out_specs=[
                pl.BlockSpec((ROWS, 128), lambda j, m: (0, j)),
                pl.BlockSpec((1, 2, ROWS), lambda j, m: (j, 0, 0)),
            ],
        ),
        out_shape=[
            jax.ShapeDtypeStruct((ROWS, 384), BF),
            jax.ShapeDtypeStruct((3, 2, ROWS), F32),
        ],
        compiler_params=params(8),
        name="attn_forward",
        cost_estimate=cost(14),
    )(meta, qkv)


def attn_back_part(q, k, v, grad, lse, limit):
    grad_k, grad_v, grad_q = None, None, None
    for head in range(2):
        q_head = head_lanes(q, head)
        g_head = head_lanes(grad, head)
        scores = dot_nt(k, q_head)
        index = lax.broadcasted_iota(jnp.int32, scores.shape, 0)
        probs = jnp.exp(scores - lse[head : head + 1])
        probs = jnp.where(index < limit, probs, 0.0)
        grad_probs = dot_nt(v, g_head)
        row_dot = jnp.sum(probs * grad_probs, axis=0, keepdims=True)
        grad_scores = (probs * (grad_probs - row_dot)).astype(BF)
        add_v = dot_nn(probs.astype(BF), g_head)
        add_k = dot_nn(grad_scores, q_head)
        grad_v = add_v if grad_v is None else grad_v + add_v
        grad_k = add_k if grad_k is None else grad_k + add_k
        add_q = lax.dot_general(
            grad_scores, head_lanes(k, head), (((0,), (0,)), ((), ())), preferred_element_type=F32
        )
        grad_q = add_q if grad_q is None else grad_q + add_q
    return (grad_q * 0.125).astype(BF), grad_k, grad_v


def attn_back_kernel(meta, qkv_ref, grad_ref, lse_ref, out_ref, acc_k, acc_v):
    pair = pl.program_id(0)

    def lanes(kind):
        return pl.ds(pl.multiple_of(384 * kind + 128 * pair, 128), 128)

    def part(kind, start, size):
        return qkv_ref[start : start + size, lanes(kind)]

    @pl.when(is_short(meta))
    def _():
        for member in range(4):
            rows = slice(256 * member, 256 * member + 256)
            start = 256 * member
            q = part(0, start, 256) * BF(0.125)
            k = part(1, start, 256)
            grad_q, grad_k, grad_v = attn_back_part(
                q, k, part(2, start, 256), grad_ref[rows, :], lse_ref[0, :, rows], meta[1 + member]
            )
            out_ref[rows, lanes(0)] = grad_q
            out_ref[rows, lanes(1)] = grad_k.astype(BF)
            out_ref[rows, lanes(2)] = grad_v.astype(BF)

    @pl.when(jnp.logical_not(is_short(meta)))
    def _():
        k = part(1, 0, 768)
        v = part(2, 0, 768)
        for member in range(3):
            rows = slice(256 * member, 256 * member + 256)
            start = 256 * member
            q = part(0, start, 256) * BF(0.125)
            grad_q, grad_k, grad_v = attn_back_part(
                q, k, v, grad_ref[rows, :], lse_ref[0, :, rows], meta[1]
            )
            out_ref[rows, lanes(0)] = grad_q
            if member == 0:
                acc_k[...] = grad_k
                acc_v[...] = grad_v
            else:
                acc_k[...] += grad_k
                acc_v[...] += grad_v
        out_ref[0:768, lanes(1)] = acc_k[...].astype(BF)
        out_ref[0:768, lanes(2)] = acc_v[...].astype(BF)


def attn_back(meta, qkv, grad, lse):
    return pl.pallas_call(
        attn_back_kernel,
        grid_spec=pltpu.PrefetchScalarGridSpec(
            num_scalar_prefetch=1,
            grid=(3,),
            in_specs=[
                whole(ROWS, 1152),
                pl.BlockSpec((ROWS, 128), lambda j, m: (0, j)),
                pl.BlockSpec((1, 2, ROWS), lambda j, m: (j, 0, 0)),
            ],
            out_specs=whole(ROWS, 1152),
            scratch_shapes=[pltpu.VMEM((768, 128), F32), pltpu.VMEM((768, 128), F32)],
        ),
        out_shape=jax.ShapeDtypeStruct((ROWS, 1152), BF),
        compiler_params=params(10),
        name="attn_back",
        cost_estimate=cost(0.1),
    )(meta, qkv, grad, lse)


def mid_kernel(meta, att0_ref, att1_ref, stream_ref, wout_ref, sm_ref, mid_ref, n2_ref, n2t_ref):
    @pl.when(active(meta, pl.program_id(0)))
    def _():
        attended = jnp.concatenate([att0_ref[...], att1_ref[...]], axis=1)
        mid = stream_ref[...] + dot_nt(attended, wout_ref[...]) + sm_ref[7:8, :]
        mid_ref[...] = mid
        xhat, _ = norm_parts(mid)
        normed = (xhat * sm_ref[8:9, :] + sm_ref[9:10, :]).astype(BF)
        n2_ref[...] = normed
        n2t_ref[...] = flip(normed)


def mid_stage(meta, attended, stream, wout, smalls):
    row = lambda width: pl.BlockSpec((BLK, width), lambda i, m: (i, 0))
    return pl.pallas_call(
        mid_kernel,
        grid_spec=pltpu.PrefetchScalarGridSpec(
            num_scalar_prefetch=1,
            grid=(4,),
            in_specs=[
                row(384),
                row(384),
                row(768),
                whole(768, 768),
                whole(16, 768),
            ],
            out_specs=[row(768), row(768), pl.BlockSpec((768, BLK), lambda i, m: (0, i))],
        ),
        out_shape=[
            jax.ShapeDtypeStruct((ROWS, 768), F32),
            jax.ShapeDtypeStruct((ROWS, 768), BF),
            jax.ShapeDtypeStruct((768, ROWS), BF),
        ],
        compiler_params=params(8),
        name="mid_stage",
        cost_estimate=cost(7),
    )(meta, *attended, stream, wout, smalls)


INV_ROOT2 = 0.7071067811865476
INV_ROOT2PI = 0.3989422804014327


def mlp_kernel(
    other,
    meta, n2_ref, n2_t, cot_ref, cot_t, up_near, up_far, down_00, down_01, down_10, down_11, bias_ref,
    out_ref, gn_ref, keep_ref, send_ref, gbias_ref,
    wup_pieces, wdown_pieces, hid, gpre, held, out_sum, gn_sum,
):
    step = pl.program_id(0)
    down = (down_00, down_01), (down_10, down_11)
    for core, place, group, half, _ in places(meta, GATHER_UP):
        if half == other:
            wup_pieces[group] = (up_near, up_far)[core][place % 8]
    for core, place, group, half, _ in places(meta, GATHER_DOWN):
        if half == other:
            wdown_pieces[group] = down[core][place // 8][place % 8 // 2, 0]
    bias = bias_ref[0]

    gbias_ref[...] = jnp.zeros_like(gbias_ref)

    @pl.loop(0, jnp.where(is_short(meta), 4, 3))
    def _(block):
        wup = wup_pieces[...].reshape(768, 768)
        wdown = wdown_pieces[...].reshape(768, 768)
        rows = pl.ds(pl.multiple_of(256 * block, 256), 256)
        pre = dot_nn(n2_ref[rows, :], wup) + bias
        cdf = 0.5 + 0.5 * lax.erf(pre * INV_ROOT2)
        hidden = (pre * cdf).astype(BF)
        hid[rows, :] = hidden
        slope = cdf + pre * (jnp.exp(pre * pre * -0.5) * INV_ROOT2PI)
        grad_pre = (dot_nn(cot_ref[rows, :], wdown) * slope).astype(BF)
        gpre[rows, :] = grad_pre
        gbias_ref[0] += jnp.sum(grad_pre.astype(F32), axis=0, keepdims=True)
        out_add = dot_nt(hidden, wdown)
        gn_add = dot_nt(grad_pre, wup)

        @pl.when(step == 0)
        def _():
            out_sum[rows, :] = out_add
            gn_sum[rows, :] = gn_add

        @pl.when(step > 0)
        def _():
            out_ref[rows, :] = (out_sum[rows, :] + out_add).astype(BF)
            gn_ref[rows, :] = (gn_sum[rows, :] + gn_add).astype(BF)

    for size, chosen in ((1024, is_short(meta)), (768, jnp.logical_not(is_short(meta)))):

        @pl.when(chosen)
        def _(size=size):
            rows = slice(0, size)
            for kind, left, right in ((0, n2_t, gpre), (1, cot_t, hid)):
                hold_pieces(held, dot_nn(left[:, rows], right[rows, :]))
                lanes = slice(768 * kind, 768 * kind + 768)
                for core, place, group in relatives(meta, HALVES[other]):
                    (keep_ref, send_ref)[core][place, :, lanes] = held[group]


def mlp_half(meta, other, n2, n2_t, cot, cot_t, up_all, down_all, up_bias):
    rows, turned = whole(ROWS, 768), whole(768, ROWS)
    bias = pl.BlockSpec((1, 1, 768), lambda c, m: (2 * jnp.bitwise_xor(other, m[5]) + c, 0, 0))
    return pl.pallas_call(
        partial(mlp_kernel, other),
        grid_spec=pltpu.PrefetchScalarGridSpec(
            num_scalar_prefetch=1,
            grid=(2,),
            in_specs=[
                rows,
                turned,
                rows,
                turned,
                *[pl.BlockSpec((8, 48, 768), lambda c, m: (0, 0, c))] * 2,
                *[pl.BlockSpec((4, 1, 48, 768), lambda c, m: (0, other, 0, c))] * 4,
                bias,
            ],
            out_specs=[
                rows,
                rows,
                pl.BlockSpec((8, 48, 1536), lambda c, m: (0, 0, c)),
                pl.BlockSpec((8, 48, 1536), lambda c, m: (0, 0, c)),
                pl.BlockSpec((1, 1, 768), lambda c, m: (c, 0, 0)),
            ],
            scratch_shapes=[
                pltpu.VMEM((16, 48, 768), BF),
                pltpu.VMEM((16, 48, 768), BF),
                pltpu.VMEM((ROWS, 768), BF),
                pltpu.VMEM((ROWS, 768), BF),
                pltpu.VMEM((16, 48, 768), BF),
                pltpu.VMEM((ROWS, 768), F32),
                pltpu.VMEM((ROWS, 768), F32),
            ],
        ),
        out_shape=[
            jax.ShapeDtypeStruct((ROWS, 768), BF),
            jax.ShapeDtypeStruct((ROWS, 768), BF),
            *halves_shapes(3072),
            jax.ShapeDtypeStruct((2, 1, 768), F32),
        ],
        compiler_params=params(32),
        name="mlp_half",
        cost_estimate=cost(0.1),
    )(
        meta, n2, n2_t, cot, cot_t,
        up_all[other], up_all[2 + other],
        *(part.reshape(4, 2, 48, 1536) for part in down_all),
        up_bias,
    )


def back_mid_kernel(
    meta, mlp0_ref, gn0_ref, mlp1_ref, gn1_ref, mid_ref, cot_ref, att0_ref, att1_ref, wout_ref, sm_ref,
    out_ref, gmid_ref, gatt0_ref, gatt1_ref, gout0_keep, gout0_send, gout1_keep, gout1_send, sums_ref,
    low_t, held,
):
    step = pl.program_id(0)

    @pl.when(step == 0)
    def _():
        sums_ref[...] = jnp.zeros_like(sums_ref)

    @pl.when(jnp.logical_and(active(meta, step), step < 4))
    def _():
        mid = mid_ref[...]
        out_ref[...] = (mid + (mlp0_ref[...].astype(F32) + mlp1_ref[...].astype(F32)) + sm_ref[10:11, :]).astype(BF)
        xhat, inverse = norm_parts(mid)
        grad = gn0_ref[...].astype(F32) + gn1_ref[...].astype(F32)
        cot = cot_ref[...].astype(F32)
        grad_mid = cot + norm_back(xhat, inverse, grad * sm_ref[8:9, :])
        gmid_ref[...] = grad_mid
        low = grad_mid.astype(BF)
        grad_att = dot_nn(low, wout_ref[...]).astype(BF)
        gatt0_ref[...] = grad_att[:, 0:384]
        gatt1_ref[...] = grad_att[:, 384:768]
        low_t[step] = flip(low)
        sums_ref[0:1, :] += jnp.sum(grad_mid, axis=0, keepdims=True)
        sums_ref[1:2, :] += jnp.sum(grad * xhat, axis=0, keepdims=True)
        sums_ref[2:3, :] += jnp.sum(grad, axis=0, keepdims=True)

    for half, att_ref in enumerate((att0_ref, att1_ref)):
        for count, chosen in ((4, is_short(meta)), (3, jnp.logical_not(is_short(meta)))):

            @pl.when(jnp.logical_and(chosen, step == 4 + half))
            def _(count=count, att_ref=att_ref, half=half):
                total = None
                for block in range(count):
                    add = dot_nn(low_t[block], att_ref[256 * block : 256 * block + 256, :])
                    total = add if total is None else total + add
                hold_pieces(held, total)
                gouts = ((gout0_keep, gout0_send), (gout1_keep, gout1_send))[half]
                for core, place, group in relatives(meta, HALVES[half]):
                    gouts[core][place] = held[group]


def back_mid(meta, mlp_sums, mid, cot, attended, wout, smalls):
    row = pl.BlockSpec((BLK, 768), lambda i, m: (jnp.minimum(i, 3), 0))
    thin = pl.BlockSpec((BLK, 384), lambda i, m: (jnp.minimum(i, 3), 0))
    return pl.pallas_call(
        back_mid_kernel,
        grid_spec=pltpu.PrefetchScalarGridSpec(
            num_scalar_prefetch=1,
            grid=(6,),
            in_specs=[
                row,
                row,
                row,
                row,
                row,
                row,
                whole(ROWS, 384),
                whole(ROWS, 384),
                whole(768, 768),
                whole(16, 768),
            ],
            out_specs=[
                row,
                row,
                thin,
                thin,
                *[whole(8, 48, 384)] * 4,
                whole(8, 768),
            ],
            scratch_shapes=[
                pltpu.VMEM((4, 768, 256), BF),
                pltpu.VMEM((16, 48, 384), BF),
            ],
        ),
        out_shape=[
            jax.ShapeDtypeStruct((ROWS, 768), BF),
            jax.ShapeDtypeStruct((ROWS, 768), F32),
            jax.ShapeDtypeStruct((ROWS, 384), BF),
            jax.ShapeDtypeStruct((ROWS, 384), BF),
            *halves_shapes(384),
            *halves_shapes(384),
            jax.ShapeDtypeStruct((8, 768), F32),
        ],
        compiler_params=params(12),
        name="back_mid",
        cost_estimate=cost(0.1),
    )(meta, *mlp_sums, mid, cot, *attended, wout, smalls)


def back_in_kernel(
    meta, dqkv0_ref, dqkv1_ref, stream_ref, gmid_ref, wqkv_ref, sm_ref, low_ref, sums_ref, qsum_ref
):
    step = pl.program_id(0)

    @pl.when(step == 0)
    def _():
        sums_ref[...] = jnp.zeros_like(sums_ref)
        qsum_ref[...] = jnp.zeros_like(qsum_ref)

    @pl.when(active(meta, step))
    def _():
        grad = None
        for half, dqkv_ref in enumerate((dqkv0_ref, dqkv1_ref)):
            dqkv = dqkv_ref[...]
            add = dot_nt(dqkv, wqkv_ref[half].reshape(768, 1152))
            grad = add if grad is None else grad + add
            qsum_ref[half : half + 1, :] += jnp.sum(dqkv.astype(F32), axis=0, keepdims=True)
        xhat, inverse = norm_parts(stream_ref[...])
        grad_in = gmid_ref[...] + norm_back(xhat, inverse, grad * sm_ref[3:4, :])
        low_ref[...] = grad_in.astype(BF)
        with_image = jnp.logical_or(is_short(meta), step == 0)
        limit = jnp.where(with_image, 198, 0)
        index = lax.broadcasted_iota(jnp.int32, (BLK, 768), 0)
        before = jnp.sum(jnp.where(index < limit, grad_in, 0.0), axis=0, keepdims=True)
        cls = jnp.where(with_image, grad_in[0:1], 0.0)
        everything = jnp.sum(grad_in, axis=0, keepdims=True)
        sums_ref[0:1, :] += before - cls
        sums_ref[1:2, :] += everything - before
        sums_ref[2:3, :] += cls
        sums_ref[3:4, :] += jnp.sum(grad * xhat, axis=0, keepdims=True)
        sums_ref[4:5, :] += jnp.sum(grad, axis=0, keepdims=True)


def back_in(meta, dqkv, stream, grad_mid, wqkv, smalls):
    row = lambda width: pl.BlockSpec((BLK, width), lambda i, m: (i, 0))
    return pl.pallas_call(
        back_in_kernel,
        grid_spec=pltpu.PrefetchScalarGridSpec(
            num_scalar_prefetch=1,
            grid=(4,),
            in_specs=[row(1152), row(1152), row(768), row(768), whole(2, 16, 48, 1152), whole(16, 768)],
            out_specs=[row(768), whole(8, 768), whole(2, 1152)],
        ),
        out_shape=[
            jax.ShapeDtypeStruct((ROWS, 768), BF),
            jax.ShapeDtypeStruct((8, 768), F32),
            jax.ShapeDtypeStruct((2, 1152), F32),
        ],
        compiler_params=params(12),
        name="back_in",
        cost_estimate=cost(0.1),
    )(meta, *dqkv, stream, grad_mid, wqkv, smalls)


def proj_grad_kernel(other, meta, n1t_ref, dqkv_ref, gout_keep, gout_send, keep_ref, send_ref, held):
    step = pl.program_id(0)
    for size, chosen in ((1024, is_short(meta)), (768, jnp.logical_not(is_short(meta)))):

        @pl.when(jnp.logical_and(chosen, step < 3))
        def _(size=size):
            hold_pieces(held, dot_nn(n1t_ref[:, 0:size], dqkv_ref[0:size, :]))
            for core, place, group in relatives(meta, HALVES[other]):
                (keep_ref, send_ref)[core][place] = held[group]

    @pl.when(step == 3)
    def _():
        keep_ref[...] = gout_keep[...]
        send_ref[...] = gout_send[...]


def proj_grad(meta, other, n1_t, dqkv, grad_out):
    columns = pl.BlockSpec((8, 48, 384), lambda c, m: (0, 0, c))
    return pl.pallas_call(
        partial(proj_grad_kernel, other),
        grid_spec=pltpu.PrefetchScalarGridSpec(
            num_scalar_prefetch=1,
            grid=(4,),
            in_specs=[
                whole(768, ROWS),
                pl.BlockSpec((ROWS, 384), lambda c, m: (0, jnp.minimum(c, 2))),
                whole(8, 48, 384),
                whole(8, 48, 384),
            ],
            out_specs=[columns, columns],
            scratch_shapes=[pltpu.VMEM((16, 48, 384), BF)],
        ),
        out_shape=halves_shapes(1536),
        compiler_params=params(10),
        name="proj_grad",
        cost_estimate=cost(0.1),
    )(meta, n1_t, dqkv, *grad_out)


def tower_grad_kernel(
    meta, x_t, low_ref, one_ref, two_ref, qkv_ref, down_ref, up0_ref, up1_ref,
    keep_ref, send_ref, gimg, gtext, wimg, wtext, vectors, columns,
):
    vectors[...] = jnp.zeros_like(vectors)
    vectors[0:5, :] = one_ref[0:5, :]
    for half in range(2):
        lanes = pl.ds(pl.multiple_of(384 * jnp.bitwise_xor(meta[5], half), 128), 384)
        vectors[5:6, lanes] = qkv_ref[half : half + 1, 0:384]
        vectors[6:7, lanes] = qkv_ref[half : half + 1, 768:1152]
    vectors[7:10, :] = two_ref[0:3, :]
    vectors[10:11, :] = down_ref[...]
    for half, up_ref in enumerate((up0_ref, up1_ref)):
        for chunk in range(2):
            vectors[pl.ds(11 + 2 * jnp.bitwise_xor(meta[5], half) + chunk, 1), :] = up_ref[chunk]
    columns[...] = vectors[...].T
    for block in range(4):
        rows = slice(256 * block, 256 * block + 256)
        with_image = jnp.logical_or(is_short(meta), block == 0)
        limit = jnp.where(with_image, 198, 0)
        index = lax.broadcasted_iota(jnp.int32, (BLK, 768), 0)
        low = low_ref[rows, :].astype(F32)
        gimg[rows, :] = jnp.where(index < limit, low, 0.0).astype(BF)
        gtext[rows, :] = jnp.where(index < limit, 0.0, low).astype(BF)

    for size, chosen in ((1024, is_short(meta)), (768, jnp.logical_not(is_short(meta)))):

        @pl.when(chosen)
        def _(size=size):
            wtext[...] = dot_nn(x_t[:, 0:size], gtext[0:size, :])
            image_size = size if size == 1024 else 256
            wimg[...] = dot_nn(x_t[:, 0:image_size], gimg[0:image_size, :])

    lane = lax.broadcasted_iota(jnp.int32, (24, 128), 1)
    for core, place, group in relatives(meta, TOWERS):
        ref = (keep_ref, send_ref)[core]
        for half in range(2):
            device = 2 * group + jnp.bitwise_xor(meta[5], half)
            rows = pl.ds(pl.multiple_of(24 * device, 8), 24)
            piece = jnp.concatenate([wimg[rows, :], wtext[rows, :]], axis=0).astype(BF)
            ref[place, half, :, 0:768] = piece
            small = jnp.where(lane < 11, columns[rows, :], 0.0)
            for part in range(4):
                start = 96 * jnp.bitwise_and(device, 7) + 24 * part
                some = columns[pl.ds(pl.multiple_of(start, 8), 24), :]
                some = jnp.where(lane == 11 + lax.shift_right_logical(device, 3), some, 0.0)
                small += some if part == 0 else pltpu.roll(some, part, 1)
            ref[place, half, :, 768:896] = jnp.concatenate([small, jnp.zeros_like(small)], axis=0).astype(BF)


def tower_grad(meta, x_t, low, *sums):
    return pl.pallas_call(
        tower_grad_kernel,
        grid_spec=pltpu.PrefetchScalarGridSpec(
            num_scalar_prefetch=1,
            grid=(1,),
            in_specs=[
                whole(768, ROWS),
                whole(ROWS, 768),
                whole(8, 768),
                whole(8, 768),
                whole(2, 1152),
                whole(1, 768),
                whole(2, 1, 768),
                whole(2, 1, 768),
            ],
            out_specs=[whole(8, 2, 48, 896)] * 2,
            scratch_shapes=[
                pltpu.VMEM((ROWS, 768), BF),
                pltpu.VMEM((ROWS, 768), BF),
                pltpu.VMEM((768, 768), F32),
                pltpu.VMEM((768, 768), F32),
                pltpu.VMEM((128, 768), F32),
                pltpu.VMEM((768, 128), F32),
            ],
        ),
        out_shape=[jax.ShapeDtypeStruct((8, 2, 48, 896), BF)] * 2,
        compiler_params=params(13),
        name="tower_grad",
        cost_estimate=cost(0.1),
    )(meta, x_t, low, *sums)


def input_grad_kernel(own, meta, rows_ref, wimg_ref, wtext_ref, si_ref, st_ref, li_ref, lt_ref, held):
    short = is_short(meta) if own else jnp.logical_not(is_short(meta))

    @pl.when(short)
    def _():
        for pair in range(4):
            start = 256 * pair
            held[0:208, :] = dot_nt(rows_ref[start : start + 208, :], wimg_ref[...])
            si_ref[:, pair, :] = held[1:198, :]
            held[0:64, :] = dot_nt(rows_ref[start + 192 : start + 256, :], wtext_ref[...])
            st_ref[:, pair, :] = held[6:64, :]

    @pl.when(jnp.logical_not(short))
    def _():
        held[0:208, :] = dot_nt(rows_ref[0:208, :], wimg_ref[...])
        li_ref[:, 0, :] = held[1:198, :]
        held[0:576, :] = dot_nt(rows_ref[192:768, :], wtext_ref[...])
        lt_ref[...] = held[6:518, :]


def input_grad(meta, own, rows, wimg, wtext):
    shapes = [(197, 4, 768), (58, 4, 768), (197, 1, 768), (512, 768)]
    return pl.pallas_call(
        partial(input_grad_kernel, own),
        grid_spec=pltpu.PrefetchScalarGridSpec(
            num_scalar_prefetch=1,
            grid=(1,),
            in_specs=[whole(ROWS, 768), whole(768, 768), whole(768, 768)],
            out_specs=[whole(*shape) for shape in shapes],
            scratch_shapes=[pltpu.VMEM((576, 768), F32)],
        ),
        out_shape=[jax.ShapeDtypeStruct(shape, F32) for shape in shapes],
        compiler_params=params(14),
        name="input_grad",
        cost_estimate=cost(0.1),
    )(meta, rows, wimg, wtext)


def swap(values, bits):
    if bits == Y:
        return lax.ppermute(values, TP, [(0, 1), (1, 0)])
    if bits < Y:
        return lax.ppermute(values, DP, [(i, i ^ bits) for i in range(16)])
    step = 2 * (bits - Y) + 1
    return lax.ppermute(values, (DP, TP), [(i, i ^ step) for i in range(32)])


def after(values, *others):
    return lax.optimization_barrier((values, *others))[0]


def plus(left, right):
    return (left.astype(F32) + right.astype(F32)).astype(BF)


def absolute(arrays, order):
    width = arrays[0].shape[-1]
    both = jnp.stack(arrays).reshape(2, *(2 for _ in order), 48, width)
    at = {bit: 1 + k for k, bit in enumerate(order)}
    first = [at[Y]] if Y in at else []
    both = both.transpose(*first, at[HIGH], at[LOW], at[X], 0, len(order) + 1, len(order) + 2)
    return both.reshape(-1, width)


class Scatter:
    def __init__(self, pieces, order):
        self.order = (CORE, *order)
        self.arrived = None
        if lax.axis_size(DP) != 16:
            rows = absolute(pieces, order)
            self.total = lax.psum_scatter(rows, BOTH, scatter_dimension=0, tiled=True).astype(F32)
            self.order = ()
            return
        shape = (2, 2, 2, 2, 48, pieces[0].shape[-1])
        self.keep, self.sent = pieces[0].reshape(shape), pieces[1].reshape(shape)

    def send(self):
        if self.order:
            self.arrived = swap(self.sent, self.order[0])

    def add(self):
        if self.order:
            if len(self.order) == 1:
                self.total = self.keep.astype(F32) + self.arrived.astype(F32)
            else:
                self.keep, self.sent = plus(self.keep[0], self.arrived[0]), plus(self.keep[1], self.arrived[1])
            self.arrived = None
            self.order = self.order[1:]


class Half:
    def __init__(self, pieces, other):
        self.other = other
        self.order = (CORE, *HALVES[other][0:2])
        self.arrived = None
        self.pieces = pieces
        if lax.axis_size(DP) != 16:
            self.order = ()
            return
        shape = (2, 2, 2, 48, pieces[0].shape[-1])
        self.keep, self.sent = pieces[0].reshape(shape), pieces[1].reshape(shape)

    def send(self):
        if self.order:
            self.arrived = swap(self.sent, self.order[0])

    def add(self):
        if self.order:
            self.order = self.order[1:]
            if self.order:
                self.keep, self.sent = plus(self.keep[0], self.arrived[0]), plus(self.keep[1], self.arrived[1])
            else:
                self.keep = plus(self.keep, self.arrived)
            self.arrived = None


class Cross:
    def __init__(self, own, other):
        self.own, self.other = own, other
        self.arrived = None
        self.order = (Y, HIGH)
        if lax.axis_size(DP) != 16:
            rows = jnp.concatenate([absolute(half.pieces, HALVES[half.other]) for half in (own, other)])
            self.total = lax.psum_scatter(rows, BOTH, scatter_dimension=0, tiled=True).astype(F32)
            self.order = ()

    def send(self):
        if self.order and self.order[0] == Y and not self.other.order:
            self.arrived = swap(self.other.keep, Y)
        elif self.order and self.order[0] == HIGH and not self.own.order:
            self.sent = plus(self.own.keep[1], self.crossed[1])
            self.arrived = swap(self.sent, HIGH)

    def add(self):
        if self.order and self.order[0] == Y:
            self.crossed = self.arrived
        elif self.order:
            keep = self.own.keep[0].astype(F32) + self.crossed[0].astype(F32)
            self.total = keep + self.arrived.astype(F32)
        self.arrived = None
        self.order = self.order[1:]


class Gather:
    def __init__(self, joined, widths, phases, orders, whole=None):
        self.joined, self.widths, self.phases = joined, widths, phases
        self.parts = None if joined is None else self.split(joined)
        self.arrived = None
        if lax.axis_size(DP) != 16:
            if whole is None:
                whole = lax.all_gather(joined[0], BOTH, axis=0, tiled=True)
            rows = whole.reshape(2, 2, 2, 2, 2, 48, sum(widths))
            at = {Y: 0, HIGH: 1, LOW: 2, X: 3}
            self.rows = tuple(
                tuple(self.split(rows.transpose(4, *(at[bit] for bit in order), 5, 6).reshape(4, 8, 48, -1))[kind])
                for kind, order in enumerate(orders)
            )
            self.phases = ()

    def split(self, values):
        return values[..., : self.widths[0]], values[..., self.widths[0] :]

    def send(self):
        if not self.phases:
            return
        if self.phases[0] in (HIGH, LOW):
            if self.joined is None:
                self.joined = jnp.concatenate(self.parts, axis=-1)
            self.arrived = swap(self.joined, self.phases[0])
            return
        first, second = self.parts
        if self.phases[0] == X:
            self.arrived = swap(first, X), swap(second, Y)
        elif self.phases[0] == Y:
            self.arrived = swap(first, Y), swap(second, X)
        else:
            self.arrived = tuple(tuple(swap(part, CORE) for part in rows) for rows in self.rows)

    def add(self):
        joined = None
        if self.phases[0] == HIGH:
            joined = jnp.concatenate([self.joined, self.arrived], axis=0)
        elif self.phases[0] == LOW:
            pieces = self.split(self.joined), self.split(self.arrived)
            self.parts = tuple(jnp.concatenate([piece[kind] for piece in pieces], axis=0) for kind in range(2))
        elif self.phases[0] == X:
            self.parts = tuple(jnp.concatenate(pair, axis=0) for pair in zip(self.parts, self.arrived))
        elif self.phases[0] == Y:
            self.rows = tuple(zip(self.parts, self.arrived))
        else:
            self.rows = tuple(near + far for near, far in zip(self.rows, self.arrived))
        self.joined, self.arrived = joined, None
        self.phases = self.phases[1:]


def seal(values, movers, swaps=()):
    flying = [mover for mover in movers if mover.arrived is not None]
    values, arrived, swaps = lax.optimization_barrier(
        (tuple(values), tuple(mover.arrived for mover in flying), tuple(swaps))
    )
    for mover, data in zip(flying, arrived):
        mover.arrived = data
        mover.add()
    for mover in movers:
        mover.send()
    return values, swaps


def on_device(
    short_images, short_texts, short_lengths, short_cotangent,
    long_images, long_texts, long_lengths, long_cotangent,
    img_weight, img_bias, text_weight, text_bias, cls_token, attn_gain, attn_shift,
    query_weight, query_bias, key_weight, value_weight, value_bias, out_weight, out_bias,
    mlp_gain, mlp_shift, up_weight, up_bias, down_weight, down_bias,
):
    half = lax.axis_index(TP)
    short = half == 1
    part = img_weight.shape[0]
    devices = 768 // part
    grouped = lax.axis_size(DP) == 16

    vectors = [img_bias, text_bias, cls_token, attn_gain, attn_shift, query_bias, value_bias, out_bias,
               mlp_gain, mlp_shift, down_bias]
    if grouped:
        small = jnp.concatenate([jnp.stack(vectors), up_bias.reshape(4, 24), jnp.zeros((1, 24), BF)])
        shard = pack(query_weight, key_weight, value_weight, img_weight, text_weight, out_weight.T, small)
        towers = None
    else:
        every = lambda v: lax.all_gather(v, (DP, TP), axis=0, tiled=True)
        towers = every(jnp.concatenate([img_weight, text_weight], axis=1))
        towers = towers.reshape(16, 2, 24, 2, 768).transpose(1, 0, 3, 2, 4).reshape(2, 768, 768)
        columns = jnp.stack([every(v) for v in vectors]).reshape(11, 32, 24).transpose(1, 2, 0)
        columns = jnp.concatenate([columns, every(up_bias).reshape(32, 4, 24).transpose(0, 2, 1)], axis=2)
        columns = jnp.pad(columns, ((0, 0), (0, 24), (0, 113)))
        columns = columns.reshape(16, 2, 48, 128).transpose(1, 0, 2, 3).reshape(2, 768, 128)
        outs = lax.all_gather(out_weight.T, BOTH, axis=0, tiled=True).reshape(2, 768, 384)
        towers = jnp.concatenate([towers, outs, columns], axis=2)
        qkv = jnp.concatenate([query_weight, key_weight, value_weight], axis=1)
        towers = jnp.concatenate([lax.all_gather(qkv, BOTH, axis=0, tiled=True).reshape(2, 768, 1152), towers], axis=2)
        shard = None
    joined = None if grouped else jnp.concatenate([up_weight, down_weight.T], axis=1)[None]
    first_gather = Gather(shard, (1152, 1280), (HIGH, LOW, X, Y, CORE), (GATHER_QKV, GATHER_TOWER), towers)
    wide_gather = Gather(joined, (1536, 1536), (X, HIGH, LOW, Y, CORE), (GATHER_UP, GATHER_DOWN))
    wide_gather.parts = up_weight[None], down_weight.T[None]
    near, wide = [first_gather], [wide_gather]
    first_gather.send()
    wide_gather.send()
    seal((), near + wide)
    seal((), near)
    seal((), near + wide)

    zero = jnp.zeros((4, 1, 768), BF)
    short_rows = jnp.concatenate([zero, short_images, short_texts], axis=1).reshape(ROWS, 768)
    long_rows = jnp.concatenate([zero[0, 0:1], long_images[0], long_texts[0], jnp.zeros((ROWS - 710, 768), BF)], axis=0)
    x = jnp.where(short, short_rows, long_rows)
    cot = jnp.where(
        short,
        short_cotangent.reshape(ROWS, 768),
        jnp.concatenate([long_cotangent[0], jnp.zeros((ROWS - 710, 768), BF)], axis=0),
    )
    place = lax.axis_index(DP) if grouped else jnp.int32(0)
    half_place = half.astype(jnp.int32) if grouped else jnp.int32(0)
    limits = 198 + jnp.where(short, short_lengths, jnp.broadcast_to(long_lengths, (4,)))
    meta = jnp.concatenate(
        [
            half.astype(jnp.int32)[None],
            limits.astype(jnp.int32),
            half_place[None],
            place.astype(jnp.int32)[None],
            jnp.zeros((1,), jnp.int32),
        ]
    )

    x_t, cot_t, cot_sum = prepare(x, cot)
    (x, cot, x_t, cot_t, meta), _ = seal((x, cot, x_t, cot_t, meta), near)
    seal((), near)
    (x,), _ = seal((x,), near + wide)
    stream, n1_t, qkv0, qkv1, wimg, wtext, wqkv, wout, smalls, up_bias_all = embed(
        meta, x, *first_gather.rows
    )
    att1, lse1 = attn_forward(meta, qkv1)
    (att1, qkv0), _ = seal((att1, qkv0), wide)
    att0, lse0 = attn_forward(meta, qkv0)
    mid, n2, n2_t = mid_stage(meta, (att0, att1), stream, wout, smalls)
    (n2,), _ = seal((n2,), wide)
    weights = (*wide_gather.rows, up_bias_all)
    mlp1, gn1, *rest = mlp_half(meta, 1, n2, n2_t, cot, cot_t, *weights)
    ff_other, grad_up_bias1 = Half(rest[0:2], 1), rest[2]
    ff_other.send()
    mlp0, gn0, *rest = mlp_half(meta, 0, after(n2, mlp1), n2_t, cot, cot_t, *weights)
    (mlp0, *rest), _ = seal((mlp0, *rest), [ff_other])
    ff_own, grad_up_bias0 = Half(rest[0:2], 0), rest[2]
    ff_own.send()
    ff = Cross(ff_own, ff_other)
    out, grad_mid, gatt0, gatt1, *rest = back_mid(
        meta, (mlp0, gn0, mlp1, gn1), mid, cot, (att0, att1), wout, smalls
    )
    gout0, gout1, sums_two = rest[0:2], rest[2:4], rest[4]
    (out, gatt0, gatt1), _ = seal((out, gatt0, gatt1), [ff_own])
    out_other = swap(out, Y)
    dqkv1 = attn_back(meta, qkv1, gatt1, lse1)
    (*rest, gatt0), _ = seal((*proj_grad(meta, 1, n1_t, dqkv1, gout1), gatt0), [ff_other])
    proj_other = Half(rest, 1)
    proj_other.send()
    dqkv0 = attn_back(meta, qkv0, gatt0, lse0)
    (dqkv0,), _ = seal((dqkv0,), [ff_own])
    rest = proj_grad(meta, 0, n1_t, dqkv0, gout0)
    (dqkv0, *rest), (out_other,) = seal((dqkv0, *rest), [ff_other], (out_other,))
    proj_own = Half(rest, 0)
    proj_own.send()
    ff = Cross(ff_own, ff_other)
    ff.send()
    low, sums_one, qkv_sums = back_in(meta, (dqkv0, dqkv1), stream, grad_mid, wqkv, smalls)
    (low, x_t), _ = seal((low, x_t), [ff_own, proj_own, proj_other])
    low_other = swap(low, Y)
    towers = tower_grad(meta, x_t, low, sums_one, sums_two, qkv_sums, cot_sum, grad_up_bias0, grad_up_bias1)
    (*towers, low, out, out_other), _ = seal((*towers, low, out, out_other), [])
    tower = Scatter(towers, TOWERS)
    tower.send()
    proj = Cross(proj_own, proj_other)
    short_output = jnp.where(short, out, out_other).reshape(4, 256, 768)
    long_output = jnp.where(short, out_other, out)[None, 0:710]
    (short_output, long_output, low), _ = seal((short_output, long_output, low), [tower])
    mine = input_grad(meta, True, low, wimg, wtext)
    mine, _ = seal(mine, [ff, proj_other])
    seal((), [proj_own, proj_other, tower])
    proj.send()
    _, (low_other,) = seal((), [proj_own, ff, proj], (low_other,))
    (low_other,), _ = seal((low_other,), [tower])
    theirs = input_grad(meta, False, low_other, wimg, wtext)
    theirs, _ = seal(theirs, [proj, tower])
    si, st = (jnp.where(short, mine[k], theirs[k]) for k in (0, 1))
    li, lt = (jnp.where(short, theirs[k], mine[k]) for k in (2, 3))
    si, st, li, lt = si.transpose(1, 0, 2), st.transpose(1, 0, 2), li.transpose(1, 0, 2), lt[None]
    seal((), [tower])
    red_ff, red_proj = ff.total, proj.total
    if grouped:
        red_tower = tower.total
        red_img, red_text = red_tower[0:24, 0:768], red_tower[24:48, 0:768]
        red_vectors = [red_tower[0:24, 768 + k] for k in range(11)]
        device = 2 * lax.axis_index(DP) + lax.axis_index(TP)
        red_up_bias = lax.dynamic_slice(red_tower, (0, 779 + device // 8), (24, 4))
        red_vectors.append(red_up_bias.T.reshape(96))
    else:
        mats = jnp.stack([absolute([part_[:, half_, :, 0:768] for part_ in towers], TOWERS[0:3]) for half_ in range(2)])
        mats = mats.reshape(2, 16, 2, 24, 768).transpose(2, 1, 0, 3, 4).reshape(2, 768, 768)
        red_img = lax.psum_scatter(mats[0], (DP, TP), scatter_dimension=0, tiled=True)
        red_text = lax.psum_scatter(mats[1], (DP, TP), scatter_dimension=0, tiled=True)
        sums = [*sums_one[0:5], qkv_sums[:, 0:384].reshape(768), qkv_sums[:, 768:1152].reshape(768),
                *sums_two[0:3], cot_sum[0], jnp.concatenate([grad_up_bias0, grad_up_bias1]).reshape(3072)]
        red_vectors = [lax.psum_scatter(v, (DP, TP), scatter_dimension=0, tiled=True) for v in sums]

    f = lambda v: v.astype(F32)
    vec = [f(v) for v in red_vectors]
    return (
        short_output, long_output, si, st, li, lt,
        f(red_img), vec[0], f(red_text), vec[1], vec[2], vec[3], vec[4],
        red_proj[:, 0:384], vec[5], red_proj[:, 384:768], red_proj[:, 768:1152], vec[6],
        red_proj[:, 1152:1536].T, vec[7], vec[8], vec[9],
        jnp.concatenate([red_ff[:, 0:768], red_ff[:, 1536:2304]], axis=1), vec[11],
        jnp.concatenate([red_ff[:, 768:1536], red_ff[:, 2304:3072]], axis=1).T, vec[10],
    )


def solution(mesh):
    rows = P(DP, None, None)
    vec = P((DP, TP))
    tower = P((DP, TP), None)
    col = P(DP, TP)
    back = P(TP, DP)
    return jax.shard_map(
        on_device,
        mesh=mesh,
        in_specs=(
            rows, rows, P(DP), rows, rows, rows, P(DP), rows,
            tower, vec, tower, vec, vec, vec, vec,
            col, vec, col, col, vec, back, vec, vec, vec, col, vec, back, vec,
        ),
        out_specs=(
            rows, rows, rows, rows, rows, rows,
            tower, vec, tower, vec, vec, vec, vec,
            col, vec, col, col, vec, back, vec, vec, vec, col, vec, back, vec,
        ),
        check_vma=False,
    )
```

```python
from functools import partial

import jax
import jax.numpy as jnp
from jax import lax
from jax.experimental import pallas as pl
from jax.experimental.pallas import tpu as pltpu
from jax.sharding import PartitionSpec as P

DP = "dp"
TP = "tensor"
BOTH = (TP, DP)
EPS = 1e-06
NEG = -1e30
BF = jnp.bfloat16
F32 = jnp.float32
ROWS = 1024
BLK = 256
MIB = 1 << 20


def dot_nn(left, right):
    return lax.dot_general(left, right, (((1,), (0,)), ((), ())), preferred_element_type=F32)


def dot_nt(left, right):
    return lax.dot_general(left, right, (((1,), (1,)), ((), ())), preferred_element_type=F32)


def flip(values):
    return values.astype(F32).T.astype(BF)


def cost(micros):
    return pl.CostEstimate(flops=int(micros * 2e8), bytes_accessed=int(micros * 1e5), transcendentals=0)


def params(limit=56):
    return pltpu.CompilerParams(dimension_semantics=("arbitrary",), vmem_limit_bytes=limit * MIB)


def whole(*shape):
    return pl.BlockSpec(shape, lambda *_: (0,) * len(shape), pipeline_mode=pl.Buffered(1))


def norm_parts(values):
    row_mean = jnp.mean(values, axis=-1, keepdims=True)
    centred = values - row_mean
    row_var = jnp.mean(centred * centred, axis=-1, keepdims=True)
    inverse = lax.rsqrt(row_var + EPS)
    return centred * inverse, inverse


def norm_back(xhat, inverse, scaled):
    first = jnp.mean(scaled, axis=-1, keepdims=True)
    second = jnp.mean(scaled * xhat, axis=-1, keepdims=True)
    return (scaled - first - xhat * second) * inverse


def is_short(meta):
    return meta[0] == 1


def active(meta, step):
    return jnp.logical_or(is_short(meta), step < 3)


CORE, X, LOW, HIGH, Y = 1, 2, 4, 8, 16
HALVES = ((LOW, X, HIGH), (X, LOW, HIGH))
TOWERS = (X, LOW, HIGH, Y)
GATHER_QKV = (Y, X, LOW, HIGH)
GATHER_TOWER = (X, Y, LOW, HIGH)
GATHER_UP = (Y, LOW, HIGH, X)
GATHER_DOWN = (X, LOW, HIGH, Y)


def relatives(meta, order):
    rest = [bit for bit in order if bit != Y]
    for core in range(2):
        for place in range(8):
            offset = core * CORE + sum(bit * (place >> (2 - k) & 1) for k, bit in enumerate(rest))
            yield core, place, jnp.bitwise_xor(meta[6], offset)


def places(meta, order):
    for core in range(2):
        for place in range(16):
            offset = core * CORE + sum(bit * (place >> (3 - k) & 1) for k, bit in enumerate(order))
            other = offset // 16
            yield core, place, jnp.bitwise_xor(meta[6], offset % 16), other, jnp.bitwise_xor(meta[5], other)


def hold_pieces(held, result):
    for group in range(16):
        held[group] = result[group * 48 : (group + 1) * 48].astype(BF)


def halves_shapes(width):
    return [jax.ShapeDtypeStruct((8, 48, width), BF)] * 2


def pack_kernel(q_ref, k_ref, v_ref, img_ref, text_ref, out_ref, small_ref, packed_ref):
    packed_ref[0, :, 0:384] = q_ref[...]
    packed_ref[0, :, 384:768] = k_ref[...]
    packed_ref[0, :, 768:1152] = v_ref[...]
    tower = jnp.concatenate([img_ref[...].astype(F32), text_ref[...].astype(F32)], axis=0)
    packed_ref[0, :, 1152:1920] = tower.astype(BF)
    packed_ref[0, :, 1920:2304] = out_ref[...]
    small = jnp.concatenate([small_ref[...].astype(F32), jnp.zeros((112, 24), F32)], axis=0).T
    packed_ref[0, :, 2304:2432] = jnp.concatenate([small, jnp.zeros((24, 128), F32)], axis=0).astype(BF)


def pack(*args):
    return pl.pallas_call(
        pack_kernel,
        grid=(1,),
        in_specs=[whole(*arg.shape) for arg in args],
        out_specs=whole(1, 48, 2432),
        out_shape=jax.ShapeDtypeStruct((1, 48, 2432), BF),
        compiler_params=params(40),
        name="pack",
        cost_estimate=cost(2),
    )(*args)


def prepare_kernel(x_ref, cot_ref, xt_ref, cott_ref, sum_ref):
    xt_ref[...] = flip(x_ref[...])
    cott_ref[...] = flip(cot_ref[...])

    @pl.when(pl.program_id(0) == 0)
    def _():
        sum_ref[...] = jnp.zeros_like(sum_ref)

    sum_ref[...] += jnp.sum(cot_ref[...].astype(F32), axis=0, keepdims=True)


def prepare(x, cot):
    row = pl.BlockSpec((BLK, 768), lambda i: (i, 0))
    column = pl.BlockSpec((768, BLK), lambda i: (0, i))
    return pl.pallas_call(
        prepare_kernel,
        grid=(4,),
        in_specs=[row, row],
        out_specs=[column, column, whole(1, 768)],
        out_shape=[
            jax.ShapeDtypeStruct((768, ROWS), BF),
            jax.ShapeDtypeStruct((768, ROWS), BF),
            jax.ShapeDtypeStruct((1, 768), F32),
        ],
        compiler_params=params(5),
        name="prepare",
        cost_estimate=cost(0.1),
    )(x, cot)


def embed_kernel(
    meta, x_ref, qkv_00, qkv_01, qkv_10, qkv_11, tower_00, tower_01, tower_10, tower_11,
    stream_ref, n1t_ref, qkv0_ref, qkv1_ref, wimg_ref, wtext_ref, wqkv_ref, wout_ref, sm_ref, bias_ref,
    wimg_f, wtext_f, wout_pieces, columns, up_columns,
):
    step = pl.program_id(0)
    qkv = (qkv_00, qkv_01), (qkv_10, qkv_11)
    towers = (tower_00, tower_01), (tower_10, tower_11)

    @pl.when(step == 0)
    def _():
        for core, place, group, other, _ in places(meta, GATHER_QKV):
            wqkv_ref[other, group] = qkv[core][place // 8][place % 8]
        for core, place, group, other, half in places(meta, GATHER_TOWER):
            tower = towers[core][place // 8].at[place % 8]
            piece = tower[:, 0:768].astype(F32)
            rows = pl.ds(pl.multiple_of(24 * (2 * group + half), 8), 24)
            wimg_f[rows, :] = piece[0:24]
            wtext_f[rows, :] = piece[24:48]
            wout_pieces[other, group] = tower[:, 768:1152]
            device = 2 * group + half
            small = tower[0:32, 1152:1280].astype(F32)[0:24]
            columns[rows, :] = small
            for part in range(4):
                start = pl.multiple_of(96 * device + 24 * part, 8)
                up_columns[pl.ds(start, 24), :] = pltpu.roll(small, 128 - 11 - part, 1)
        wimg_ref[...] = wimg_f[...].astype(BF)
        wtext_ref[...] = wtext_f[...].astype(BF)
        for half in range(2):
            wout_ref[:, 384 * half : 384 * half + 384] = wout_pieces[half].reshape(768, 384)
        sm_ref[...] = columns[...].T[0:16]
        for chunk in range(4):
            bias_ref[chunk] = up_columns[768 * chunk : 768 * chunk + 768, :].T[0:1]

    @pl.when(active(meta, step))
    def _():
        with_image = jnp.logical_or(is_short(meta), step == 0)

        @pl.when(with_image)
        def _():
            first = dot_nn(x_ref[0:208, :], wimg_ref[...]) + sm_ref[0:1, :]
            second = dot_nn(x_ref[192:256, :], wtext_ref[...]) + sm_ref[1:2, :]
            index = lax.broadcasted_iota(jnp.int32, (16, 768), 0)
            stream_ref[0:192, :] = first[0:192]
            stream_ref[192:208, :] = jnp.where(index < 6, first[192:208], second[0:16])
            stream_ref[208:256, :] = second[16:64]
            stream_ref[0:1, :] = sm_ref[2:3, :]

        @pl.when(jnp.logical_not(with_image))
        def _():
            stream_ref[...] = dot_nn(x_ref[...], wtext_ref[...]) + sm_ref[1:2, :]

        xhat, _ = norm_parts(stream_ref[...])
        scaled = xhat * sm_ref[3:4, :] + sm_ref[4:5, :]
        normed = scaled.astype(BF)
        n1t_ref[...] = flip(normed)
        for half, qkv_ref in enumerate((qkv0_ref, qkv1_ref)):
            out = dot_nn(normed, wqkv_ref[half].reshape(768, 1152))
            lanes = pl.ds(pl.multiple_of(384 * jnp.bitwise_xor(meta[5], half), 128), 384)
            qkv_ref[:, 0:384] = (out[:, 0:384] + sm_ref[5:6, lanes]).astype(BF)
            qkv_ref[:, 384:768] = out[:, 384:768].astype(BF)
            qkv_ref[:, 768:1152] = (out[:, 768:1152] + sm_ref[6:7, lanes]).astype(BF)


def embed(meta, x, qkv_all, tower_all):
    row = lambda width: pl.BlockSpec((BLK, width), lambda i, m: (i, 0))
    return pl.pallas_call(
        embed_kernel,
        grid_spec=pltpu.PrefetchScalarGridSpec(
            num_scalar_prefetch=1,
            grid=(4,),
            in_specs=[row(768)] + [whole(8, 48, 1152)] * 4 + [whole(8, 48, 1280)] * 4,
            out_specs=[
                row(768),
                pl.BlockSpec((768, BLK), lambda i, m: (0, i)),
                row(1152),
                row(1152),
                whole(768, 768),
                whole(768, 768),
                whole(2, 16, 48, 1152),
                whole(768, 768),
                whole(16, 768),
                whole(4, 1, 768),
            ],
            scratch_shapes=[
                pltpu.VMEM((768, 768), F32),
                pltpu.VMEM((768, 768), F32),
                pltpu.VMEM((2, 16, 48, 384), BF),
                pltpu.VMEM((768, 128), F32),
                pltpu.VMEM((3072, 128), F32),
            ],
        ),
        out_shape=[
            jax.ShapeDtypeStruct((ROWS, 768), F32),
            jax.ShapeDtypeStruct((768, ROWS), BF),
            jax.ShapeDtypeStruct((ROWS, 1152), BF),
            jax.ShapeDtypeStruct((ROWS, 1152), BF),
            jax.ShapeDtypeStruct((768, 768), BF),
            jax.ShapeDtypeStruct((768, 768), BF),
            jax.ShapeDtypeStruct((2, 16, 48, 1152), BF),
            jax.ShapeDtypeStruct((768, 768), BF),
            jax.ShapeDtypeStruct((16, 768), F32),
            jax.ShapeDtypeStruct((4, 1, 768), F32),
        ],
        compiler_params=params(24),
        name="embed",
        cost_estimate=cost(12),
    )(meta, x, *qkv_all, *tower_all)


def head_lanes(values, head):
    lane = lax.broadcasted_iota(jnp.int32, values.shape, 1)
    keep = lane < 64 if head == 0 else lane >= 64
    return jnp.where(keep, values, jnp.zeros_like(values))


def attn_forward_part(q, k, v, limit):
    out, lse = None, []
    for head in range(2):
        scores = dot_nt(head_lanes(q, head), k)
        index = lax.broadcasted_iota(jnp.int32, scores.shape, 1)
        scores = jnp.where(index < limit, scores, NEG)
        top = jnp.max(scores, axis=1, keepdims=True)
        weight = jnp.exp(scores - top)
        total = jnp.sum(weight, axis=1, keepdims=True)
        add = dot_nn(weight.astype(BF), head_lanes(v, head)) * (1.0 / total)
        out = add if out is None else out + add
        lse.append(jnp.broadcast_to(top + jnp.log(total), (256, 128)).T[0:1])
    return out.astype(BF), jnp.concatenate(lse, axis=0)


def attn_forward_kernel(meta, qkv_ref, out_ref, lse_ref):
    pair = pl.program_id(0)

    def part(kind, start, size):
        lanes = pl.ds(pl.multiple_of(384 * kind + 128 * pair, 128), 128)
        return qkv_ref[start : start + size, lanes]

    @pl.when(is_short(meta))
    def _():
        for member in range(4):
            start = 256 * member
            q = part(0, start, 256) * BF(0.125)
            out, lse = attn_forward_part(
                q, part(1, start, 256), part(2, start, 256), meta[1 + member]
            )
            out_ref[start : start + 256, :] = out
            lse_ref[0, :, start : start + 256] = lse

    @pl.when(jnp.logical_not(is_short(meta)))
    def _():
        k = part(1, 0, 768)
        v = part(2, 0, 768)
        for member in range(3):
            start = 256 * member
            q = part(0, start, 256) * BF(0.125)
            out, lse = attn_forward_part(q, k, v, meta[1])
            out_ref[start : start + 256, :] = out
            lse_ref[0, :, start : start + 256] = lse


def attn_forward(meta, qkv):
    return pl.pallas_call(
        attn_forward_kernel,
        grid_spec=pltpu.PrefetchScalarGridSpec(
            num_scalar_prefetch=1,
            grid=(3,),
            in_specs=[whole(ROWS, 1152)],
            out_specs=[
                pl.BlockSpec((ROWS, 128), lambda j, m: (0, j)),
                pl.BlockSpec((1, 2, ROWS), lambda j, m: (j, 0, 0)),
            ],
        ),
        out_shape=[
            jax.ShapeDtypeStruct((ROWS, 384), BF),
            jax.ShapeDtypeStruct((3, 2, ROWS), F32),
        ],
        compiler_params=params(6),
        name="attn_forward",
        cost_estimate=cost(14),
    )(meta, qkv)


def attn_back_part(q, k, v, grad, lse, limit):
    grad_k, grad_v, grad_q = None, None, None
    for head in range(2):
        q_head = head_lanes(q, head)
        g_head = head_lanes(grad, head)
        scores = dot_nt(k, q_head)
        index = lax.broadcasted_iota(jnp.int32, scores.shape, 0)
        probs = jnp.exp(scores - lse[head : head + 1])
        probs = jnp.where(index < limit, probs, 0.0)
        grad_probs = dot_nt(v, g_head)
        row_dot = jnp.sum(probs * grad_probs, axis=0, keepdims=True)
        grad_scores = (probs * (grad_probs - row_dot)).astype(BF)
        add_v = dot_nn(probs.astype(BF), g_head)
        add_k = dot_nn(grad_scores, q_head)
        grad_v = add_v if grad_v is None else grad_v + add_v
        grad_k = add_k if grad_k is None else grad_k + add_k
        add_q = lax.dot_general(
            grad_scores, head_lanes(k, head), (((0,), (0,)), ((), ())), preferred_element_type=F32
        )
        grad_q = add_q if grad_q is None else grad_q + add_q
    return (grad_q * 0.125).astype(BF), grad_k, grad_v


def attn_back_kernel(meta, qkv_ref, grad_ref, lse_ref, out_ref, acc_k, acc_v):
    pair = pl.program_id(0)

    def lanes(kind):
        return pl.ds(pl.multiple_of(384 * kind + 128 * pair, 128), 128)

    def part(kind, start, size):
        return qkv_ref[start : start + size, lanes(kind)]

    @pl.when(is_short(meta))
    def _():
        for member in range(4):
            rows = slice(256 * member, 256 * member + 256)
            start = 256 * member
            q = part(0, start, 256) * BF(0.125)
            k = part(1, start, 256)
            grad_q, grad_k, grad_v = attn_back_part(
                q, k, part(2, start, 256), grad_ref[rows, :], lse_ref[0, :, rows], meta[1 + member]
            )
            out_ref[rows, lanes(0)] = grad_q
            out_ref[rows, lanes(1)] = grad_k.astype(BF)
            out_ref[rows, lanes(2)] = grad_v.astype(BF)

    @pl.when(jnp.logical_not(is_short(meta)))
    def _():
        k = part(1, 0, 768)
        v = part(2, 0, 768)
        for member in range(3):
            rows = slice(256 * member, 256 * member + 256)
            start = 256 * member
            q = part(0, start, 256) * BF(0.125)
            grad_q, grad_k, grad_v = attn_back_part(
                q, k, v, grad_ref[rows, :], lse_ref[0, :, rows], meta[1]
            )
            out_ref[rows, lanes(0)] = grad_q
            if member == 0:
                acc_k[...] = grad_k
                acc_v[...] = grad_v
            else:
                acc_k[...] += grad_k
                acc_v[...] += grad_v
        out_ref[0:768, lanes(1)] = acc_k[...].astype(BF)
        out_ref[0:768, lanes(2)] = acc_v[...].astype(BF)


def attn_back(meta, qkv, grad, lse):
    return pl.pallas_call(
        attn_back_kernel,
        grid_spec=pltpu.PrefetchScalarGridSpec(
            num_scalar_prefetch=1,
            grid=(3,),
            in_specs=[
                whole(ROWS, 1152),
                pl.BlockSpec((ROWS, 128), lambda j, m: (0, j)),
                pl.BlockSpec((1, 2, ROWS), lambda j, m: (j, 0, 0)),
            ],
            out_specs=whole(ROWS, 1152),
            scratch_shapes=[pltpu.VMEM((768, 128), F32), pltpu.VMEM((768, 128), F32)],
        ),
        out_shape=jax.ShapeDtypeStruct((ROWS, 1152), BF),
        compiler_params=params(8),
        name="attn_back",
        cost_estimate=cost(0.1),
    )(meta, qkv, grad, lse)


def mid_kernel(meta, att0_ref, att1_ref, stream_ref, wout_ref, sm_ref, mid_ref, n2_ref, n2t_ref):
    @pl.when(active(meta, pl.program_id(0)))
    def _():
        attended = jnp.concatenate([att0_ref[...], att1_ref[...]], axis=1)
        mid = stream_ref[...] + dot_nt(attended, wout_ref[...]) + sm_ref[7:8, :]
        mid_ref[...] = mid
        xhat, _ = norm_parts(mid)
        normed = (xhat * sm_ref[8:9, :] + sm_ref[9:10, :]).astype(BF)
        n2_ref[...] = normed
        n2t_ref[...] = flip(normed)

    @pl.when(jnp.logical_not(active(meta, pl.program_id(0))))
    def _():
        n2t_ref[...] = jnp.zeros_like(n2t_ref)


def mid_stage(meta, attended, stream, wout, smalls):
    row = lambda width: pl.BlockSpec((BLK, width), lambda i, m: (i, 0))
    return pl.pallas_call(
        mid_kernel,
        grid_spec=pltpu.PrefetchScalarGridSpec(
            num_scalar_prefetch=1,
            grid=(4,),
            in_specs=[
                row(384),
                row(384),
                row(768),
                whole(768, 768),
                whole(16, 768),
            ],
            out_specs=[row(768), row(768), pl.BlockSpec((768, BLK), lambda i, m: (0, i))],
        ),
        out_shape=[
            jax.ShapeDtypeStruct((ROWS, 768), F32),
            jax.ShapeDtypeStruct((ROWS, 768), BF),
            jax.ShapeDtypeStruct((768, ROWS), BF),
        ],
        compiler_params=params(6),
        name="mid_stage",
        cost_estimate=cost(7),
    )(meta, *attended, stream, wout, smalls)


INV_ROOT2 = 0.7071067811865476
INV_ROOT2PI = 0.3989422804014327


def mlp_kernel(
    other,
    meta, n2_ref, n2_t, cot_ref, cot_t, up_near, up_far, down_00, down_01, down_10, down_11, bias_ref,
    out_ref, gn_ref, keep_ref, send_ref, gbias_ref,
    wup_pieces, wdown_pieces, hid, gpre, out_sum, gn_sum,
):
    step = pl.program_id(0)
    down = (down_00, down_01), (down_10, down_11)
    for core, place, group, half, _ in places(meta, GATHER_UP):
        if half == other:
            wup_pieces[group] = (up_near, up_far)[core][place % 8]
    for core, place, group, half, _ in places(meta, GATHER_DOWN):
        if half == other:
            wdown_pieces[group] = down[core][place // 8][place % 8 // 2, 0]
    bias = bias_ref[0]

    gbias_ref[...] = jnp.zeros_like(gbias_ref)

    @pl.loop(0, jnp.where(is_short(meta), 4, 3))
    def _(block):
        wup = wup_pieces[...].reshape(768, 768)
        wdown = wdown_pieces[...].reshape(768, 768)
        rows = pl.ds(pl.multiple_of(256 * block, 256), 256)
        pre = dot_nn(n2_ref[rows, :], wup) + bias
        cdf = 0.5 + 0.5 * lax.erf(pre * INV_ROOT2)
        hidden = (pre * cdf).astype(BF)
        hid[rows, :] = hidden
        slope = cdf + pre * (jnp.exp(pre * pre * -0.5) * INV_ROOT2PI)
        grad_pre = (dot_nn(cot_ref[rows, :], wdown) * slope).astype(BF)
        gpre[rows, :] = grad_pre
        gbias_ref[0] += jnp.sum(grad_pre.astype(F32), axis=0, keepdims=True)
        out_add = dot_nt(hidden, wdown)
        gn_add = dot_nt(grad_pre, wup)

        @pl.when(step == 0)
        def _():
            out_sum[rows, :] = out_add
            gn_sum[rows, :] = gn_add

        @pl.when(step > 0)
        def _():
            out_ref[rows, :] = (out_sum[rows, :] + out_add).astype(BF)
            gn_ref[rows, :] = (gn_sum[rows, :] + gn_add).astype(BF)

    @pl.when(jnp.logical_and(jnp.logical_not(is_short(meta)), step == 0))
    def _():
        hid[768:1024, :] = jnp.zeros((256, 768), BF)
        gpre[768:1024, :] = jnp.zeros((256, 768), BF)

    held = wup_pieces
    for kind, left, right in ((0, n2_t, gpre), (1, cot_t, hid)):
        hold_pieces(held, dot_nn(left[...], right[...]))
        lanes = slice(768 * kind, 768 * kind + 768)
        for core, place, group in relatives(meta, HALVES[other]):
            (keep_ref, send_ref)[core][place, :, lanes] = held[group]


def mlp_half(meta, other, n2, n2_t, cot, cot_t, up_all, down_all, up_bias):
    rows, turned = whole(ROWS, 768), whole(768, ROWS)
    bias = pl.BlockSpec((1, 1, 768), lambda c, m: (2 * jnp.bitwise_xor(other, m[5]) + c, 0, 0))
    return pl.pallas_call(
        partial(mlp_kernel, other),
        grid_spec=pltpu.PrefetchScalarGridSpec(
            num_scalar_prefetch=1,
            grid=(2,),
            in_specs=[
                rows,
                turned,
                rows,
                turned,
                *[pl.BlockSpec((8, 48, 768), lambda c, m: (0, 0, c))] * 2,
                *[pl.BlockSpec((4, 1, 48, 768), lambda c, m: (0, other, 0, c))] * 4,
                bias,
            ],
            out_specs=[
                rows,
                rows,
                pl.BlockSpec((8, 48, 1536), lambda c, m: (0, 0, c)),
                pl.BlockSpec((8, 48, 1536), lambda c, m: (0, 0, c)),
                pl.BlockSpec((1, 1, 768), lambda c, m: (c, 0, 0)),
            ],
            scratch_shapes=[
                pltpu.VMEM((16, 48, 768), BF),
                pltpu.VMEM((16, 48, 768), BF),
                pltpu.VMEM((ROWS, 768), BF),
                pltpu.VMEM((ROWS, 768), BF),
                pltpu.VMEM((ROWS, 768), F32),
                pltpu.VMEM((ROWS, 768), F32),
            ],
        ),
        out_shape=[
            jax.ShapeDtypeStruct((ROWS, 768), BF),
            jax.ShapeDtypeStruct((ROWS, 768), BF),
            *halves_shapes(3072),
            jax.ShapeDtypeStruct((2, 1, 768), F32),
        ],
        compiler_params=params(26),
        name="mlp_half",
        cost_estimate=cost(0.1),
    )(
        meta, n2, n2_t, cot, cot_t,
        up_all[other], up_all[2 + other],
        *(part.reshape(4, 2, 48, 1536) for part in down_all),
        up_bias,
    )


def back_mid_kernel(
    meta, mlp0_ref, gn0_ref, mlp1_ref, gn1_ref, mid_ref, cot_ref, att0_ref, att1_ref, wout_ref, sm_ref,
    out_ref, gmid_ref, gatt0_ref, gatt1_ref, gout0_keep, gout0_send, gout1_keep, gout1_send, sums_ref,
    low_t, held,
):
    step = pl.program_id(0)

    @pl.when(step == 0)
    def _():
        sums_ref[...] = jnp.zeros_like(sums_ref)

    @pl.when(jnp.logical_and(active(meta, step), step < 4))
    def _():
        mid = mid_ref[...]
        out_ref[...] = (mid + (mlp0_ref[...].astype(F32) + mlp1_ref[...].astype(F32)) + sm_ref[10:11, :]).astype(BF)
        xhat, inverse = norm_parts(mid)
        grad = gn0_ref[...].astype(F32) + gn1_ref[...].astype(F32)
        cot = cot_ref[...].astype(F32)
        grad_mid = cot + norm_back(xhat, inverse, grad * sm_ref[8:9, :])
        gmid_ref[...] = grad_mid
        low = grad_mid.astype(BF)
        grad_att = dot_nn(low, wout_ref[...]).astype(BF)
        gatt0_ref[...] = grad_att[:, 0:384]
        gatt1_ref[...] = grad_att[:, 384:768]
        low_t[step] = flip(low)
        sums_ref[0:1, :] += jnp.sum(grad_mid, axis=0, keepdims=True)
        sums_ref[1:2, :] += jnp.sum(grad * xhat, axis=0, keepdims=True)
        sums_ref[2:3, :] += jnp.sum(grad, axis=0, keepdims=True)

    for half, att_ref in enumerate((att0_ref, att1_ref)):
        for count, chosen in ((4, is_short(meta)), (3, jnp.logical_not(is_short(meta)))):

            @pl.when(jnp.logical_and(chosen, step == 4 + half))
            def _(count=count, att_ref=att_ref, half=half):
                total = None
                for block in range(count):
                    add = dot_nn(low_t[block], att_ref[256 * block : 256 * block + 256, :])
                    total = add if total is None else total + add
                hold_pieces(held, total)
                gouts = ((gout0_keep, gout0_send), (gout1_keep, gout1_send))[half]
                for core, place, group in relatives(meta, HALVES[half]):
                    gouts[core][place] = held[group]


def back_mid(meta, mlp_sums, mid, cot, attended, wout, smalls):
    row = pl.BlockSpec((BLK, 768), lambda i, m: (jnp.minimum(i, 3), 0))
    thin = pl.BlockSpec((BLK, 384), lambda i, m: (jnp.minimum(i, 3), 0))
    return pl.pallas_call(
        back_mid_kernel,
        grid_spec=pltpu.PrefetchScalarGridSpec(
            num_scalar_prefetch=1,
            grid=(6,),
            in_specs=[
                row,
                row,
                row,
                row,
                row,
                row,
                whole(ROWS, 384),
                whole(ROWS, 384),
                whole(768, 768),
                whole(16, 768),
            ],
            out_specs=[
                row,
                row,
                thin,
                thin,
                *[whole(8, 48, 384)] * 4,
                whole(8, 768),
            ],
            scratch_shapes=[
                pltpu.VMEM((4, 768, 256), BF),
                pltpu.VMEM((16, 48, 384), BF),
            ],
        ),
        out_shape=[
            jax.ShapeDtypeStruct((ROWS, 768), BF),
            jax.ShapeDtypeStruct((ROWS, 768), F32),
            jax.ShapeDtypeStruct((ROWS, 384), BF),
            jax.ShapeDtypeStruct((ROWS, 384), BF),
            *halves_shapes(384),
            *halves_shapes(384),
            jax.ShapeDtypeStruct((8, 768), F32),
        ],
        compiler_params=params(10),
        name="back_mid",
        cost_estimate=cost(0.1),
    )(meta, *mlp_sums, mid, cot, *attended, wout, smalls)


def back_in_kernel(
    meta, dqkv0_ref, dqkv1_ref, stream_ref, gmid_ref, wqkv_ref, sm_ref, low_ref, sums_ref, qsum_ref
):
    step = pl.program_id(0)

    @pl.when(step == 0)
    def _():
        sums_ref[...] = jnp.zeros_like(sums_ref)
        qsum_ref[...] = jnp.zeros_like(qsum_ref)

    @pl.when(active(meta, step))
    def _():
        grad = None
        for half, dqkv_ref in enumerate((dqkv0_ref, dqkv1_ref)):
            dqkv = dqkv_ref[...]
            add = dot_nt(dqkv, wqkv_ref[half].reshape(768, 1152))
            grad = add if grad is None else grad + add
            qsum_ref[half : half + 1, :] += jnp.sum(dqkv.astype(F32), axis=0, keepdims=True)
        xhat, inverse = norm_parts(stream_ref[...])
        grad_in = gmid_ref[...] + norm_back(xhat, inverse, grad * sm_ref[3:4, :])
        low_ref[...] = grad_in.astype(BF)
        with_image = jnp.logical_or(is_short(meta), step == 0)
        limit = jnp.where(with_image, 198, 0)
        index = lax.broadcasted_iota(jnp.int32, (BLK, 768), 0)
        before = jnp.sum(jnp.where(index < limit, grad_in, 0.0), axis=0, keepdims=True)
        cls = jnp.where(with_image, grad_in[0:1], 0.0)
        everything = jnp.sum(grad_in, axis=0, keepdims=True)
        sums_ref[0:1, :] += before - cls
        sums_ref[1:2, :] += everything - before
        sums_ref[2:3, :] += cls
        sums_ref[3:4, :] += jnp.sum(grad * xhat, axis=0, keepdims=True)
        sums_ref[4:5, :] += jnp.sum(grad, axis=0, keepdims=True)


def back_in(meta, dqkv, stream, grad_mid, wqkv, smalls):
    row = lambda width: pl.BlockSpec((BLK, width), lambda i, m: (i, 0))
    return pl.pallas_call(
        back_in_kernel,
        grid_spec=pltpu.PrefetchScalarGridSpec(
            num_scalar_prefetch=1,
            grid=(4,),
            in_specs=[row(1152), row(1152), row(768), row(768), whole(2, 16, 48, 1152), whole(16, 768)],
            out_specs=[row(768), whole(8, 768), whole(2, 1152)],
        ),
        out_shape=[
            jax.ShapeDtypeStruct((ROWS, 768), BF),
            jax.ShapeDtypeStruct((8, 768), F32),
            jax.ShapeDtypeStruct((2, 1152), F32),
        ],
        compiler_params=params(10),
        name="back_in",
        cost_estimate=cost(0.1),
    )(meta, *dqkv, stream, grad_mid, wqkv, smalls)


def proj_grad_kernel(other, meta, n1t_ref, dqkv_ref, gout_keep, gout_send, keep_ref, send_ref, held):
    step = pl.program_id(0)
    for size, chosen in ((1024, is_short(meta)), (768, jnp.logical_not(is_short(meta)))):

        @pl.when(jnp.logical_and(chosen, step < 3))
        def _(size=size):
            hold_pieces(held, dot_nn(n1t_ref[:, 0:size], dqkv_ref[0:size, :]))
            for core, place, group in relatives(meta, HALVES[other]):
                (keep_ref, send_ref)[core][place] = held[group]

    @pl.when(step == 3)
    def _():
        keep_ref[...] = gout_keep[...]
        send_ref[...] = gout_send[...]


def proj_grad(meta, other, n1_t, dqkv, grad_out):
    columns = pl.BlockSpec((8, 48, 384), lambda c, m: (0, 0, c))
    return pl.pallas_call(
        partial(proj_grad_kernel, other),
        grid_spec=pltpu.PrefetchScalarGridSpec(
            num_scalar_prefetch=1,
            grid=(4,),
            in_specs=[
                whole(768, ROWS),
                pl.BlockSpec((ROWS, 384), lambda c, m: (0, jnp.minimum(c, 2))),
                whole(8, 48, 384),
                whole(8, 48, 384),
            ],
            out_specs=[columns, columns],
            scratch_shapes=[pltpu.VMEM((16, 48, 384), BF)],
        ),
        out_shape=halves_shapes(1536),
        compiler_params=params(8),
        name="proj_grad",
        cost_estimate=cost(0.1),
    )(meta, n1_t, dqkv, *grad_out)


def tower_grad_kernel(
    meta, x_t, low_ref, one_ref, two_ref, qkv_ref, down_ref, up0_ref, up1_ref,
    keep_ref, send_ref, gimg, gtext, wimg, wtext, vectors, columns,
):
    vectors[...] = jnp.zeros_like(vectors)
    vectors[0:5, :] = one_ref[0:5, :]
    for half in range(2):
        lanes = pl.ds(pl.multiple_of(384 * jnp.bitwise_xor(meta[5], half), 128), 384)
        vectors[5:6, lanes] = qkv_ref[half : half + 1, 0:384]
        vectors[6:7, lanes] = qkv_ref[half : half + 1, 768:1152]
    vectors[7:10, :] = two_ref[0:3, :]
    vectors[10:11, :] = down_ref[...]
    for half, up_ref in enumerate((up0_ref, up1_ref)):
        for chunk in range(2):
            vectors[pl.ds(11 + 2 * jnp.bitwise_xor(meta[5], half) + chunk, 1), :] = up_ref[chunk]
    columns[...] = vectors[...].T
    for block in range(4):
        rows = slice(256 * block, 256 * block + 256)
        with_image = jnp.logical_or(is_short(meta), block == 0)
        limit = jnp.where(with_image, 198, 0)
        index = lax.broadcasted_iota(jnp.int32, (BLK, 768), 0)
        low = low_ref[rows, :].astype(F32)
        gimg[rows, :] = jnp.where(index < limit, low, 0.0).astype(BF)
        gtext[rows, :] = jnp.where(index < limit, 0.0, low).astype(BF)

    for size, chosen in ((1024, is_short(meta)), (768, jnp.logical_not(is_short(meta)))):

        @pl.when(chosen)
        def _(size=size):
            wtext[...] = dot_nn(x_t[:, 0:size], gtext[0:size, :])
            image_size = size if size == 1024 else 256
            wimg[...] = dot_nn(x_t[:, 0:image_size], gimg[0:image_size, :])

    lane = lax.broadcasted_iota(jnp.int32, (24, 128), 1)
    for core, place, group in relatives(meta, TOWERS):
        ref = (keep_ref, send_ref)[core]
        for half in range(2):
            device = 2 * group + jnp.bitwise_xor(meta[5], half)
            rows = pl.ds(pl.multiple_of(24 * device, 8), 24)
            piece = jnp.concatenate([wimg[rows, :], wtext[rows, :]], axis=0).astype(BF)
            ref[place, half, :, 0:768] = piece
            small = jnp.where(lane < 11, columns[rows, :], 0.0)
            for part in range(4):
                start = 96 * jnp.bitwise_and(device, 7) + 24 * part
                some = columns[pl.ds(pl.multiple_of(start, 8), 24), :]
                some = jnp.where(lane == 11 + lax.shift_right_logical(device, 3), some, 0.0)
                small += some if part == 0 else pltpu.roll(some, part, 1)
            ref[place, half, :, 768:896] = jnp.concatenate([small, jnp.zeros_like(small)], axis=0).astype(BF)


def tower_grad(meta, x_t, low, *sums):
    return pl.pallas_call(
        tower_grad_kernel,
        grid_spec=pltpu.PrefetchScalarGridSpec(
            num_scalar_prefetch=1,
            grid=(1,),
            in_specs=[
                whole(768, ROWS),
                whole(ROWS, 768),
                whole(8, 768),
                whole(8, 768),
                whole(2, 1152),
                whole(1, 768),
                whole(2, 1, 768),
                whole(2, 1, 768),
            ],
            out_specs=[whole(8, 2, 48, 896)] * 2,
            scratch_shapes=[
                pltpu.VMEM((ROWS, 768), BF),
                pltpu.VMEM((ROWS, 768), BF),
                pltpu.VMEM((768, 768), F32),
                pltpu.VMEM((768, 768), F32),
                pltpu.VMEM((128, 768), F32),
                pltpu.VMEM((768, 128), F32),
            ],
        ),
        out_shape=[jax.ShapeDtypeStruct((8, 2, 48, 896), BF)] * 2,
        compiler_params=params(11),
        name="tower_grad",
        cost_estimate=cost(0.1),
    )(meta, x_t, low, *sums)


def input_grad_kernel(own, meta, rows_ref, wimg_ref, wtext_ref, si_ref, st_ref, li_ref, lt_ref, held):
    short = is_short(meta) if own else jnp.logical_not(is_short(meta))

    @pl.when(short)
    def _():
        for pair in range(4):
            start = 256 * pair
            held[0:208, :] = dot_nt(rows_ref[start : start + 208, :], wimg_ref[...])
            si_ref[:, pair, :] = held[1:198, :]
            held[0:64, :] = dot_nt(rows_ref[start + 192 : start + 256, :], wtext_ref[...])
            st_ref[:, pair, :] = held[6:64, :]

    @pl.when(jnp.logical_not(short))
    def _():
        held[0:208, :] = dot_nt(rows_ref[0:208, :], wimg_ref[...])
        li_ref[:, 0, :] = held[1:198, :]
        held[0:576, :] = dot_nt(rows_ref[192:768, :], wtext_ref[...])
        lt_ref[...] = held[6:518, :]


def input_grad(meta, own, rows, wimg, wtext):
    shapes = [(197, 4, 768), (58, 4, 768), (197, 1, 768), (512, 768)]
    return pl.pallas_call(
        partial(input_grad_kernel, own),
        grid_spec=pltpu.PrefetchScalarGridSpec(
            num_scalar_prefetch=1,
            grid=(1,),
            in_specs=[whole(ROWS, 768), whole(768, 768), whole(768, 768)],
            out_specs=[whole(*shape) for shape in shapes],
            scratch_shapes=[pltpu.VMEM((576, 768), F32)],
        ),
        out_shape=[jax.ShapeDtypeStruct(shape, F32) for shape in shapes],
        compiler_params=params(12),
        name="input_grad",
        cost_estimate=cost(0.1),
    )(meta, rows, wimg, wtext)


def swap(values, bits):
    if bits == Y:
        return lax.ppermute(values, TP, [(0, 1), (1, 0)])
    if bits < Y:
        return lax.ppermute(values, DP, [(i, i ^ bits) for i in range(16)])
    step = 2 * (bits - Y) + 1
    return lax.ppermute(values, (DP, TP), [(i, i ^ step) for i in range(32)])


def after(values, *others):
    return lax.optimization_barrier((values, *others))[0]


def plus(left, right):
    return (left.astype(F32) + right.astype(F32)).astype(BF)


def absolute(arrays, order):
    width = arrays[0].shape[-1]
    both = jnp.stack(arrays).reshape(2, *(2 for _ in order), 48, width)
    at = {bit: 1 + k for k, bit in enumerate(order)}
    first = [at[Y]] if Y in at else []
    both = both.transpose(*first, at[HIGH], at[LOW], at[X], 0, len(order) + 1, len(order) + 2)
    return both.reshape(-1, width)


class Scatter:
    def __init__(self, pieces, order):
        self.order = (CORE, *order)
        self.arrived = None
        if lax.axis_size(DP) != 16:
            rows = absolute(pieces, order)
            self.total = lax.psum_scatter(rows, BOTH, scatter_dimension=0, tiled=True).astype(F32)
            self.order = ()
            return
        shape = (2, 2, 2, 2, 48, pieces[0].shape[-1])
        self.keep, self.sent = pieces[0].reshape(shape), pieces[1].reshape(shape)

    def send(self):
        if self.order:
            self.arrived = swap(self.sent, self.order[0])

    def add(self):
        if self.order:
            if len(self.order) == 1:
                self.total = self.keep.astype(F32) + self.arrived.astype(F32)
            else:
                self.keep, self.sent = plus(self.keep[0], self.arrived[0]), plus(self.keep[1], self.arrived[1])
            self.arrived = None
            self.order = self.order[1:]


class Half:
    def __init__(self, pieces, other):
        self.other = other
        self.order = (CORE, *HALVES[other][0:2])
        self.arrived = None
        self.pieces = pieces
        if lax.axis_size(DP) != 16:
            self.order = ()
            return
        shape = (2, 2, 2, 48, pieces[0].shape[-1])
        self.keep, self.sent = pieces[0].reshape(shape), pieces[1].reshape(shape)

    def send(self):
        if self.order:
            self.arrived = swap(self.sent, self.order[0])

    def add(self):
        if self.order:
            self.order = self.order[1:]
            if self.order:
                self.keep, self.sent = plus(self.keep[0], self.arrived[0]), plus(self.keep[1], self.arrived[1])
            else:
                self.keep = plus(self.keep, self.arrived)
            self.arrived = None


class Cross:
    def __init__(self, own, other):
        self.own, self.other = own, other
        self.arrived = None
        self.order = (Y, HIGH)
        if lax.axis_size(DP) != 16:
            rows = jnp.concatenate([absolute(half.pieces, HALVES[half.other]) for half in (own, other)])
            self.total = lax.psum_scatter(rows, BOTH, scatter_dimension=0, tiled=True).astype(F32)
            self.order = ()

    def send(self):
        if self.order and self.order[0] == Y and not self.other.order:
            self.arrived = swap(self.other.keep, Y)
        elif self.order and self.order[0] == HIGH and not self.own.order:
            self.sent = plus(self.own.keep[1], self.crossed[1])
            self.arrived = swap(self.sent, HIGH)

    def add(self):
        if self.order and self.order[0] == Y:
            self.crossed = self.arrived
        elif self.order:
            keep = self.own.keep[0].astype(F32) + self.crossed[0].astype(F32)
            self.total = keep + self.arrived.astype(F32)
        self.arrived = None
        self.order = self.order[1:]


class Gather:
    def __init__(self, joined, widths, phases, orders, whole=None):
        self.joined, self.widths, self.phases = joined, widths, phases
        self.parts = None if joined is None else self.split(joined)
        self.arrived = None
        if lax.axis_size(DP) != 16:
            if whole is None:
                whole = lax.all_gather(joined[0], BOTH, axis=0, tiled=True)
            rows = whole.reshape(2, 2, 2, 2, 2, 48, sum(widths))
            at = {Y: 0, HIGH: 1, LOW: 2, X: 3}
            self.rows = tuple(
                tuple(self.split(rows.transpose(4, *(at[bit] for bit in order), 5, 6).reshape(4, 8, 48, -1))[kind])
                for kind, order in enumerate(orders)
            )
            self.phases = ()

    def split(self, values):
        return values[..., : self.widths[0]], values[..., self.widths[0] :]

    def send(self):
        if not self.phases:
            return
        if self.phases[0] in (HIGH, LOW):
            if self.joined is None:
                self.joined = jnp.concatenate(self.parts, axis=-1)
            self.arrived = swap(self.joined, self.phases[0])
            return
        first, second = self.parts
        if self.phases[0] == X:
            self.arrived = swap(first, X), swap(second, Y)
        elif self.phases[0] == Y:
            self.arrived = swap(first, Y), swap(second, X)
        else:
            self.arrived = tuple(tuple(swap(part, CORE) for part in rows) for rows in self.rows)

    def add(self):
        joined = None
        if self.phases[0] == HIGH:
            joined = jnp.concatenate([self.joined, self.arrived], axis=0)
        elif self.phases[0] == LOW:
            pieces = self.split(self.joined), self.split(self.arrived)
            self.parts = tuple(jnp.concatenate([piece[kind] for piece in pieces], axis=0) for kind in range(2))
        elif self.phases[0] == X:
            self.parts = tuple(jnp.concatenate(pair, axis=0) for pair in zip(self.parts, self.arrived))
        elif self.phases[0] == Y:
            self.rows = tuple(zip(self.parts, self.arrived))
        else:
            self.rows = tuple(near + far for near, far in zip(self.rows, self.arrived))
        self.joined, self.arrived = joined, None
        self.phases = self.phases[1:]


def seal(values, movers, swaps=()):
    flying = [mover for mover in movers if mover.arrived is not None]
    values, arrived, swaps = lax.optimization_barrier(
        (tuple(values), tuple(mover.arrived for mover in flying), tuple(swaps))
    )
    for mover, data in zip(flying, arrived):
        mover.arrived = data
        mover.add()
    for mover in movers:
        mover.send()
    return values, swaps


def on_device(
    short_images, short_texts, short_lengths, short_cotangent,
    long_images, long_texts, long_lengths, long_cotangent,
    img_weight, img_bias, text_weight, text_bias, cls_token, attn_gain, attn_shift,
    query_weight, query_bias, key_weight, value_weight, value_bias, out_weight, out_bias,
    mlp_gain, mlp_shift, up_weight, up_bias, down_weight, down_bias,
):
    half = lax.axis_index(TP)
    short = half == 1
    part = img_weight.shape[0]
    devices = 768 // part
    grouped = lax.axis_size(DP) == 16

    vectors = [img_bias, text_bias, cls_token, attn_gain, attn_shift, query_bias, value_bias, out_bias,
               mlp_gain, mlp_shift, down_bias]
    if grouped:
        small = jnp.concatenate([jnp.stack(vectors), up_bias.reshape(4, 24), jnp.zeros((1, 24), BF)])
        shard = pack(query_weight, key_weight, value_weight, img_weight, text_weight, out_weight.T, small)
        towers = None
    else:
        every = lambda v: lax.all_gather(v, (DP, TP), axis=0, tiled=True)
        towers = every(jnp.concatenate([img_weight, text_weight], axis=1))
        towers = towers.reshape(16, 2, 24, 2, 768).transpose(1, 0, 3, 2, 4).reshape(2, 768, 768)
        columns = jnp.stack([every(v) for v in vectors]).reshape(11, 32, 24).transpose(1, 2, 0)
        columns = jnp.concatenate([columns, every(up_bias).reshape(32, 4, 24).transpose(0, 2, 1)], axis=2)
        columns = jnp.pad(columns, ((0, 0), (0, 24), (0, 113)))
        columns = columns.reshape(16, 2, 48, 128).transpose(1, 0, 2, 3).reshape(2, 768, 128)
        outs = lax.all_gather(out_weight.T, BOTH, axis=0, tiled=True).reshape(2, 768, 384)
        towers = jnp.concatenate([towers, outs, columns], axis=2)
        qkv = jnp.concatenate([query_weight, key_weight, value_weight], axis=1)
        towers = jnp.concatenate([lax.all_gather(qkv, BOTH, axis=0, tiled=True).reshape(2, 768, 1152), towers], axis=2)
        shard = None
    joined = None if grouped else jnp.concatenate([up_weight, down_weight.T], axis=1)[None]
    first_gather = Gather(shard, (1152, 1280), (HIGH, LOW, X, Y, CORE), (GATHER_QKV, GATHER_TOWER), towers)
    wide_gather = Gather(joined, (1536, 1536), (X, HIGH, LOW, Y, CORE), (GATHER_UP, GATHER_DOWN))
    wide_gather.parts = up_weight[None], down_weight.T[None]
    near, wide = [first_gather], [wide_gather]
    first_gather.send()
    wide_gather.send()
    seal((), near + wide)
    seal((), near)
    seal((), near + wide)

    zero = jnp.zeros((4, 1, 768), BF)
    short_rows = jnp.concatenate([zero, short_images, short_texts], axis=1).reshape(ROWS, 768)
    long_rows = jnp.concatenate([zero[0, 0:1], long_images[0], long_texts[0], jnp.zeros((ROWS - 710, 768), BF)], axis=0)
    x = jnp.where(short, short_rows, long_rows)
    cot = jnp.where(
        short,
        short_cotangent.reshape(ROWS, 768),
        jnp.concatenate([long_cotangent[0], jnp.zeros((ROWS - 710, 768), BF)], axis=0),
    )
    place = lax.axis_index(DP) if grouped else jnp.int32(0)
    half_place = half.astype(jnp.int32) if grouped else jnp.int32(0)
    limits = 198 + jnp.where(short, short_lengths, jnp.broadcast_to(long_lengths, (4,)))
    meta = jnp.concatenate(
        [
            half.astype(jnp.int32)[None],
            limits.astype(jnp.int32),
            half_place[None],
            place.astype(jnp.int32)[None],
            jnp.zeros((1,), jnp.int32),
        ]
    )

    x_t, cot_t, cot_sum = prepare(x, cot)
    (x, cot, x_t, cot_t, meta), _ = seal((x, cot, x_t, cot_t, meta), near)
    seal((), near)
    (x,), _ = seal((x,), near + wide)
    stream, n1_t, qkv0, qkv1, wimg, wtext, wqkv, wout, smalls, up_bias_all = embed(
        meta, x, *first_gather.rows
    )
    att1, lse1 = attn_forward(meta, qkv1)
    (att1, qkv0), _ = seal((att1, qkv0), wide)
    att0, lse0 = attn_forward(meta, qkv0)
    mid, n2, n2_t = mid_stage(meta, (att0, att1), stream, wout, smalls)
    (n2,), _ = seal((n2,), wide)
    weights = (*wide_gather.rows, up_bias_all)
    mlp1, gn1, *rest = mlp_half(meta, 1, n2, n2_t, cot, cot_t, *weights)
    ff_other, grad_up_bias1 = Half(rest[0:2], 1), rest[2]
    ff_other.send()
    mlp0, gn0, *rest = mlp_half(meta, 0, after(n2, mlp1), n2_t, cot, cot_t, *weights)
    (mlp0, *rest), _ = seal((mlp0, *rest), [ff_other])
    ff_own, grad_up_bias0 = Half(rest[0:2], 0), rest[2]
    ff_own.send()
    ff = Cross(ff_own, ff_other)
    out, grad_mid, gatt0, gatt1, *rest = back_mid(
        meta, (mlp0, gn0, mlp1, gn1), mid, cot, (att0, att1), wout, smalls
    )
    gout0, gout1, sums_two = rest[0:2], rest[2:4], rest[4]
    (out, gatt0, gatt1), _ = seal((out, gatt0, gatt1), [ff_own])
    out_other = swap(out, Y)
    dqkv1 = attn_back(meta, qkv1, gatt1, lse1)
    (*rest, gatt0), _ = seal((*proj_grad(meta, 1, n1_t, dqkv1, gout1), gatt0), [ff_other])
    proj_other = Half(rest, 1)
    proj_other.send()
    dqkv0 = attn_back(meta, qkv0, gatt0, lse0)
    (dqkv0,), _ = seal((dqkv0,), [ff_own])
    rest = proj_grad(meta, 0, n1_t, dqkv0, gout0)
    (dqkv0, *rest), (out_other,) = seal((dqkv0, *rest), [ff_other], (out_other,))
    proj_own = Half(rest, 0)
    proj_own.send()
    ff = Cross(ff_own, ff_other)
    ff.send()
    low, sums_one, qkv_sums = back_in(meta, (dqkv0, dqkv1), stream, grad_mid, wqkv, smalls)
    (low, x_t), _ = seal((low, x_t), [ff_own, proj_own, proj_other])
    low_other = swap(low, Y)
    towers = tower_grad(meta, x_t, low, sums_one, sums_two, qkv_sums, cot_sum, grad_up_bias0, grad_up_bias1)
    (*towers, low, out, out_other), _ = seal((*towers, low, out, out_other), [])
    tower = Scatter(towers, TOWERS)
    tower.send()
    proj = Cross(proj_own, proj_other)
    short_output = jnp.where(short, out, out_other).reshape(4, 256, 768)
    long_output = jnp.where(short, out_other, out)[None, 0:710]
    (short_output, long_output, low), _ = seal((short_output, long_output, low), [tower])
    mine = input_grad(meta, True, low, wimg, wtext)
    mine, _ = seal(mine, [ff, proj_other])
    seal((), [proj_own, proj_other, tower])
    proj.send()
    _, (low_other,) = seal((), [proj_own, ff, proj], (low_other,))
    (low_other,), _ = seal((low_other,), [tower])
    theirs = input_grad(meta, False, low_other, wimg, wtext)
    si, st = (jnp.where(short, mine[k], theirs[k]) for k in (0, 1))
    li, lt = (jnp.where(short, theirs[k], mine[k]) for k in (2, 3))
    (si, st, li, lt), _ = seal((si, st, li, lt), [proj, tower])
    si, st, li, lt = si.transpose(1, 0, 2), st.transpose(1, 0, 2), li.transpose(1, 0, 2), lt[None]
    seal((), [tower])
    red_ff, red_proj = ff.total, proj.total
    if grouped:
        red_tower = tower.total
        red_img, red_text = red_tower[0:24, 0:768], red_tower[24:48, 0:768]
        red_vectors = [red_tower[0:24, 768 + k] for k in range(11)]
        device = 2 * lax.axis_index(DP) + lax.axis_index(TP)
        red_up_bias = lax.dynamic_slice(red_tower, (0, 779 + device // 8), (24, 4))
        red_vectors.append(red_up_bias.T.reshape(96))
    else:
        mats = jnp.stack([absolute([part_[:, half_, :, 0:768] for part_ in towers], TOWERS[0:3]) for half_ in range(2)])
        mats = mats.reshape(2, 16, 2, 24, 768).transpose(2, 1, 0, 3, 4).reshape(2, 768, 768)
        red_img = lax.psum_scatter(mats[0], (DP, TP), scatter_dimension=0, tiled=True)
        red_text = lax.psum_scatter(mats[1], (DP, TP), scatter_dimension=0, tiled=True)
        sums = [*sums_one[0:5], qkv_sums[:, 0:384].reshape(768), qkv_sums[:, 768:1152].reshape(768),
                *sums_two[0:3], cot_sum[0], jnp.concatenate([grad_up_bias0, grad_up_bias1]).reshape(3072)]
        red_vectors = [lax.psum_scatter(v, (DP, TP), scatter_dimension=0, tiled=True) for v in sums]

    f = lambda v: v.astype(F32)
    vec = [f(v) for v in red_vectors]
    return (
        short_output, long_output, si, st, li, lt,
        f(red_img), vec[0], f(red_text), vec[1], vec[2], vec[3], vec[4],
        red_proj[:, 0:384], vec[5], red_proj[:, 384:768], red_proj[:, 768:1152], vec[6],
        red_proj[:, 1152:1536].T, vec[7], vec[8], vec[9],
        jnp.concatenate([red_ff[:, 0:768], red_ff[:, 1536:2304]], axis=1), vec[11],
        jnp.concatenate([red_ff[:, 768:1536], red_ff[:, 2304:3072]], axis=1).T, vec[10],
    )


def solution(mesh):
    rows = P(DP, None, None)
    vec = P((DP, TP))
    tower = P((DP, TP), None)
    col = P(DP, TP)
    back = P(TP, DP)
    return jax.shard_map(
        on_device,
        mesh=mesh,
        in_specs=(
            rows, rows, P(DP), rows, rows, rows, P(DP), rows,
            tower, vec, tower, vec, vec, vec, vec,
            col, vec, col, col, vec, back, vec, vec, vec, col, vec, back, vec,
        ),
        out_specs=(
            rows, rows, rows, rows, rows, rows,
            tower, vec, tower, vec, vec, vec, vec,
            col, vec, col, col, vec, back, vec, vec, vec, col, vec, back, vec,
        ),
        check_vma=False,
    )
```

```python
from functools import partial

import jax
import jax.numpy as jnp
from jax import lax
from jax.experimental import pallas as pl
from jax.experimental.pallas import tpu as pltpu
from jax.sharding import PartitionSpec as P

DP = "dp"
TP = "tensor"
BOTH = (TP, DP)
EPS = 1e-06
NEG = -1e30
BF = jnp.bfloat16
F32 = jnp.float32
ROWS = 1024
BLK = 256
MIB = 1 << 20


def dot_nn(left, right):
    return lax.dot_general(left, right, (((1,), (0,)), ((), ())), preferred_element_type=F32)


def dot_nt(left, right):
    return lax.dot_general(left, right, (((1,), (1,)), ((), ())), preferred_element_type=F32)


def flip(values):
    return values.astype(F32).T.astype(BF)


def cost(micros):
    return pl.CostEstimate(flops=int(micros * 2e8), bytes_accessed=int(micros * 1e5), transcendentals=0)


def params(limit=56):
    return pltpu.CompilerParams(dimension_semantics=("arbitrary",), vmem_limit_bytes=limit * MIB)


def whole(*shape):
    return pl.BlockSpec(shape, lambda *_: (0,) * len(shape), pipeline_mode=pl.Buffered(1))


def norm_parts(values):
    row_mean = jnp.mean(values, axis=-1, keepdims=True)
    centred = values - row_mean
    row_var = jnp.mean(centred * centred, axis=-1, keepdims=True)
    inverse = lax.rsqrt(row_var + EPS)
    return centred * inverse, inverse


def norm_back(xhat, inverse, scaled):
    first = jnp.mean(scaled, axis=-1, keepdims=True)
    second = jnp.mean(scaled * xhat, axis=-1, keepdims=True)
    return (scaled - first - xhat * second) * inverse


def is_short(meta):
    return meta[0] == 1


def active(meta, step):
    return jnp.logical_or(is_short(meta), step < 3)


CORE, X, LOW, HIGH, Y = 1, 2, 4, 8, 16
HALVES = ((LOW, X, HIGH), (X, LOW, HIGH))
TOWERS = (X, LOW, HIGH, Y)
GATHER_QKV = (Y, X, LOW, HIGH)
GATHER_TOWER = (X, Y, LOW, HIGH)
GATHER_UP = (Y, LOW, HIGH, X)
GATHER_DOWN = (X, LOW, HIGH, Y)


def relatives(meta, order):
    rest = [bit for bit in order if bit != Y]
    for core in range(2):
        for place in range(8):
            offset = core * CORE + sum(bit * (place >> (2 - k) & 1) for k, bit in enumerate(rest))
            yield core, place, jnp.bitwise_xor(meta[6], offset)


def places(meta, order):
    for core in range(2):
        for place in range(16):
            offset = core * CORE + sum(bit * (place >> (3 - k) & 1) for k, bit in enumerate(order))
            other = offset // 16
            yield core, place, jnp.bitwise_xor(meta[6], offset % 16), other, jnp.bitwise_xor(meta[5], other)


def hold_pieces(held, result):
    for group in range(16):
        held[group] = result[group * 48 : (group + 1) * 48].astype(BF)


def halves_shapes(width):
    return [jax.ShapeDtypeStruct((8, 48, width), BF)] * 2


def pack_kernel(q_ref, k_ref, v_ref, img_ref, text_ref, out_ref, small_ref, packed_ref):
    packed_ref[0, :, 0:384] = q_ref[...]
    packed_ref[0, :, 384:768] = k_ref[...]
    packed_ref[0, :, 768:1152] = v_ref[...]
    tower = jnp.concatenate([img_ref[...].astype(F32), text_ref[...].astype(F32)], axis=0)
    packed_ref[0, :, 1152:1920] = tower.astype(BF)
    packed_ref[0, :, 1920:2304] = out_ref[...]
    small = jnp.concatenate([small_ref[...].astype(F32), jnp.zeros((112, 24), F32)], axis=0).T
    packed_ref[0, :, 2304:2432] = jnp.concatenate([small, jnp.zeros((24, 128), F32)], axis=0).astype(BF)


def pack(*args):
    return pl.pallas_call(
        pack_kernel,
        grid=(1,),
        in_specs=[whole(*arg.shape) for arg in args],
        out_specs=whole(1, 48, 2432),
        out_shape=jax.ShapeDtypeStruct((1, 48, 2432), BF),
        compiler_params=params(60),
        name="pack",
        cost_estimate=cost(2),
    )(*args)


def prepare_kernel(x_ref, cot_ref, xt_ref, cott_ref, sum_ref):
    xt_ref[...] = flip(x_ref[...])
    cott_ref[...] = flip(cot_ref[...])

    @pl.when(pl.program_id(0) == 0)
    def _():
        sum_ref[...] = jnp.zeros_like(sum_ref)

    sum_ref[...] += jnp.sum(cot_ref[...].astype(F32), axis=0, keepdims=True)


def prepare(x, cot):
    row = pl.BlockSpec((BLK, 768), lambda i: (i, 0))
    column = pl.BlockSpec((768, BLK), lambda i: (0, i))
    return pl.pallas_call(
        prepare_kernel,
        grid=(4,),
        in_specs=[row, row],
        out_specs=[column, column, whole(1, 768)],
        out_shape=[
            jax.ShapeDtypeStruct((768, ROWS), BF),
            jax.ShapeDtypeStruct((768, ROWS), BF),
            jax.ShapeDtypeStruct((1, 768), F32),
        ],
        compiler_params=params(5),
        name="prepare",
        cost_estimate=cost(0.1),
    )(x, cot)


def embed_kernel(
    meta, x_ref, qkv_00, qkv_01, qkv_10, qkv_11, tower_00, tower_01, tower_10, tower_11,
    stream_ref, n1t_ref, qkv0_ref, qkv1_ref, wimg_ref, wtext_ref, wqkv_ref, wout_ref, sm_ref, bias_ref,
    wimg_f, wtext_f, wout_pieces, columns, up_columns,
):
    step = pl.program_id(0)
    qkv = (qkv_00, qkv_01), (qkv_10, qkv_11)
    towers = (tower_00, tower_01), (tower_10, tower_11)

    @pl.when(step == 0)
    def _():
        for core, place, group, other, _ in places(meta, GATHER_QKV):
            wqkv_ref[other, group] = qkv[core][place // 8][place % 8]
        for core, place, group, other, half in places(meta, GATHER_TOWER):
            tower = towers[core][place // 8].at[place % 8]
            piece = tower[:, 0:768].astype(F32)
            rows = pl.ds(pl.multiple_of(24 * (2 * group + half), 8), 24)
            wimg_f[rows, :] = piece[0:24]
            wtext_f[rows, :] = piece[24:48]
            wout_pieces[other, group] = tower[:, 768:1152]
            device = 2 * group + half
            small = tower[0:32, 1152:1280].astype(F32)[0:24]
            columns[rows, :] = small
            for part in range(4):
                start = pl.multiple_of(96 * device + 24 * part, 8)
                up_columns[pl.ds(start, 24), :] = pltpu.roll(small, 128 - 11 - part, 1)
        wimg_ref[...] = wimg_f[...].astype(BF)
        wtext_ref[...] = wtext_f[...].astype(BF)
        for half in range(2):
            wout_ref[:, 384 * half : 384 * half + 384] = wout_pieces[half].reshape(768, 384)
        sm_ref[...] = columns[...].T[0:16]
        for chunk in range(4):
            bias_ref[chunk] = up_columns[768 * chunk : 768 * chunk + 768, :].T[0:1]

    @pl.when(active(meta, step))
    def _():
        with_image = jnp.logical_or(is_short(meta), step == 0)

        @pl.when(with_image)
        def _():
            first = dot_nn(x_ref[0:208, :], wimg_ref[...]) + sm_ref[0:1, :]
            second = dot_nn(x_ref[192:256, :], wtext_ref[...]) + sm_ref[1:2, :]
            index = lax.broadcasted_iota(jnp.int32, (16, 768), 0)
            stream_ref[0:192, :] = first[0:192]
            stream_ref[192:208, :] = jnp.where(index < 6, first[192:208], second[0:16])
            stream_ref[208:256, :] = second[16:64]
            stream_ref[0:1, :] = sm_ref[2:3, :]

        @pl.when(jnp.logical_not(with_image))
        def _():
            stream_ref[...] = dot_nn(x_ref[...], wtext_ref[...]) + sm_ref[1:2, :]

        xhat, _ = norm_parts(stream_ref[...])
        scaled = xhat * sm_ref[3:4, :] + sm_ref[4:5, :]
        normed = scaled.astype(BF)
        n1t_ref[...] = flip(normed)
        for half, qkv_ref in enumerate((qkv0_ref, qkv1_ref)):
            out = dot_nn(normed, wqkv_ref[half].reshape(768, 1152))
            lanes = pl.ds(pl.multiple_of(384 * jnp.bitwise_xor(meta[5], half), 128), 384)
            qkv_ref[:, 0:384] = (out[:, 0:384] + sm_ref[5:6, lanes]).astype(BF)
            qkv_ref[:, 384:768] = out[:, 384:768].astype(BF)
            qkv_ref[:, 768:1152] = (out[:, 768:1152] + sm_ref[6:7, lanes]).astype(BF)


def embed(meta, x, qkv_all, tower_all):
    row = lambda width: pl.BlockSpec((BLK, width), lambda i, m: (i, 0))
    return pl.pallas_call(
        embed_kernel,
        grid_spec=pltpu.PrefetchScalarGridSpec(
            num_scalar_prefetch=1,
            grid=(4,),
            in_specs=[row(768)] + [whole(8, 48, 1152)] * 4 + [whole(8, 48, 1280)] * 4,
            out_specs=[
                row(768),
                pl.BlockSpec((768, BLK), lambda i, m: (0, i)),
                row(1152),
                row(1152),
                whole(768, 768),
                whole(768, 768),
                whole(2, 16, 48, 1152),
                whole(768, 768),
                whole(16, 768),
                whole(4, 1, 768),
            ],
            scratch_shapes=[
                pltpu.VMEM((768, 768), F32),
                pltpu.VMEM((768, 768), F32),
                pltpu.VMEM((2, 16, 48, 384), BF),
                pltpu.VMEM((768, 128), F32),
                pltpu.VMEM((3072, 128), F32),
            ],
        ),
        out_shape=[
            jax.ShapeDtypeStruct((ROWS, 768), F32),
            jax.ShapeDtypeStruct((768, ROWS), BF),
            jax.ShapeDtypeStruct((ROWS, 1152), BF),
            jax.ShapeDtypeStruct((ROWS, 1152), BF),
            jax.ShapeDtypeStruct((768, 768), BF),
            jax.ShapeDtypeStruct((768, 768), BF),
            jax.ShapeDtypeStruct((2, 16, 48, 1152), BF),
            jax.ShapeDtypeStruct((768, 768), BF),
            jax.ShapeDtypeStruct((16, 768), F32),
            jax.ShapeDtypeStruct((4, 1, 768), F32),
        ],
        compiler_params=params(24),
        name="embed",
        cost_estimate=cost(12),
    )(meta, x, *qkv_all, *tower_all)


def head_lanes(values, head):
    lane = lax.broadcasted_iota(jnp.int32, values.shape, 1)
    keep = lane < 64 if head == 0 else lane >= 64
    return jnp.where(keep, values, jnp.zeros_like(values))


def attn_forward_part(q, k, v, limit):
    out, lse = None, []
    for head in range(2):
        scores = dot_nt(head_lanes(q, head), k)
        index = lax.broadcasted_iota(jnp.int32, scores.shape, 1)
        scores = jnp.where(index < limit, scores, NEG)
        top = jnp.max(scores, axis=1, keepdims=True)
        weight = jnp.exp(scores - top)
        total = jnp.sum(weight, axis=1, keepdims=True)
        add = dot_nn(weight.astype(BF), head_lanes(v, head)) * (1.0 / total)
        out = add if out is None else out + add
        lse.append(jnp.broadcast_to(top + jnp.log(total), (256, 128)).T[0:1])
    return out.astype(BF), jnp.concatenate(lse, axis=0)


def attn_forward_kernel(meta, qkv_ref, out_ref, lse_ref):
    pair = pl.program_id(0)

    def part(kind, start, size):
        lanes = pl.ds(pl.multiple_of(384 * kind + 128 * pair, 128), 128)
        return qkv_ref[start : start + size, lanes]

    @pl.when(is_short(meta))
    def _():
        for member in range(4):
            start = 256 * member
            q = part(0, start, 256) * BF(0.125)
            out, lse = attn_forward_part(
                q, part(1, start, 256), part(2, start, 256), meta[1 + member]
            )
            out_ref[start : start + 256, :] = out
            lse_ref[0, :, start : start + 256] = lse

    @pl.when(jnp.logical_not(is_short(meta)))
    def _():
        k = part(1, 0, 768)
        v = part(2, 0, 768)
        for member in range(3):
            start = 256 * member
            q = part(0, start, 256) * BF(0.125)
            out, lse = attn_forward_part(q, k, v, meta[1])
            out_ref[start : start + 256, :] = out
            lse_ref[0, :, start : start + 256] = lse


def attn_forward(meta, qkv):
    return pl.pallas_call(
        attn_forward_kernel,
        grid_spec=pltpu.PrefetchScalarGridSpec(
            num_scalar_prefetch=1,
            grid=(3,),
            in_specs=[whole(ROWS, 1152)],
            out_specs=[
                pl.BlockSpec((ROWS, 128), lambda j, m: (0, j)),
                pl.BlockSpec((1, 2, ROWS), lambda j, m: (j, 0, 0)),
            ],
        ),
        out_shape=[
            jax.ShapeDtypeStruct((ROWS, 384), BF),
            jax.ShapeDtypeStruct((3, 2, ROWS), F32),
        ],
        compiler_params=params(6),
        name="attn_forward",
        cost_estimate=cost(14),
    )(meta, qkv)


def attn_back_part(q, k, v, grad, lse, limit):
    grad_k, grad_v, grad_q = None, None, None
    for head in range(2):
        q_head = head_lanes(q, head)
        g_head = head_lanes(grad, head)
        scores = dot_nt(k, q_head)
        index = lax.broadcasted_iota(jnp.int32, scores.shape, 0)
        probs = jnp.exp(scores - lse[head : head + 1])
        probs = jnp.where(index < limit, probs, 0.0)
        grad_probs = dot_nt(v, g_head)
        row_dot = jnp.sum(probs * grad_probs, axis=0, keepdims=True)
        grad_scores = (probs * (grad_probs - row_dot)).astype(BF)
        add_v = dot_nn(probs.astype(BF), g_head)
        add_k = dot_nn(grad_scores, q_head)
        grad_v = add_v if grad_v is None else grad_v + add_v
        grad_k = add_k if grad_k is None else grad_k + add_k
        add_q = lax.dot_general(
            grad_scores, head_lanes(k, head), (((0,), (0,)), ((), ())), preferred_element_type=F32
        )
        grad_q = add_q if grad_q is None else grad_q + add_q
    return (grad_q * 0.125).astype(BF), grad_k, grad_v


def attn_back_kernel(meta, qkv_ref, grad_ref, lse_ref, out_ref, acc_k, acc_v):
    pair = pl.program_id(0)

    def lanes(kind):
        return pl.ds(pl.multiple_of(384 * kind + 128 * pair, 128), 128)

    def part(kind, start, size):
        return qkv_ref[start : start + size, lanes(kind)]

    @pl.when(is_short(meta))
    def _():
        for member in range(4):
            rows = slice(256 * member, 256 * member + 256)
            start = 256 * member
            q = part(0, start, 256) * BF(0.125)
            k = part(1, start, 256)
            grad_q, grad_k, grad_v = attn_back_part(
                q, k, part(2, start, 256), grad_ref[rows, :], lse_ref[0, :, rows], meta[1 + member]
            )
            out_ref[rows, lanes(0)] = grad_q
            out_ref[rows, lanes(1)] = grad_k.astype(BF)
            out_ref[rows, lanes(2)] = grad_v.astype(BF)

    @pl.when(jnp.logical_not(is_short(meta)))
    def _():
        k = part(1, 0, 768)
        v = part(2, 0, 768)
        for member in range(3):
            rows = slice(256 * member, 256 * member + 256)
            start = 256 * member
            q = part(0, start, 256) * BF(0.125)
            grad_q, grad_k, grad_v = attn_back_part(
                q, k, v, grad_ref[rows, :], lse_ref[0, :, rows], meta[1]
            )
            out_ref[rows, lanes(0)] = grad_q
            if member == 0:
                acc_k[...] = grad_k
                acc_v[...] = grad_v
            else:
                acc_k[...] += grad_k
                acc_v[...] += grad_v
        out_ref[0:768, lanes(1)] = acc_k[...].astype(BF)
        out_ref[0:768, lanes(2)] = acc_v[...].astype(BF)


def attn_back(meta, qkv, grad, lse):
    return pl.pallas_call(
        attn_back_kernel,
        grid_spec=pltpu.PrefetchScalarGridSpec(
            num_scalar_prefetch=1,
            grid=(3,),
            in_specs=[
                whole(ROWS, 1152),
                pl.BlockSpec((ROWS, 128), lambda j, m: (0, j)),
                pl.BlockSpec((1, 2, ROWS), lambda j, m: (j, 0, 0)),
            ],
            out_specs=whole(ROWS, 1152),
            scratch_shapes=[pltpu.VMEM((768, 128), F32), pltpu.VMEM((768, 128), F32)],
        ),
        out_shape=jax.ShapeDtypeStruct((ROWS, 1152), BF),
        compiler_params=params(8),
        name="attn_back",
        cost_estimate=cost(0.1),
    )(meta, qkv, grad, lse)


def mid_kernel(meta, att0_ref, att1_ref, stream_ref, wout_ref, sm_ref, mid_ref, n2_ref, n2t_ref):
    @pl.when(active(meta, pl.program_id(0)))
    def _():
        attended = jnp.concatenate([att0_ref[...], att1_ref[...]], axis=1)
        mid = stream_ref[...] + dot_nt(attended, wout_ref[...]) + sm_ref[7:8, :]
        mid_ref[...] = mid
        xhat, _ = norm_parts(mid)
        normed = (xhat * sm_ref[8:9, :] + sm_ref[9:10, :]).astype(BF)
        n2_ref[...] = normed
        n2t_ref[...] = flip(normed)

    @pl.when(jnp.logical_not(active(meta, pl.program_id(0))))
    def _():
        n2t_ref[...] = jnp.zeros_like(n2t_ref)


def mid_stage(meta, attended, stream, wout, smalls):
    row = lambda width: pl.BlockSpec((BLK, width), lambda i, m: (i, 0))
    return pl.pallas_call(
        mid_kernel,
        grid_spec=pltpu.PrefetchScalarGridSpec(
            num_scalar_prefetch=1,
            grid=(4,),
            in_specs=[
                row(384),
                row(384),
                row(768),
                whole(768, 768),
                whole(16, 768),
            ],
            out_specs=[row(768), row(768), pl.BlockSpec((768, BLK), lambda i, m: (0, i))],
        ),
        out_shape=[
            jax.ShapeDtypeStruct((ROWS, 768), F32),
            jax.ShapeDtypeStruct((ROWS, 768), BF),
            jax.ShapeDtypeStruct((768, ROWS), BF),
        ],
        compiler_params=params(6),
        name="mid_stage",
        cost_estimate=cost(7),
    )(meta, *attended, stream, wout, smalls)


INV_ROOT2 = 0.7071067811865476
INV_ROOT2PI = 0.3989422804014327


def mlp_kernel(
    other,
    meta, n2_ref, n2_t, cot_ref, cot_t, up_near, up_far, down_00, down_01, down_10, down_11, bias_ref,
    out_ref, gn_ref, keep_ref, send_ref, gbias_ref,
    wup_pieces, wdown_pieces, hid, gpre, out_sum, gn_sum,
):
    step = pl.program_id(0)
    down = (down_00, down_01), (down_10, down_11)
    for core, place, group, half, _ in places(meta, GATHER_UP):
        if half == other:
            wup_pieces[group] = (up_near, up_far)[core][place % 8]
    for core, place, group, half, _ in places(meta, GATHER_DOWN):
        if half == other:
            wdown_pieces[group] = down[core][place // 8][place % 8 // 2, 0]
    bias = bias_ref[0]

    gbias_ref[...] = jnp.zeros_like(gbias_ref)

    @pl.loop(0, jnp.where(is_short(meta), 4, 3))
    def _(block):
        wup = wup_pieces[...].reshape(768, 768)
        wdown = wdown_pieces[...].reshape(768, 768)
        rows = pl.ds(pl.multiple_of(256 * block, 256), 256)
        pre = dot_nn(n2_ref[rows, :], wup) + bias
        cdf = 0.5 + 0.5 * lax.erf(pre * INV_ROOT2)
        hidden = (pre * cdf).astype(BF)
        hid[rows, :] = hidden
        slope = cdf + pre * (jnp.exp(pre * pre * -0.5) * INV_ROOT2PI)
        grad_pre = (dot_nn(cot_ref[rows, :], wdown) * slope).astype(BF)
        gpre[rows, :] = grad_pre
        gbias_ref[0] += jnp.sum(grad_pre.astype(F32), axis=0, keepdims=True)
        out_add = dot_nt(hidden, wdown)
        gn_add = dot_nt(grad_pre, wup)

        @pl.when(step == 0)
        def _():
            out_sum[rows, :] = out_add
            gn_sum[rows, :] = gn_add

        @pl.when(step > 0)
        def _():
            out_ref[rows, :] = (out_sum[rows, :] + out_add).astype(BF)
            gn_ref[rows, :] = (gn_sum[rows, :] + gn_add).astype(BF)

    @pl.when(jnp.logical_and(jnp.logical_not(is_short(meta)), step == 0))
    def _():
        hid[768:1024, :] = jnp.zeros((256, 768), BF)
        gpre[768:1024, :] = jnp.zeros((256, 768), BF)

    held = wup_pieces
    for kind, left, right in ((0, n2_t, gpre), (1, cot_t, hid)):
        hold_pieces(held, dot_nn(left[...], right[...]))
        lanes = slice(768 * kind, 768 * kind + 768)
        for core, place, group in relatives(meta, HALVES[other]):
            (keep_ref, send_ref)[core][place, :, lanes] = held[group]


def mlp_half(meta, other, n2, n2_t, cot, cot_t, up_all, down_all, up_bias):
    rows, turned = whole(ROWS, 768), whole(768, ROWS)
    bias = pl.BlockSpec((1, 1, 768), lambda c, m: (2 * jnp.bitwise_xor(other, m[5]) + c, 0, 0))
    return pl.pallas_call(
        partial(mlp_kernel, other),
        grid_spec=pltpu.PrefetchScalarGridSpec(
            num_scalar_prefetch=1,
            grid=(2,),
            in_specs=[
                rows,
                turned,
                rows,
                turned,
                *[pl.BlockSpec((8, 48, 768), lambda c, m: (0, 0, c))] * 2,
                *[pl.BlockSpec((4, 1, 48, 768), lambda c, m: (0, other, 0, c))] * 4,
                bias,
            ],
            out_specs=[
                rows,
                rows,
                pl.BlockSpec((8, 48, 1536), lambda c, m: (0, 0, c)),
                pl.BlockSpec((8, 48, 1536), lambda c, m: (0, 0, c)),
                pl.BlockSpec((1, 1, 768), lambda c, m: (c, 0, 0)),
            ],
            scratch_shapes=[
                pltpu.VMEM((16, 48, 768), BF),
                pltpu.VMEM((16, 48, 768), BF),
                pltpu.VMEM((ROWS, 768), BF),
                pltpu.VMEM((ROWS, 768), BF),
                pltpu.VMEM((ROWS, 768), F32),
                pltpu.VMEM((ROWS, 768), F32),
            ],
        ),
        out_shape=[
            jax.ShapeDtypeStruct((ROWS, 768), BF),
            jax.ShapeDtypeStruct((ROWS, 768), BF),
            *halves_shapes(3072),
            jax.ShapeDtypeStruct((2, 1, 768), F32),
        ],
        compiler_params=params(26),
        name="mlp_half",
        cost_estimate=cost(0.1),
    )(
        meta, n2, n2_t, cot, cot_t,
        up_all[other], up_all[2 + other],
        *(part.reshape(4, 2, 48, 1536) for part in down_all),
        up_bias,
    )


def back_mid_kernel(
    meta, mlp0_ref, gn0_ref, mlp1_ref, gn1_ref, mid_ref, cot_ref, att0_ref, att1_ref, wout_ref, sm_ref,
    out_ref, gmid_ref, gatt0_ref, gatt1_ref, gout0_keep, gout0_send, gout1_keep, gout1_send, sums_ref,
    low_t, held,
):
    step = pl.program_id(0)

    @pl.when(step == 0)
    def _():
        sums_ref[...] = jnp.zeros_like(sums_ref)

    @pl.when(jnp.logical_and(active(meta, step), step < 4))
    def _():
        mid = mid_ref[...]
        out_ref[...] = (mid + (mlp0_ref[...].astype(F32) + mlp1_ref[...].astype(F32)) + sm_ref[10:11, :]).astype(BF)
        xhat, inverse = norm_parts(mid)
        grad = gn0_ref[...].astype(F32) + gn1_ref[...].astype(F32)
        cot = cot_ref[...].astype(F32)
        grad_mid = cot + norm_back(xhat, inverse, grad * sm_ref[8:9, :])
        gmid_ref[...] = grad_mid
        low = grad_mid.astype(BF)
        grad_att = dot_nn(low, wout_ref[...]).astype(BF)
        gatt0_ref[...] = grad_att[:, 0:384]
        gatt1_ref[...] = grad_att[:, 384:768]
        low_t[step] = flip(low)
        sums_ref[0:1, :] += jnp.sum(grad_mid, axis=0, keepdims=True)
        sums_ref[1:2, :] += jnp.sum(grad * xhat, axis=0, keepdims=True)
        sums_ref[2:3, :] += jnp.sum(grad, axis=0, keepdims=True)

    for half, att_ref in enumerate((att0_ref, att1_ref)):
        for count, chosen in ((4, is_short(meta)), (3, jnp.logical_not(is_short(meta)))):

            @pl.when(jnp.logical_and(chosen, step == 4 + half))
            def _(count=count, att_ref=att_ref, half=half):
                total = None
                for block in range(count):
                    add = dot_nn(low_t[block], att_ref[256 * block : 256 * block + 256, :])
                    total = add if total is None else total + add
                hold_pieces(held, total)
                gouts = ((gout0_keep, gout0_send), (gout1_keep, gout1_send))[half]
                for core, place, group in relatives(meta, HALVES[half]):
                    gouts[core][place] = held[group]


def back_mid(meta, mlp_sums, mid, cot, attended, wout, smalls):
    row = pl.BlockSpec((BLK, 768), lambda i, m: (jnp.minimum(i, 3), 0))
    thin = pl.BlockSpec((BLK, 384), lambda i, m: (jnp.minimum(i, 3), 0))
    return pl.pallas_call(
        back_mid_kernel,
        grid_spec=pltpu.PrefetchScalarGridSpec(
            num_scalar_prefetch=1,
            grid=(6,),
            in_specs=[
                row,
                row,
                row,
                row,
                row,
                row,
                whole(ROWS, 384),
                whole(ROWS, 384),
                whole(768, 768),
                whole(16, 768),
            ],
            out_specs=[
                row,
                row,
                thin,
                thin,
                *[whole(8, 48, 384)] * 4,
                whole(8, 768),
            ],
            scratch_shapes=[
                pltpu.VMEM((4, 768, 256), BF),
                pltpu.VMEM((16, 48, 384), BF),
            ],
        ),
        out_shape=[
            jax.ShapeDtypeStruct((ROWS, 768), BF),
            jax.ShapeDtypeStruct((ROWS, 768), F32),
            jax.ShapeDtypeStruct((ROWS, 384), BF),
            jax.ShapeDtypeStruct((ROWS, 384), BF),
            *halves_shapes(384),
            *halves_shapes(384),
            jax.ShapeDtypeStruct((8, 768), F32),
        ],
        compiler_params=params(10),
        name="back_mid",
        cost_estimate=cost(0.1),
    )(meta, *mlp_sums, mid, cot, *attended, wout, smalls)


def back_in_kernel(
    meta, dqkv0_ref, dqkv1_ref, stream_ref, gmid_ref, wqkv_ref, sm_ref, low_ref, sums_ref, qsum_ref
):
    step = pl.program_id(0)

    @pl.when(step == 0)
    def _():
        sums_ref[...] = jnp.zeros_like(sums_ref)
        qsum_ref[...] = jnp.zeros_like(qsum_ref)

    @pl.when(active(meta, step))
    def _():
        grad = None
        for half, dqkv_ref in enumerate((dqkv0_ref, dqkv1_ref)):
            dqkv = dqkv_ref[...]
            add = dot_nt(dqkv, wqkv_ref[half].reshape(768, 1152))
            grad = add if grad is None else grad + add
            qsum_ref[half : half + 1, :] += jnp.sum(dqkv.astype(F32), axis=0, keepdims=True)
        xhat, inverse = norm_parts(stream_ref[...])
        grad_in = gmid_ref[...] + norm_back(xhat, inverse, grad * sm_ref[3:4, :])
        low_ref[...] = grad_in.astype(BF)
        with_image = jnp.logical_or(is_short(meta), step == 0)
        limit = jnp.where(with_image, 198, 0)
        index = lax.broadcasted_iota(jnp.int32, (BLK, 768), 0)
        before = jnp.sum(jnp.where(index < limit, grad_in, 0.0), axis=0, keepdims=True)
        cls = jnp.where(with_image, grad_in[0:1], 0.0)
        everything = jnp.sum(grad_in, axis=0, keepdims=True)
        sums_ref[0:1, :] += before - cls
        sums_ref[1:2, :] += everything - before
        sums_ref[2:3, :] += cls
        sums_ref[3:4, :] += jnp.sum(grad * xhat, axis=0, keepdims=True)
        sums_ref[4:5, :] += jnp.sum(grad, axis=0, keepdims=True)


def back_in(meta, dqkv, stream, grad_mid, wqkv, smalls):
    row = lambda width: pl.BlockSpec((BLK, width), lambda i, m: (i, 0))
    return pl.pallas_call(
        back_in_kernel,
        grid_spec=pltpu.PrefetchScalarGridSpec(
            num_scalar_prefetch=1,
            grid=(4,),
            in_specs=[row(1152), row(1152), row(768), row(768), whole(2, 16, 48, 1152), whole(16, 768)],
            out_specs=[row(768), whole(8, 768), whole(2, 1152)],
        ),
        out_shape=[
            jax.ShapeDtypeStruct((ROWS, 768), BF),
            jax.ShapeDtypeStruct((8, 768), F32),
            jax.ShapeDtypeStruct((2, 1152), F32),
        ],
        compiler_params=params(10),
        name="back_in",
        cost_estimate=cost(0.1),
    )(meta, *dqkv, stream, grad_mid, wqkv, smalls)


def proj_grad_kernel(other, meta, n1t_ref, dqkv_ref, gout_keep, gout_send, keep_ref, send_ref, held):
    step = pl.program_id(0)
    for size, chosen in ((1024, is_short(meta)), (768, jnp.logical_not(is_short(meta)))):

        @pl.when(jnp.logical_and(chosen, step < 3))
        def _(size=size):
            hold_pieces(held, dot_nn(n1t_ref[:, 0:size], dqkv_ref[0:size, :]))
            for core, place, group in relatives(meta, HALVES[other]):
                (keep_ref, send_ref)[core][place] = held[group]

    @pl.when(step == 3)
    def _():
        keep_ref[...] = gout_keep[...]
        send_ref[...] = gout_send[...]


def proj_grad(meta, other, n1_t, dqkv, grad_out):
    columns = pl.BlockSpec((8, 48, 384), lambda c, m: (0, 0, c))
    return pl.pallas_call(
        partial(proj_grad_kernel, other),
        grid_spec=pltpu.PrefetchScalarGridSpec(
            num_scalar_prefetch=1,
            grid=(4,),
            in_specs=[
                whole(768, ROWS),
                pl.BlockSpec((ROWS, 384), lambda c, m: (0, jnp.minimum(c, 2))),
                whole(8, 48, 384),
                whole(8, 48, 384),
            ],
            out_specs=[columns, columns],
            scratch_shapes=[pltpu.VMEM((16, 48, 384), BF)],
        ),
        out_shape=halves_shapes(1536),
        compiler_params=params(8),
        name="proj_grad",
        cost_estimate=cost(0.1),
    )(meta, n1_t, dqkv, *grad_out)


def tower_grad_kernel(
    meta, x_t, low_ref, one_ref, two_ref, qkv_ref, down_ref, up0_ref, up1_ref,
    keep_ref, send_ref, gimg, gtext, wimg, wtext, vectors, columns,
):
    vectors[...] = jnp.zeros_like(vectors)
    vectors[0:5, :] = one_ref[0:5, :]
    for half in range(2):
        lanes = pl.ds(pl.multiple_of(384 * jnp.bitwise_xor(meta[5], half), 128), 384)
        vectors[5:6, lanes] = qkv_ref[half : half + 1, 0:384]
        vectors[6:7, lanes] = qkv_ref[half : half + 1, 768:1152]
    vectors[7:10, :] = two_ref[0:3, :]
    vectors[10:11, :] = down_ref[...]
    for half, up_ref in enumerate((up0_ref, up1_ref)):
        for chunk in range(2):
            vectors[pl.ds(11 + 2 * jnp.bitwise_xor(meta[5], half) + chunk, 1), :] = up_ref[chunk]
    columns[...] = vectors[...].T
    for block in range(4):
        rows = slice(256 * block, 256 * block + 256)
        with_image = jnp.logical_or(is_short(meta), block == 0)
        limit = jnp.where(with_image, 198, 0)
        index = lax.broadcasted_iota(jnp.int32, (BLK, 768), 0)
        low = low_ref[rows, :].astype(F32)
        gimg[rows, :] = jnp.where(index < limit, low, 0.0).astype(BF)
        gtext[rows, :] = jnp.where(index < limit, 0.0, low).astype(BF)

    for size, chosen in ((1024, is_short(meta)), (768, jnp.logical_not(is_short(meta)))):

        @pl.when(chosen)
        def _(size=size):
            wtext[...] = dot_nn(x_t[:, 0:size], gtext[0:size, :])
            image_size = size if size == 1024 else 256
            wimg[...] = dot_nn(x_t[:, 0:image_size], gimg[0:image_size, :])

    lane = lax.broadcasted_iota(jnp.int32, (24, 128), 1)
    for core, place, group in relatives(meta, TOWERS):
        ref = (keep_ref, send_ref)[core]
        for half in range(2):
            device = 2 * group + jnp.bitwise_xor(meta[5], half)
            rows = pl.ds(pl.multiple_of(24 * device, 8), 24)
            piece = jnp.concatenate([wimg[rows, :], wtext[rows, :]], axis=0).astype(BF)
            ref[place, half, :, 0:768] = piece
            small = jnp.where(lane < 11, columns[rows, :], 0.0)
            for part in range(4):
                start = 96 * jnp.bitwise_and(device, 7) + 24 * part
                some = columns[pl.ds(pl.multiple_of(start, 8), 24), :]
                some = jnp.where(lane == 11 + lax.shift_right_logical(device, 3), some, 0.0)
                small += some if part == 0 else pltpu.roll(some, part, 1)
            ref[place, half, :, 768:896] = jnp.concatenate([small, jnp.zeros_like(small)], axis=0).astype(BF)


def tower_grad(meta, x_t, low, *sums):
    return pl.pallas_call(
        tower_grad_kernel,
        grid_spec=pltpu.PrefetchScalarGridSpec(
            num_scalar_prefetch=1,
            grid=(1,),
            in_specs=[
                whole(768, ROWS),
                whole(ROWS, 768),
                whole(8, 768),
                whole(8, 768),
                whole(2, 1152),
                whole(1, 768),
                whole(2, 1, 768),
                whole(2, 1, 768),
            ],
            out_specs=[whole(8, 2, 48, 896)] * 2,
            scratch_shapes=[
                pltpu.VMEM((ROWS, 768), BF),
                pltpu.VMEM((ROWS, 768), BF),
                pltpu.VMEM((768, 768), F32),
                pltpu.VMEM((768, 768), F32),
                pltpu.VMEM((128, 768), F32),
                pltpu.VMEM((768, 128), F32),
            ],
        ),
        out_shape=[jax.ShapeDtypeStruct((8, 2, 48, 896), BF)] * 2,
        compiler_params=params(11),
        name="tower_grad",
        cost_estimate=cost(0.1),
    )(meta, x_t, low, *sums)


def input_grad_kernel(own, meta, rows_ref, wimg_ref, wtext_ref, si_ref, st_ref, li_ref, lt_ref, held):
    short = is_short(meta) if own else jnp.logical_not(is_short(meta))

    @pl.when(short)
    def _():
        for pair in range(4):
            start = 256 * pair
            held[0:208, :] = dot_nt(rows_ref[start : start + 208, :], wimg_ref[...])
            si_ref[:, pair, :] = held[1:198, :]
            held[0:64, :] = dot_nt(rows_ref[start + 192 : start + 256, :], wtext_ref[...])
            st_ref[:, pair, :] = held[6:64, :]

    @pl.when(jnp.logical_not(short))
    def _():
        held[0:208, :] = dot_nt(rows_ref[0:208, :], wimg_ref[...])
        li_ref[:, 0, :] = held[1:198, :]
        held[0:576, :] = dot_nt(rows_ref[192:768, :], wtext_ref[...])
        lt_ref[...] = held[6:518, :]


def input_grad(meta, own, rows, wimg, wtext):
    shapes = [(197, 4, 768), (58, 4, 768), (197, 1, 768), (512, 768)]
    return pl.pallas_call(
        partial(input_grad_kernel, own),
        grid_spec=pltpu.PrefetchScalarGridSpec(
            num_scalar_prefetch=1,
            grid=(1,),
            in_specs=[whole(ROWS, 768), whole(768, 768), whole(768, 768)],
            out_specs=[whole(*shape) for shape in shapes],
            scratch_shapes=[pltpu.VMEM((576, 768), F32)],
        ),
        out_shape=[jax.ShapeDtypeStruct(shape, F32) for shape in shapes],
        compiler_params=params(12),
        name="input_grad",
        cost_estimate=cost(0.1),
    )(meta, rows, wimg, wtext)


def swap(values, bits):
    if bits == Y:
        return lax.ppermute(values, TP, [(0, 1), (1, 0)])
    if bits < Y:
        return lax.ppermute(values, DP, [(i, i ^ bits) for i in range(16)])
    step = 2 * (bits - Y) + 1
    return lax.ppermute(values, (DP, TP), [(i, i ^ step) for i in range(32)])


def after(values, *others):
    return lax.optimization_barrier((values, *others))[0]


def plus(left, right):
    return (left.astype(F32) + right.astype(F32)).astype(BF)


def absolute(arrays, order):
    width = arrays[0].shape[-1]
    both = jnp.stack(arrays).reshape(2, *(2 for _ in order), 48, width)
    at = {bit: 1 + k for k, bit in enumerate(order)}
    first = [at[Y]] if Y in at else []
    both = both.transpose(*first, at[HIGH], at[LOW], at[X], 0, len(order) + 1, len(order) + 2)
    return both.reshape(-1, width)


class Scatter:
    def __init__(self, pieces, order):
        self.order = (CORE, *order)
        self.arrived = None
        if lax.axis_size(DP) != 16:
            rows = absolute(pieces, order)
            self.total = lax.psum_scatter(rows, BOTH, scatter_dimension=0, tiled=True).astype(F32)
            self.order = ()
            return
        shape = (2, 2, 2, 2, 48, pieces[0].shape[-1])
        self.keep, self.sent = pieces[0].reshape(shape), pieces[1].reshape(shape)

    def send(self):
        if self.order:
            self.arrived = swap(self.sent, self.order[0])

    def add(self):
        if self.order:
            if len(self.order) == 1:
                self.total = self.keep.astype(F32) + self.arrived.astype(F32)
            else:
                self.keep, self.sent = plus(self.keep[0], self.arrived[0]), plus(self.keep[1], self.arrived[1])
            self.arrived = None
            self.order = self.order[1:]


class Half:
    def __init__(self, pieces, other):
        self.other = other
        self.order = (CORE, *HALVES[other][0:2])
        self.arrived = None
        self.pieces = pieces
        if lax.axis_size(DP) != 16:
            self.order = ()
            return
        shape = (2, 2, 2, 48, pieces[0].shape[-1])
        self.keep, self.sent = pieces[0].reshape(shape), pieces[1].reshape(shape)

    def send(self):
        if self.order:
            self.arrived = swap(self.sent, self.order[0])

    def add(self):
        if self.order:
            self.order = self.order[1:]
            if self.order:
                self.keep, self.sent = plus(self.keep[0], self.arrived[0]), plus(self.keep[1], self.arrived[1])
            else:
                self.keep = plus(self.keep, self.arrived)
            self.arrived = None


class Cross:
    def __init__(self, own, other):
        self.own, self.other = own, other
        self.arrived = None
        self.order = (Y, HIGH)
        if lax.axis_size(DP) != 16:
            rows = jnp.concatenate([absolute(half.pieces, HALVES[half.other]) for half in (own, other)])
            self.total = lax.psum_scatter(rows, BOTH, scatter_dimension=0, tiled=True).astype(F32)
            self.order = ()

    def send(self):
        if self.order and self.order[0] == Y and not self.other.order:
            self.arrived = swap(self.other.keep, Y)
        elif self.order and self.order[0] == HIGH and not self.own.order:
            self.sent = plus(self.own.keep[1], self.crossed[1])
            self.arrived = swap(self.sent, HIGH)

    def add(self):
        if self.order and self.order[0] == Y:
            self.crossed = self.arrived
        elif self.order:
            keep = self.own.keep[0].astype(F32) + self.crossed[0].astype(F32)
            self.total = keep + self.arrived.astype(F32)
        self.arrived = None
        self.order = self.order[1:]


class Gather:
    def __init__(self, joined, widths, phases, orders, whole=None):
        self.joined, self.widths, self.phases = joined, widths, phases
        self.parts = None if joined is None else self.split(joined)
        self.arrived = None
        if lax.axis_size(DP) != 16:
            if whole is None:
                whole = lax.all_gather(joined[0], BOTH, axis=0, tiled=True)
            rows = whole.reshape(2, 2, 2, 2, 2, 48, sum(widths))
            at = {Y: 0, HIGH: 1, LOW: 2, X: 3}
            self.rows = tuple(
                tuple(self.split(rows.transpose(4, *(at[bit] for bit in order), 5, 6).reshape(4, 8, 48, -1))[kind])
                for kind, order in enumerate(orders)
            )
            self.phases = ()

    def split(self, values):
        return values[..., : self.widths[0]], values[..., self.widths[0] :]

    def send(self):
        if not self.phases:
            return
        if self.phases[0] in (HIGH, LOW):
            if self.joined is None:
                self.joined = jnp.concatenate(self.parts, axis=-1)
            self.arrived = swap(self.joined, self.phases[0])
            return
        first, second = self.parts
        if self.phases[0] == X:
            self.arrived = swap(first, X), swap(second, Y)
        elif self.phases[0] == Y:
            self.arrived = swap(first, Y), swap(second, X)
        else:
            self.arrived = tuple(tuple(swap(part, CORE) for part in rows) for rows in self.rows)

    def add(self):
        joined = None
        if self.phases[0] == HIGH:
            joined = jnp.concatenate([self.joined, self.arrived], axis=0)
        elif self.phases[0] == LOW:
            pieces = self.split(self.joined), self.split(self.arrived)
            self.parts = tuple(jnp.concatenate([piece[kind] for piece in pieces], axis=0) for kind in range(2))
        elif self.phases[0] == X:
            self.parts = tuple(jnp.concatenate(pair, axis=0) for pair in zip(self.parts, self.arrived))
        elif self.phases[0] == Y:
            self.rows = tuple(zip(self.parts, self.arrived))
        else:
            self.rows = tuple(near + far for near, far in zip(self.rows, self.arrived))
        self.joined, self.arrived = joined, None
        self.phases = self.phases[1:]


def seal(values, movers, swaps=()):
    flying = [mover for mover in movers if mover.arrived is not None]
    values, arrived, swaps = lax.optimization_barrier(
        (tuple(values), tuple(mover.arrived for mover in flying), tuple(swaps))
    )
    for mover, data in zip(flying, arrived):
        mover.arrived = data
        mover.add()
    for mover in movers:
        mover.send()
    return values, swaps


def on_device(
    short_images, short_texts, short_lengths, short_cotangent,
    long_images, long_texts, long_lengths, long_cotangent,
    img_weight, img_bias, text_weight, text_bias, cls_token, attn_gain, attn_shift,
    query_weight, query_bias, key_weight, value_weight, value_bias, out_weight, out_bias,
    mlp_gain, mlp_shift, up_weight, up_bias, down_weight, down_bias,
):
    half = lax.axis_index(TP)
    short = half == 1
    part = img_weight.shape[0]
    devices = 768 // part
    grouped = lax.axis_size(DP) == 16

    vectors = [img_bias, text_bias, cls_token, attn_gain, attn_shift, query_bias, value_bias, out_bias,
               mlp_gain, mlp_shift, down_bias]
    if grouped:
        small = jnp.concatenate([jnp.stack(vectors), up_bias.reshape(4, 24), jnp.zeros((1, 24), BF)])
        shard = pack(query_weight, key_weight, value_weight, img_weight, text_weight, out_weight.T, small)
        towers = None
    else:
        every = lambda v: lax.all_gather(v, (DP, TP), axis=0, tiled=True)
        towers = every(jnp.concatenate([img_weight, text_weight], axis=1))
        towers = towers.reshape(16, 2, 24, 2, 768).transpose(1, 0, 3, 2, 4).reshape(2, 768, 768)
        columns = jnp.stack([every(v) for v in vectors]).reshape(11, 32, 24).transpose(1, 2, 0)
        columns = jnp.concatenate([columns, every(up_bias).reshape(32, 4, 24).transpose(0, 2, 1)], axis=2)
        columns = jnp.pad(columns, ((0, 0), (0, 24), (0, 113)))
        columns = columns.reshape(16, 2, 48, 128).transpose(1, 0, 2, 3).reshape(2, 768, 128)
        outs = lax.all_gather(out_weight.T, BOTH, axis=0, tiled=True).reshape(2, 768, 384)
        towers = jnp.concatenate([towers, outs, columns], axis=2)
        qkv = jnp.concatenate([query_weight, key_weight, value_weight], axis=1)
        towers = jnp.concatenate([lax.all_gather(qkv, BOTH, axis=0, tiled=True).reshape(2, 768, 1152), towers], axis=2)
        shard = None
    joined = None if grouped else jnp.concatenate([up_weight, down_weight.T], axis=1)[None]
    first_gather = Gather(shard, (1152, 1280), (HIGH, LOW, X, Y, CORE), (GATHER_QKV, GATHER_TOWER), towers)
    wide_gather = Gather(joined, (1536, 1536), (X, HIGH, LOW, Y, CORE), (GATHER_UP, GATHER_DOWN))
    wide_gather.parts = up_weight[None], down_weight.T[None]
    near, wide = [first_gather], [wide_gather]
    first_gather.send()
    wide_gather.send()
    seal((), near + wide)
    seal((), near)
    seal((), near + wide)

    zero = jnp.zeros((4, 1, 768), BF)
    short_rows = jnp.concatenate([zero, short_images, short_texts], axis=1).reshape(ROWS, 768)
    long_rows = jnp.concatenate([zero[0, 0:1], long_images[0], long_texts[0], jnp.zeros((ROWS - 710, 768), BF)], axis=0)
    x = jnp.where(short, short_rows, long_rows)
    cot = jnp.where(
        short,
        short_cotangent.reshape(ROWS, 768),
        jnp.concatenate([long_cotangent[0], jnp.zeros((ROWS - 710, 768), BF)], axis=0),
    )
    place = lax.axis_index(DP) if grouped else jnp.int32(0)
    half_place = half.astype(jnp.int32) if grouped else jnp.int32(0)
    limits = 198 + jnp.where(short, short_lengths, jnp.broadcast_to(long_lengths, (4,)))
    meta = jnp.concatenate(
        [
            half.astype(jnp.int32)[None],
            limits.astype(jnp.int32),
            half_place[None],
            place.astype(jnp.int32)[None],
            jnp.zeros((1,), jnp.int32),
        ]
    )

    x_t, cot_t, cot_sum = prepare(x, cot)
    (x, cot, x_t, cot_t, meta), _ = seal((x, cot, x_t, cot_t, meta), near)
    seal((), near)
    (x,), _ = seal((x,), near + wide)
    stream, n1_t, qkv0, qkv1, wimg, wtext, wqkv, wout, smalls, up_bias_all = embed(
        meta, x, *first_gather.rows
    )
    att1, lse1 = attn_forward(meta, qkv1)
    (att1, qkv0), _ = seal((att1, qkv0), wide)
    att0, lse0 = attn_forward(meta, qkv0)
    mid, n2, n2_t = mid_stage(meta, (att0, att1), stream, wout, smalls)
    (n2,), _ = seal((n2,), wide)
    weights = (*wide_gather.rows, up_bias_all)
    mlp1, gn1, *rest = mlp_half(meta, 1, n2, n2_t, cot, cot_t, *weights)
    ff_other, grad_up_bias1 = Half(rest[0:2], 1), rest[2]
    ff_other.send()
    mlp0, gn0, *rest = mlp_half(meta, 0, after(n2, mlp1), n2_t, cot, cot_t, *weights)
    (mlp0, *rest), _ = seal((mlp0, *rest), [ff_other])
    ff_own, grad_up_bias0 = Half(rest[0:2], 0), rest[2]
    ff_own.send()
    ff = Cross(ff_own, ff_other)
    out, grad_mid, gatt0, gatt1, *rest = back_mid(
        meta, (mlp0, gn0, mlp1, gn1), mid, cot, (att0, att1), wout, smalls
    )
    gout0, gout1, sums_two = rest[0:2], rest[2:4], rest[4]
    (out, gatt0, gatt1), _ = seal((out, gatt0, gatt1), [ff_own])
    out_other = swap(out, Y)
    dqkv1 = attn_back(meta, qkv1, gatt1, lse1)
    (*rest, gatt0), _ = seal((*proj_grad(meta, 1, n1_t, dqkv1, gout1), gatt0), [ff_other])
    proj_other = Half(rest, 1)
    proj_other.send()
    dqkv0 = attn_back(meta, qkv0, gatt0, lse0)
    (dqkv0,), _ = seal((dqkv0,), [ff_own])
    rest = proj_grad(meta, 0, n1_t, dqkv0, gout0)
    (dqkv0, *rest), (out_other,) = seal((dqkv0, *rest), [ff_other], (out_other,))
    proj_own = Half(rest, 0)
    proj_own.send()
    ff = Cross(ff_own, ff_other)
    ff.send()
    low, sums_one, qkv_sums = back_in(meta, (dqkv0, dqkv1), stream, grad_mid, wqkv, smalls)
    (low, x_t), _ = seal((low, x_t), [ff_own, proj_own, proj_other])
    low_other = swap(low, Y)
    towers = tower_grad(meta, x_t, low, sums_one, sums_two, qkv_sums, cot_sum, grad_up_bias0, grad_up_bias1)
    (*towers, low, out, out_other), _ = seal((*towers, low, out, out_other), [])
    tower = Scatter(towers, TOWERS)
    tower.send()
    proj = Cross(proj_own, proj_other)
    short_output = jnp.where(short, out, out_other).reshape(4, 256, 768)
    long_output = jnp.where(short, out_other, out)[None, 0:710]
    (short_output, long_output, low), _ = seal((short_output, long_output, low), [tower])
    mine = input_grad(meta, True, low, wimg, wtext)
    mine, _ = seal(mine, [ff, proj_other])
    seal((), [proj_own, proj_other, tower])
    proj.send()
    _, (low_other,) = seal((), [proj_own, ff, proj], (low_other,))
    (low_other,), _ = seal((low_other,), [tower])
    theirs = input_grad(meta, False, low_other, wimg, wtext)
    si, st = (jnp.where(short, mine[k], theirs[k]) for k in (0, 1))
    li, lt = (jnp.where(short, theirs[k], mine[k]) for k in (2, 3))
    (si, st, li, lt), _ = seal((si, st, li, lt), [proj, tower])
    si, st, li, lt = si.transpose(1, 0, 2), st.transpose(1, 0, 2), li.transpose(1, 0, 2), lt[None]
    seal((), [tower])
    red_ff, red_proj = ff.total, proj.total
    if grouped:
        red_tower = tower.total
        red_img, red_text = red_tower[0:24, 0:768], red_tower[24:48, 0:768]
        red_vectors = [red_tower[0:24, 768 + k] for k in range(11)]
        device = 2 * lax.axis_index(DP) + lax.axis_index(TP)
        red_up_bias = lax.dynamic_slice(red_tower, (0, 779 + device // 8), (24, 4))
        red_vectors.append(red_up_bias.T.reshape(96))
    else:
        mats = jnp.stack([absolute([part_[:, half_, :, 0:768] for part_ in towers], TOWERS[0:3]) for half_ in range(2)])
        mats = mats.reshape(2, 16, 2, 24, 768).transpose(2, 1, 0, 3, 4).reshape(2, 768, 768)
        red_img = lax.psum_scatter(mats[0], (DP, TP), scatter_dimension=0, tiled=True)
        red_text = lax.psum_scatter(mats[1], (DP, TP), scatter_dimension=0, tiled=True)
        sums = [*sums_one[0:5], qkv_sums[:, 0:384].reshape(768), qkv_sums[:, 768:1152].reshape(768),
                *sums_two[0:3], cot_sum[0], jnp.concatenate([grad_up_bias0, grad_up_bias1]).reshape(3072)]
        red_vectors = [lax.psum_scatter(v, (DP, TP), scatter_dimension=0, tiled=True) for v in sums]

    f = lambda v: v.astype(F32)
    vec = [f(v) for v in red_vectors]
    return (
        short_output, long_output, si, st, li, lt,
        f(red_img), vec[0], f(red_text), vec[1], vec[2], vec[3], vec[4],
        red_proj[:, 0:384], vec[5], red_proj[:, 384:768], red_proj[:, 768:1152], vec[6],
        red_proj[:, 1152:1536].T, vec[7], vec[8], vec[9],
        jnp.concatenate([red_ff[:, 0:768], red_ff[:, 1536:2304]], axis=1), vec[11],
        jnp.concatenate([red_ff[:, 768:1536], red_ff[:, 2304:3072]], axis=1).T, vec[10],
    )


def solution(mesh):
    rows = P(DP, None, None)
    vec = P((DP, TP))
    tower = P((DP, TP), None)
    col = P(DP, TP)
    back = P(TP, DP)
    return jax.shard_map(
        on_device,
        mesh=mesh,
        in_specs=(
            rows, rows, P(DP), rows, rows, rows, P(DP), rows,
            tower, vec, tower, vec, vec, vec, vec,
            col, vec, col, col, vec, back, vec, vec, vec, col, vec, back, vec,
        ),
        out_specs=(
            rows, rows, rows, rows, rows, rows,
            tower, vec, tower, vec, vec, vec, vec,
            col, vec, col, col, vec, back, vec, vec, vec, col, vec, back, vec,
        ),
        check_vma=False,
    )
```
